32 devices in a mesh: group: 2 (over y), visit: 16 (over z, x, core), sky: 1.
Axes of the slice: x: 2, y: 2, z: 4, core: 2. Of those that a mesh axis runs over, the one named last changes fastest.
Arguments:
- template: bfloat16 [64, 128], P(('group', 'visit'), 'sky'), parts along dimension 0, may hold values from -6 to 6
- science: float32 [32, 32, 128], P(('group', 'visit'), None, 'sky'), parts along dimension 0, may hold values from -15 to 15
- variance: float32 [32, 32, 128], P(('group', 'visit'), None, 'sky'), parts along dimension 0, may hold values from 0.5 to 4
- col_taps: bfloat16 [49, 31], replicated, may hold values from -1 to 1
- row_taps: bfloat16 [49, 31], replicated, may hold values from -1 to 1
- stamp_rows: int32 [32, 1, 16], P(('group', 'visit'), 'sky'), parts along dimension 0, may hold values from 0 to 16
- stamp_cols: int32 [32, 1, 16], P(('group', 'visit'), 'sky'), parts along dimension 0, may hold values from 0 to 112
Outputs:
- difference: float32 [32, 32, 128], P(('group', 'visit'), None, 'sky'), parts along dimension 0
- coefficients: float32 [32, 50], P(('group', 'visit')), parts along dimension 0
- detection: float32 [64, 128], P(('group', 'visit'), 'sky'), parts along dimension 0
The draws below stay inside these ranges and needn't reach their ends.
There are 2 independent parts, one for each index of `group`. The reference program is written for one: setup_inputs(seed, part) draws one part's arguments, and reference() takes and returns one part's arrays. A program takes and returns all parts, laid end to end along the dimension named above; an argument that names none is the same for every part. Nothing has to cross between parts.
All inputs are finite; a program needn't handle non-finite values.
Results may differ from the reference program's by a relative error of at most 0.0018.
Values may be sent and summed in bfloat16 or wider, within the bound.
No kernel may reach another device: no remote copies, remote signals or barrier semaphores. Data moves between devices by JAX's collectives and lax.ppermute only.
A program may use at most 128 MiB of HBM per device.

```python
import math
import jax
import jax.numpy as jnp
from jax import lax

NB = 49
TAPS = 31
STAMP = 16
STAMPS = 16
TILE_W = 128
TILE_H = 32
VISITS = 16
SKY_TILES = 1
PATCH_W = 128


def shared_field(key):
    base_field = jax.random.normal(jax.random.fold_in(key, 101), (TILE_H, PATCH_W), jnp.float32)
    return jnp.clip(base_field, -6.0, 6.0)


def draw_template(key, part):
    return shared_field(key).astype(jnp.bfloat16)


def draw_science(key, part):
    base_field = shared_field(key)
    visit_gains = jax.random.uniform(jax.random.fold_in(key, 202), (VISITS, 1, 1), jnp.float32, 0.5, 2.0)
    raw_noise = jax.random.normal(jax.random.fold_in(key, 303), (VISITS, TILE_H, PATCH_W), jnp.float32)
    noise_field = 0.5 * jnp.clip(raw_noise, -6.0, 6.0)
    return visit_gains * base_field[None, :, :] + noise_field


def plant(array, stream_key, low, top_value):
    longest = array.shape.index(max(array.shape))
    spots = []
    for shift in (0, 1):
        where = [jax.random.randint(jax.random.fold_in(stream_key, axis), (), 0, length) for axis, length in enumerate(array.shape)]
        where[longest] = (where[longest] + shift) % array.shape[longest]
        spots.append(tuple(where))
    return array.at[spots[0]].set(low).at[spots[1]].set(top_value)


def block_scale(own_key, dims, pieces, low, top_value):
    def one(dim, shards_of):
        heights = jax.random.uniform(jax.random.fold_in(jax.random.fold_in(own_key, 6), dim), (shards_of,), jnp.float32, low / len(pieces), top_value / len(pieces))
        return jnp.repeat(jnp.exp(heights), dims[dim] // shards_of).reshape((-1,) + (1,) * (len(dims) - dim - 1))

    factor_of = one(*pieces[0])
    for cut in pieces[1:]:
        factor_of = factor_of * one(*cut)
    return factor_of


def bell_draw(own_key, shape, spread, bound, held_as=jnp.bfloat16):
    entries = jax.random.normal(own_key, shape, jnp.float32) * spread
    return jnp.minimum(jnp.maximum(entries, -bound), bound).astype(held_as)


def setup_inputs(seed: int = 0, part: int = 0) -> dict:
    splits = jax.random.split(jax.random.key(seed), 8)
    part_splits = jax.random.split(jax.random.fold_in(splits[7], part), 8)
    template = draw_template(jax.random.fold_in(jax.random.fold_in(splits[7], part), 71), part)
    science = draw_science(jax.random.fold_in(jax.random.fold_in(splits[7], part), 71), part)
    variance = jnp.clip(jnp.exp(math.log(4.0) - 2.0794415 * jax.random.uniform(part_splits[2], (VISITS, TILE_H, PATCH_W), jnp.float32) ** block_scale(part_splits[2], (VISITS, TILE_H, PATCH_W), ((0, 16),), -0.2, 0.2)), 0.5, 4.0)
    col_taps = bell_draw(splits[3], (NB, TAPS), TAPS ** -0.5, 1.0)
    row_taps = bell_draw(splits[4], (NB, TAPS), TAPS ** -0.5, 1.0)
    stamp_rows = plant(jax.random.randint(part_splits[5], (VISITS, SKY_TILES, STAMPS), 0, TILE_H - STAMP + 1), jax.random.fold_in(part_splits[5], 1), 0, TILE_H - STAMP).astype(jnp.int32)
    stamp_cols = plant(jax.random.randint(part_splits[6], (VISITS, SKY_TILES, STAMPS), 0, TILE_W - STAMP + 1), jax.random.fold_in(part_splits[6], 1), 0, TILE_W - STAMP).astype(jnp.int32)
    return {"template": template, "science": science, "variance": variance, "col_taps": col_taps, "row_taps": row_taps, "stamp_rows": stamp_rows, "stamp_cols": stamp_cols}


def column_pass(padded, taps):
    out_width = padded.shape[1] - TAPS + 1
    shifted = jnp.stack([padded[:, offset:offset + out_width] for offset in range(TAPS)]).astype(jnp.float32)
    result = jnp.einsum('kj,jhw->khw', taps.astype(jnp.float32), shifted, precision=lax.Precision.HIGHEST)
    return result.astype(jnp.bfloat16)

def row_pass(columns, taps):
    margin = (TAPS - 1) // 2
    height = columns.shape[1]
    padded = jnp.pad(columns.astype(jnp.float32), ((0, 0), (margin, margin), (0, 0)))
    total = jnp.zeros(columns.shape, jnp.float32)
    for offset in range(TAPS):
        total = total + taps[:, offset].astype(jnp.float32)[:, None, None] * padded[:, offset:offset + height, :]
    return total.astype(jnp.bfloat16)

def cholesky_solve(matrix, vector):
    factor = jnp.linalg.cholesky(matrix)
    middle = lax.linalg.triangular_solve(factor, vector[:, None], left_side=True, lower=True)
    answer = lax.linalg.triangular_solve(factor, middle, left_side=True, lower=True, transpose_a=True)
    return answer[:, 0]

def reference(template, science, variance, col_taps, row_taps, stamp_rows, stamp_cols):
    margin = (TAPS - 1) // 2
    padded = jnp.pad(template, ((0, 0), (margin, margin)))
    columns = column_pass(padded, col_taps)
    convolved = row_pass(columns, row_taps)
    convolved_wide = convolved.astype(jnp.float32)
    shifts = (jnp.arange(SKY_TILES, dtype=jnp.int32) * TILE_W)[None, :, None]
    col_starts = (stamp_cols + shifts).reshape(VISITS, -1)
    row_starts = stamp_rows.reshape(VISITS, -1)

    def one_visit(inputs):
        science_map, variance_map, rows_here, cols_here = inputs

        def extract(row_start, col_start):
            block = lax.dynamic_slice(convolved, (jnp.int32(0), row_start, col_start), (NB, STAMP, STAMP))
            values = lax.dynamic_slice(science_map, (row_start, col_start), (STAMP, STAMP))
            noises = lax.dynamic_slice(variance_map, (row_start, col_start), (STAMP, STAMP))
            return (block, values, noises)
        blocks, values, noises = jax.vmap(extract)(rows_here, cols_here)
        design_core = jnp.transpose(blocks, (1, 0, 2, 3)).reshape(NB, -1)
        design = jnp.concatenate([design_core, jnp.ones((1, design_core.shape[1]), design_core.dtype)], axis=0).astype(jnp.float32)
        weights = 1.0 / noises.reshape(-1)
        normal = jnp.dot(design * weights[None, :], design.T, precision=lax.Precision.HIGHEST)
        target = jnp.dot(design, weights * values.reshape(-1), precision=lax.Precision.HIGHEST)
        solution = cholesky_solve(normal, target)
        model_map = jnp.tensordot(solution[:NB], convolved_wide, axes=1, precision=lax.Precision.HIGHEST)
        residual = science_map - model_map - solution[NB]
        return (residual / jnp.sqrt(variance_map), solution, residual / variance_map)
    differences, solutions, weighted = lax.map(one_visit, (science, variance, row_starts, col_starts))
    detection = lax.optimization_barrier(jnp.sum(weighted, axis=0)) / jnp.sqrt(lax.optimization_barrier(jnp.sum(1.0 / variance, axis=0)))
    return (differences, solutions, detection)
```

```python
import jax
import jax.numpy as jnp
from jax import lax
from jax.experimental import pallas as pl
from jax.experimental.pallas import tpu as pltpu
from jax.sharding import PartitionSpec as P

STAMP = 16
SUB = 8
LANE = 128
UNROLL = 32
F32 = jnp.float32
BF16 = jnp.bfloat16


def ceil_to(value, step):
    return (value + step - 1) // step * step


def each(count, body):
    if count <= UNROLL:
        for index in range(count):
            body(index)
    else:
        lax.fori_loop(0, count, lambda index, carry: (body(index), carry)[1], 0)


def lanes_of(index, width):
    if isinstance(index, int):
        return slice(index * width, (index + 1) * width)
    return pl.ds(pl.multiple_of(index * width, width), width)


def split_bf16(value, pieces):
    out = []
    for piece in range(pieces):
        part = value.astype(BF16)
        out.append(part)
        if piece + 1 < pieces:
            value = value - part.astype(F32)
    return out


def load_taps(taps_ref, pad_ref):
    kernels, taps = taps_ref.shape
    pad_ref[...] = jnp.zeros(pad_ref.shape, F32)
    pad_ref[0:kernels, 0:taps] = taps_ref[...].astype(F32)


def column_stage(tmpl_ref, edge_ref, col_taps_ref, pad_ref, cols_ref, tap_count):
    height, width = tmpl_ref.shape
    margin = (tap_count - 1) // 2
    span = ceil_to(tap_count, SUB)
    load_taps(col_taps_ref, pad_ref)
    flip = (
        lax.broadcasted_iota(jnp.int32, (span, span), 0)
        + lax.broadcasted_iota(jnp.int32, (span, span), 1)
        == tap_count - 1
    ).astype(BF16)
    taps = jnp.dot(
        pad_ref[:, 0:span].astype(BF16), flip, preferred_element_type=F32
    ).astype(BF16)
    place = lax.broadcasted_iota(jnp.int32, (span, width), 1) + (
        margin - lax.broadcasted_iota(jnp.int32, (span, width), 0)
    )
    inside = (place >= 0) & (place < width)
    groups = cols_ref.shape[1]

    def shifted(row):
        line = jnp.broadcast_to(tmpl_ref[pl.ds(row, 1), :], (span, width))
        line = pltpu.roll(line, width - margin, 1, stride=1, stride_axis=0)
        if edge_ref is None:
            return jnp.where(inside, line, 0.0).astype(BF16)
        side = jnp.broadcast_to(edge_ref[pl.ds(row, 1), :], (span, width))
        side = pltpu.roll(side, width - margin, 1, stride=1, stride_axis=0)
        return jnp.where(inside, line, side).astype(BF16)

    def pair(index):
        both = jnp.concatenate([shifted(2 * index), shifted(2 * index + 1)], axis=1)
        result = jnp.dot(taps, both, preferred_element_type=F32)
        result = result.astype(BF16).astype(F32)
        for half in range(2):
            for group in range(groups):
                cols_ref[2 * index + half + margin, group] = result[
                    SUB * group : SUB * (group + 1), width * half : width * (half + 1)
                ]

    each(height // 2, pair)


def row_stage(row_taps_ref, pad_ref, spread_ref, cols_ref, conv_ref, kernels, tap_count):
    height, groups, _, width = conv_ref.shape
    margin = (tap_count - 1) // 2
    load_taps(row_taps_ref, pad_ref)
    for tap in range(tap_count):
        column = jnp.broadcast_to(
            pad_ref[0 : groups * SUB, tap : tap + 1], (groups * SUB, width)
        )
        for group in range(groups):
            spread_ref[group, tap] = column[SUB * group : SUB * (group + 1)]
    static = height <= UNROLL
    if not static:
        edge = jnp.zeros((margin, groups, SUB, width), F32)
        cols_ref[0:margin] = edge
        cols_ref[height + margin : height + 2 * margin] = edge
    block = 8

    def group_body(group, first):
        acc = [None] * block
        for step in range(block + 2 * margin):
            if static and not 0 <= first + step - margin < height:
                continue
            value = cols_ref[first + step, group]
            for out in range(block):
                tap = step - out
                if 0 <= tap < tap_count:
                    term = spread_ref[group, tap] * value
                    acc[out] = term if acc[out] is None else acc[out] + term
        ones = (
            lax.broadcasted_iota(jnp.int32, (SUB, width), 0) + SUB * group == kernels
        )
        for out in range(block):
            rounded = acc[out].astype(BF16).astype(F32)
            conv_ref[first + out, group] = jnp.where(ones, 1.0, rounded)

    def loop_groups(first):
        lax.fori_loop(0, groups, lambda g, c: (group_body(g, first), c)[1], 0)

    if static:
        for first in range(0, height, block):
            loop_groups(first)
    else:
        lax.fori_loop(
            0, height // block, lambda b, c: (loop_groups(b * block), c)[1], 0
        )


def weight_stage(var_ref, rows_ref, cols_ref, weight_ref, inverse_ref):
    height, width = weight_ref.shape
    stamps = rows_ref.shape[-1]

    def block(index):
        first = index * SUB
        row = lax.broadcasted_iota(jnp.int32, (SUB, width), 0) + first
        col = lax.broadcasted_iota(jnp.int32, (SUB, width), 1)
        count = jnp.zeros((SUB, width), F32)
        for stamp in range(stamps):
            down = row - rows_ref[0, 0, stamp]
            along = col - cols_ref[0, 0, stamp]
            held = (down >= 0) & (down < STAMP) & (along >= 0) & (along < STAMP)
            count = count + jnp.where(held, 1.0, 0.0)
        if not isinstance(first, int):
            first = pl.multiple_of(first, SUB)
        inverse = 1.0 / var_ref[0, pl.ds(first, SUB), :]
        inverse_ref[pl.ds(first, SUB), :] = inverse
        weight_ref[pl.ds(first, SUB), :] = inverse * count

    each(height // SUB, block)


def normal_stage(sci_ref, weight_ref, conv_ref, left_ref, right_ref, kernels):
    height, groups, _, width = conv_ref.shape
    size = right_ref.shape[0]
    tall = groups * SUB
    line = lax.broadcasted_iota(jnp.int32, (size, width), 0)

    def one(row):
        design = conv_ref[row].reshape(tall, width)
        if size > tall:
            design = jnp.concatenate([design, jnp.zeros((size - tall, width), F32)], axis=0)
        weight = jnp.broadcast_to(weight_ref[pl.ds(row, 1), :], (size, width))
        science = jnp.broadcast_to(sci_ref[0, pl.ds(row, 1), :], (size, width))
        high, low = split_bf16(design * weight, 2)
        where = lanes_of(row, width)
        left_ref[0:size, where] = high
        left_ref[size : 2 * size, where] = low
        full = design
        for index, part in enumerate(split_bf16(science, 3)):
            full = jnp.where(line == kernels + 1 + index, part.astype(F32), full)
        right_ref[:, where] = full.astype(BF16)

    each(height, one)
    product = lax.dot_general(
        left_ref[...],
        right_ref[...],
        (((1,), (1,)), ((), ())),
        preferred_element_type=F32,
    )
    return product[0:size] + product[size : 2 * size]


def solve_stage(normal, kernels):
    unknowns = kernels + 1
    width = LANE
    groups = ceil_to(unknowns, SUB) // SUB
    size = normal.shape[1]
    parts = [normal[SUB * g : SUB * (g + 1)] for g in range(groups)]
    if size < width:
        parts = [
            jnp.concatenate([part, jnp.zeros((SUB, width - size), F32)], axis=1)
            for part in parts
        ]

    def lane(value, index):
        return jnp.broadcast_to(value[:, index : index + 1], (SUB, width))

    def sub(value, index):
        return jnp.broadcast_to(value[index : index + 1, :], (SUB, width))

    total = [
        lane(p, unknowns) + (lane(p, unknowns + 1) + lane(p, unknowns + 2)) for p in parts
    ]
    column = lax.broadcasted_iota(jnp.int32, (SUB, width), 1)
    row = lax.broadcasted_iota(jnp.int32, (SUB, width), 0)
    parts = [jnp.where(column == unknowns, t, p) for p, t in zip(parts, total)]
    step = 0
    while step < unknowns:
        if step + 1 < unknowns:
            first, second = step, step + 1
            g0, s0, g1, s1 = first // SUB, first % SUB, second // SUB, second % SUB
            c0 = [lane(p, first) for p in parts]
            c1 = [lane(p, second) for p in parts]
            r0, r1 = sub(parts[g0], s0), sub(parts[g1], s1)
            a, b = sub(c0[g0], s0), sub(c1[g0], s0)
            e, d = sub(c0[g1], s1), sub(c1[g1], s1)
            inverse = 1.0 / (a * d - b * e)
            q0 = (d * inverse) * r0 - (b * inverse) * r1
            q1 = (a * inverse) * r1 - (e * inverse) * r0
            parts = [p - x * q0 - y * q1 for p, x, y in zip(parts, c0, c1)]
            parts[g0] = jnp.where(row == s0, q0, parts[g0])
            parts[g1] = jnp.where(row == s1, q1, parts[g1])
            step += 2
        else:
            g0, s0 = step // SUB, step % SUB
            c0 = [lane(p, step) for p in parts]
            q0 = sub(parts[g0], s0) * (1.0 / sub(c0[g0], s0))
            parts = [p - x * q0 for p, x in zip(parts, c0)]
            parts[g0] = jnp.where(row == s0, q0, parts[g0])
            step += 1
    values = [lane(p, unknowns) for p in parts]
    last = [jnp.where(row + SUB * g < unknowns, v, 0.0) for g, v in enumerate(values)]
    return last


def residual_stage(values, conv_ref, sci_ref, var_ref, inverse_ref, diff_ref, out_ref, rows_each):
    height, groups, _, width = conv_ref.shape

    def block(index):
        first = index * SUB
        if not isinstance(first, int):
            first = pl.multiple_of(first, SUB)
        lines = []
        for row in range(SUB):
            total = conv_ref[first + row, 0] * values[0]
            for group in range(1, groups):
                total = total + conv_ref[first + row, group] * values[group]
            lines.append(jnp.sum(total, axis=0, keepdims=True))
        model = jnp.concatenate(lines, axis=0)
        here = pl.ds(first, SUB)
        residual = sci_ref[0, here, :] - model
        diff_ref[0, here, :] = residual / jnp.sqrt(var_ref[0, here, :])
        inverse = inverse_ref[here, :]
        weighted = residual * inverse
        for start in range(0, SUB, rows_each):
            target = (first + start) // rows_each
            out_ref[target, 0:rows_each, :] = weighted[start : start + rows_each]
            out_ref[target, rows_each : 2 * rows_each, :] = inverse[start : start + rows_each]

    each(height // SUB, block)


def store_coefficients(values, coef_ref, unknowns):
    row = lax.broadcasted_iota(jnp.int32, (SUB, LANE), 0)
    column = lax.broadcasted_iota(jnp.int32, (SUB, LANE), 1)
    total = jnp.zeros((SUB, LANE), F32)
    for group, value in enumerate(values):
        total = total + jnp.where(column == row + SUB * group, value, 0.0)
    coef_ref[...] = jnp.sum(total, axis=0, keepdims=True)[:, 0:unknowns]


def fit(template, edge, science, variance, col_taps, row_taps, stamp_rows, stamp_cols, rows_each, sky):
    height, width = template.shape
    kernels, tap_count = col_taps.shape
    unknowns = kernels + 1
    margin = (tap_count - 1) // 2
    groups = ceil_to(unknowns, SUB) // SUB
    size = ceil_to(unknowns + 3, 2 * SUB)
    whole = sky == 1
    vmem = pl.BlockSpec(memory_space=pltpu.VMEM)
    smem = pl.BlockSpec(memory_space=pltpu.SMEM)
    scratch = [
        pltpu.VMEM((ceil_to(kernels, 2 * SUB), LANE), F32),
        pltpu.VMEM((height + 2 * margin, groups, SUB, width), F32),
        pltpu.VMEM((groups, tap_count, SUB, width), F32),
        pltpu.VMEM((height, width), F32),
        pltpu.VMEM((height, width), F32),
        pltpu.VMEM((2 * size, height * width), BF16),
        pltpu.VMEM((size, height * width), BF16),
    ]
    conv_shape = (height, groups, SUB, width)
    out_shapes = [
        jax.ShapeDtypeStruct((1, height, width), F32),
        jax.ShapeDtypeStruct((1, unknowns), F32),
        jax.ShapeDtypeStruct((height // rows_each, 2 * rows_each, width), F32),
    ]
    params = pltpu.CompilerParams(vmem_limit_bytes=60 * 1024 * 1024)

    def front(tmpl_ref, edge_ref, sci_ref, var_ref, ct_ref, rt_ref, sr_ref, sc_ref, conv_ref, tmp):
        pad, cols, spread, weight, inverse, left, right = tmp
        column_stage(tmpl_ref, edge_ref, ct_ref, pad, cols, tap_count)
        row_stage(rt_ref, pad, spread, cols, conv_ref, kernels, tap_count)
        weight_stage(var_ref, sr_ref, sc_ref, weight, inverse)
        return normal_stage(sci_ref, weight, conv_ref, left, right, kernels)

    def back(normal, conv_ref, sci_ref, var_ref, inverse, diff_ref, coef_ref, out_ref):
        values = solve_stage(normal, kernels)
        store_coefficients(values, coef_ref, unknowns)
        residual_stage(values, conv_ref, sci_ref, var_ref, inverse, diff_ref, out_ref, rows_each)

    if whole:

        def kernel(tmpl, sci, var, ct, rt, sr, sc, diff, coef, out, conv, *tmp):
            normal = front(tmpl, None, sci, var, ct, rt, sr, sc, conv, tmp)
            back(normal, conv, sci, var, tmp[4], diff, coef, out)

        return pl.pallas_call(
            kernel,
            out_shape=out_shapes,
            in_specs=[vmem] * 5 + [smem] * 2,
            out_specs=[vmem] * 3,
            scratch_shapes=[pltpu.VMEM(conv_shape, F32)] + scratch,
            compiler_params=params,
        )(template, science, variance, col_taps, row_taps, stamp_rows, stamp_cols)

    def first(tmpl, edges, sci, var, ct, rt, sr, sc, conv, inv, normal, *tmp):
        normal[...] = front(tmpl, edges, sci, var, ct, rt, sr, sc, conv, tmp)
        inv[...] = tmp[4][...]

    conv, inverse, normal = pl.pallas_call(
        first,
        out_shape=[
            jax.ShapeDtypeStruct(conv_shape, F32),
            jax.ShapeDtypeStruct((height, width), F32),
            jax.ShapeDtypeStruct((size, size), F32),
        ],
        in_specs=[vmem] * 6 + [smem] * 2,
        out_specs=[vmem] * 3,
        scratch_shapes=scratch,
        compiler_params=params,
    )(template, edge, science, variance, col_taps, row_taps, stamp_rows, stamp_cols)
    normal = lax.psum(normal, "sky")

    def second(normal, conv, sci, var, inv, diff, coef, out):
        back(normal[...], conv, sci, var, inv, diff, coef, out)

    return pl.pallas_call(
        second,
        out_shape=out_shapes,
        in_specs=[vmem] * 5,
        out_specs=[vmem] * 3,
        compiler_params=params,
    )(normal, conv, science, variance, inverse)


def sky_edges(tile, margin, sky):
    ends = sky - 1
    width = tile.shape[1]
    head = tile[:, 0:margin]
    tail = tile[:, width - margin :]
    after = lax.ppermute(head, "sky", [(i + 1, i) for i in range(ends)])
    before = lax.ppermute(tail, "sky", [(i, i + 1) for i in range(ends)])
    middle = jnp.zeros((tile.shape[0], width - 2 * margin), tile.dtype)
    return jnp.concatenate([after, middle, before], axis=1)


def solution(mesh):
    visits = mesh.shape["visit"]
    sky = mesh.shape["sky"]

    def on_device(template, science, variance, col_taps, row_taps, stamp_rows, stamp_cols):
        rows_each, width = template.shape
        margin = (col_taps.shape[1] - 1) // 2
        copies = jnp.broadcast_to(template.astype(F32)[None], (visits, rows_each, width))
        tile = lax.all_to_all(copies, "visit", 0, 0, tiled=True).reshape(-1, width)
        edge = sky_edges(tile, margin, sky) if sky > 1 else None
        difference, coefficients, shares = fit(
            tile, edge, science, variance, col_taps, row_taps, stamp_rows, stamp_cols, rows_each, sky
        )
        shares = lax.all_to_all(shares, "visit", 0, 0, tiled=True)
        total = jnp.sum(shares, axis=0)
        detection = total[0:rows_each] / jnp.sqrt(total[rows_each:])
        return difference, coefficients, detection

    in_specs = (
        P(("group", "visit"), "sky"),
        P(("group", "visit"), None, "sky"),
        P(("group", "visit"), None, "sky"),
        P(),
        P(),
        P(("group", "visit"), "sky", None),
        P(("group", "visit"), "sky", None),
    )
    out_specs = (
        P(("group", "visit"), None, "sky"),
        P(("group", "visit"), None),
        P(("group", "visit"), "sky"),
    )
    return jax.shard_map(
        on_device, mesh=mesh, in_specs=in_specs, out_specs=out_specs, check_vma=False
    )
```

```python
import jax
import jax.numpy as jnp
from jax import lax
from jax.experimental import pallas as pl
from jax.experimental.pallas import tpu as pltpu
from jax.sharding import PartitionSpec as P

STAMP = 16
SUB = 8
LANE = 128
UNROLL = 32
CHUNK = 32
F32 = jnp.float32
BF16 = jnp.bfloat16


def ceil_to(value, step):
    return (value + step - 1) // step * step


def each(count, body):
    if count <= UNROLL:
        for index in range(count):
            body(index)
    else:
        lax.fori_loop(0, count, lambda index, carry: (body(index), carry)[1], 0)


def lanes_of(index, width):
    if isinstance(index, int):
        return slice(index * width, (index + 1) * width)
    return pl.ds(pl.multiple_of(index * width, width), width)


def split_bf16(value, pieces):
    out = []
    for piece in range(pieces):
        part = value.astype(BF16)
        out.append(part)
        if piece + 1 < pieces:
            value = value - part.astype(F32)
    return out


def load_taps(taps_ref, pad_ref):
    kernels, taps = taps_ref.shape
    pad_ref[...] = jnp.zeros(pad_ref.shape, F32)
    pad_ref[0:kernels, 0:taps] = taps_ref[...].astype(F32)


def chunk_rows(height):
    rows = min(CHUNK, height)
    return rows, (0 if rows == height else CHUNK // 2)


def taps_stage(col_taps_ref, row_taps_ref, pad_ref, flipped_ref, band_ref, height):
    tap_count = col_taps_ref.shape[1]
    margin = (tap_count - 1) // 2
    span = ceil_to(tap_count, SUB)
    groups = band_ref.shape[0]
    rows, side = chunk_rows(height)
    wide = SUB * (rows + 2 * side)
    load_taps(col_taps_ref, pad_ref)
    flip = (
        lax.broadcasted_iota(jnp.int32, (span, span), 0)
        + lax.broadcasted_iota(jnp.int32, (span, span), 1)
        == tap_count - 1
    ).astype(BF16)
    flipped_ref[...] = jnp.dot(
        pad_ref[:, 0:span].astype(BF16), flip, preferred_element_type=F32
    ).astype(BF16)
    load_taps(row_taps_ref, pad_ref)
    repeat = (
        lax.broadcasted_iota(jnp.int32, (span, wide), 1) // SUB
        == lax.broadcasted_iota(jnp.int32, (span, wide), 0)
    ).astype(BF16)
    spread = jnp.dot(
        pad_ref[0 : groups * SUB, 0:span].astype(BF16), repeat, preferred_element_type=F32
    )
    tall = groups * SUB
    lane = lax.broadcasted_iota(jnp.int32, (tall, wide), 1)
    own = lane % SUB == lax.broadcasted_iota(jnp.int32, (tall, wide), 0) % SUB
    spread = jnp.where(own, spread, 0.0)
    place = lane // SUB - side

    def line(row):
        moved = pltpu.roll(spread, (SUB * (row - margin + side)) % wide, 1)
        return jnp.where((place >= row - margin) & (place <= row + margin), moved, 0.0)

    for row in range(0, rows, 2):
        first, second = line(row), line(row + 1)
        for group in range(groups):
            here = slice(SUB * group, SUB * (group + 1))
            both = jnp.concatenate([first[here], second[here]], axis=0)
            band_ref[group, SUB * row : SUB * (row + 2), :] = both.astype(BF16)


def column_stage(tmpl_ref, edge_ref, flipped_ref, cols_ref, height, tap_count):
    width = tmpl_ref.shape[1]
    margin = (tap_count - 1) // 2
    span = ceil_to(tap_count, SUB)
    groups = cols_ref.shape[0]
    _, side = chunk_rows(height)
    taps = flipped_ref[...]
    place = lax.broadcasted_iota(jnp.int32, (span, width), 1) + (
        margin - lax.broadcasted_iota(jnp.int32, (span, width), 0)
    )
    inside = (place >= 0) & (place < width)
    if side:
        nothing = jnp.zeros((groups, SUB * side, width), BF16)
        cols_ref[:, 0 : SUB * side, :] = nothing
        cols_ref[:, SUB * (side + height) :, :] = nothing

    def shifted(row):
        line = jnp.broadcast_to(tmpl_ref[pl.ds(row, 1), :].astype(F32), (span, width))
        line = pltpu.roll(line, width - margin, 1, stride=1, stride_axis=0)
        if edge_ref is None:
            return jnp.where(inside, line, 0.0).astype(BF16)
        other = jnp.broadcast_to(edge_ref[pl.ds(row, 1), :].astype(F32), (span, width))
        other = pltpu.roll(other, width - margin, 1, stride=1, stride_axis=0)
        return jnp.where(inside, line, other).astype(BF16)

    def pair(index):
        both = jnp.concatenate([shifted(2 * index), shifted(2 * index + 1)], axis=1)
        result = jnp.dot(taps, both, preferred_element_type=F32)
        start = SUB * (2 * index + side)
        if not isinstance(start, int):
            start = pl.multiple_of(start, 2 * SUB)
        for group in range(groups):
            here = result[SUB * group : SUB * (group + 1)]
            two = jnp.concatenate([here[:, 0:width], here[:, width:]], axis=0)
            cols_ref[group, pl.ds(start, 2 * SUB), :] = two.astype(BF16)

    each(height // 2, pair)


def row_stage(band_ref, cols_ref, tail_ref, conv_ref):
    height, groups, _, width = conv_ref.shape
    rows, side = chunk_rows(height)

    def chunk(index):
        first = index * rows
        start = SUB * first
        if not isinstance(start, int):
            start = pl.multiple_of(start, SUB * rows)
        for group in range(groups):
            result = jnp.dot(
                band_ref[group],
                cols_ref[group, pl.ds(start, SUB * (rows + 2 * side)), :],
                preferred_element_type=F32,
            )
            for row in range(rows):
                value = result[SUB * row : SUB * (row + 1)].astype(BF16).astype(F32)
                if group == groups - 1:
                    value = value + tail_ref[first + row]
                conv_ref[first + row, group] = value

    each(height // rows, chunk)


def weight_stage(sci_ref, var_ref, rows_ref, cols_ref, weight_ref, inverse_ref, tail_ref, kernels):
    height, width = weight_ref.shape
    stamps = rows_ref.shape[-1]
    sub = lax.broadcasted_iota(jnp.int32, (SUB, width), 0)
    col = lax.broadcasted_iota(jnp.int32, (SUB, width), 1)
    ones = kernels % SUB

    def block(index):
        first = index * SUB
        row = sub + first
        count = jnp.zeros((SUB, width), F32)
        for stamp in range(stamps):
            down = row - rows_ref[0, 0, stamp]
            along = col - cols_ref[0, 0, stamp]
            held = (down >= 0) & (down < STAMP) & (along >= 0) & (along < STAMP)
            count = count + jnp.where(held, 1.0, 0.0)
        if not isinstance(first, int):
            first = pl.multiple_of(first, SUB)
        inverse = 1.0 / var_ref[0, pl.ds(first, SUB), :]
        inverse_ref[pl.ds(first, SUB), :] = inverse
        weight_ref[pl.ds(first, SUB), :] = inverse * count
        pieces = [p.astype(F32) for p in split_bf16(sci_ref[0, pl.ds(first, SUB), :], 3)]
        for line in range(SUB):
            value = jnp.where(sub == ones, 1.0, 0.0)
            for piece, part in enumerate(pieces):
                spread = jnp.broadcast_to(part[line : line + 1, :], (SUB, width))
                value = jnp.where(sub == ones + 1 + piece, spread, value)
            tail_ref[first + line] = value

    each(height // SUB, block)


def normal_stage(weight_ref, conv_ref, left_ref, right_ref):
    height, groups, _, width = conv_ref.shape
    size = right_ref.shape[0]
    tall = groups * SUB

    def one(row):
        design = conv_ref[row].reshape(tall, width)
        if size > tall:
            design = jnp.concatenate([design, jnp.zeros((size - tall, width), F32)], axis=0)
        weight = jnp.broadcast_to(weight_ref[pl.ds(row, 1), :], (size, width))
        high, low = split_bf16(design * weight, 2)
        where = lanes_of(row, width)
        left_ref[0:size, where] = high
        left_ref[size : 2 * size, where] = low
        right_ref[:, where] = design.astype(BF16)

    each(height, one)
    product = lax.dot_general(
        left_ref[...],
        right_ref[...],
        (((1,), (1,)), ((), ())),
        preferred_element_type=F32,
    )
    return product[0:size] + product[size : 2 * size]


def solve_stage(normal, kernels):
    unknowns = kernels + 1
    width = LANE
    groups = ceil_to(unknowns, SUB) // SUB
    size = normal.shape[1]
    parts = [normal[SUB * g : SUB * (g + 1)] for g in range(groups)]
    if size < width:
        parts = [
            jnp.concatenate([part, jnp.zeros((SUB, width - size), F32)], axis=1)
            for part in parts
        ]

    def pick(value, index, axis):
        where = jnp.full((SUB, width), index, jnp.int32)
        return jnp.take_along_axis(value, where, axis, mode="promise_in_bounds")

    def lane(value, index):
        return pick(value, index, 1)

    def sub(value, index):
        return pick(value, index, 0)

    total = [
        lane(p, unknowns) + (lane(p, unknowns + 1) + lane(p, unknowns + 2)) for p in parts
    ]
    column = lax.broadcasted_iota(jnp.int32, (SUB, width), 1)
    row = lax.broadcasted_iota(jnp.int32, (SUB, width), 0)
    parts = [jnp.where(column == unknowns, t, p) for p, t in zip(parts, total)]
    step = 0
    while step < unknowns:
        if step + 1 < unknowns:
            first, second = step, step + 1
            g0, s0, g1, s1 = first // SUB, first % SUB, second // SUB, second % SUB
            c0 = [lane(p, first) for p in parts]
            c1 = [lane(p, second) for p in parts]
            r0, r1 = sub(parts[g0], s0), sub(parts[g1], s1)
            a, b = lane(r0, first), lane(r0, second)
            e, d = lane(r1, first), lane(r1, second)
            inverse = 1.0 / (a * d - b * e)
            q0 = (d * inverse) * r0 - (b * inverse) * r1
            q1 = (a * inverse) * r1 - (e * inverse) * r0
            parts = [p - x * q0 - y * q1 for p, x, y in zip(parts, c0, c1)]
            parts[g0] = jnp.where(row == s0, q0, parts[g0])
            parts[g1] = jnp.where(row == s1, q1, parts[g1])
            step += 2
        else:
            g0, s0 = step // SUB, step % SUB
            c0 = [lane(p, step) for p in parts]
            r0 = sub(parts[g0], s0)
            q0 = r0 * (1.0 / lane(r0, step))
            parts = [p - x * q0 for p, x in zip(parts, c0)]
            parts[g0] = jnp.where(row == s0, q0, parts[g0])
            step += 1
    values = [lane(p, unknowns) for p in parts]
    last = [jnp.where(row + SUB * g < unknowns, v, 0.0) for g, v in enumerate(values)]
    return last


def residual_stage(values, conv_ref, sci_ref, inverse_ref, diff_ref, out_ref, rows_each):
    height, groups, _, width = conv_ref.shape

    def block(index):
        first = index * SUB
        if not isinstance(first, int):
            first = pl.multiple_of(first, SUB)
        lines = []
        for row in range(SUB):
            total = conv_ref[first + row, 0] * values[0]
            for group in range(1, groups):
                total = total + conv_ref[first + row, group] * values[group]
            lines.append(jnp.sum(total, axis=0, keepdims=True))
        model = jnp.concatenate(lines, axis=0)
        here = pl.ds(first, SUB)
        residual = sci_ref[here, :] - model
        inverse = inverse_ref[here, :]
        diff_ref[0, here, :] = residual * jnp.sqrt(inverse)
        weighted = residual * inverse
        for start in range(0, SUB, rows_each):
            target = (first + start) // rows_each
            out_ref[target, 0:rows_each, :] = weighted[start : start + rows_each]
            out_ref[target, rows_each : 2 * rows_each, :] = inverse[start : start + rows_each]

    each(height // SUB, block)


def store_coefficients(values, coef_ref, unknowns):
    row = lax.broadcasted_iota(jnp.int32, (SUB, LANE), 0)
    column = lax.broadcasted_iota(jnp.int32, (SUB, LANE), 1)
    total = jnp.zeros((SUB, LANE), F32)
    for group, value in enumerate(values):
        total = total + jnp.where(column == row + SUB * group, value, 0.0)
    coef_ref[...] = jnp.sum(total, axis=0, keepdims=True)[:, 0:unknowns]


def fit(tile, edge, science, variance, col_taps, row_taps, stamp_rows, stamp_cols, rows_each, sky):
    height, width = science.shape[1:]
    kernels, tap_count = col_taps.shape
    unknowns = kernels + 1
    groups = ceil_to(unknowns + 3, SUB) // SUB
    size = ceil_to(unknowns + 3, 2 * SUB)
    tall = ceil_to(kernels, 2 * SUB)
    rows, side = chunk_rows(height)
    local = sky == 1
    vmem = pl.BlockSpec(memory_space=pltpu.VMEM)
    smem = pl.BlockSpec(memory_space=pltpu.SMEM)
    params = pltpu.CompilerParams(vmem_limit_bytes=56 * 1024 * 1024)

    def result(shape, dtype=F32):
        return pltpu.VMEM(shape, dtype) if local else jax.ShapeDtypeStruct(shape, dtype)

    def operand(value):
        return pltpu.with_memory_space_constraint(value, pltpu.VMEM) if local else value

    def before(sci, var, ct, rt, sr, sc, flipped, band, weight, inverse, tail, image, pad):
        taps_stage(ct, rt, pad, flipped, band, height)
        weight_stage(sci, var, sr, sc, weight, inverse, tail, kernels)
        image[...] = sci[0]

    flipped, band, weight, inverse, tail, image = pl.pallas_call(
        before,
        out_shape=[
            result((tall, ceil_to(tap_count, SUB)), BF16),
            result((groups, SUB * rows, SUB * (rows + 2 * side)), BF16),
            result((height, width)),
            result((height, width)),
            result((height, SUB, width)),
            result((height, width)),
        ],
        in_specs=[vmem] * 4 + [smem] * 2,
        out_specs=[vmem] * 6,
        scratch_shapes=[pltpu.VMEM((tall, LANE), F32)],
        compiler_params=params,
        name="before",
    )(science, variance, col_taps, row_taps, stamp_rows, stamp_cols)

    conv_shape = (height, groups, SUB, width)
    out_shapes = [
        result((1, height, width)),
        result((1, unknowns)),
        result((height // rows_each, 2 * rows_each, width)),
    ]
    scratch = [
        pltpu.VMEM((groups, SUB * (height + 2 * side), width), BF16),
        pltpu.VMEM((2 * size, height * width), BF16),
        pltpu.VMEM((size, height * width), BF16),
    ]

    def front(tmpl, edges, flipped, band, weight, tail, conv, tmp):
        cols, left, right = tmp
        column_stage(tmpl, edges, flipped, cols, height, tap_count)
        row_stage(band, cols, tail, conv)
        return normal_stage(weight, conv, left, right)

    def back(normal, conv, sci, inverse, diff, coef, out):
        values = solve_stage(normal, kernels)
        store_coefficients(values, coef, unknowns)
        residual_stage(values, conv, sci, inverse, diff, out, rows_each)

    if local:

        def kernel(tmpl, flipped, band, weight, inverse, tail, image, diff, coef, out, conv, *tmp):
            normal = front(tmpl, None, flipped, band, weight, tail, conv, tmp)
            back(normal, conv, image, inverse, diff, coef, out)

        args = (tile, flipped, band, weight, inverse, tail, image)
        return pl.pallas_call(
            kernel,
            out_shape=out_shapes,
            in_specs=[vmem] * 7,
            out_specs=[vmem] * 3,
            scratch_shapes=[pltpu.VMEM(conv_shape, F32)] + scratch,
            compiler_params=params,
            name="fit",
        )(*[operand(arg) for arg in args])

    def first(tmpl, edges, flipped, band, weight, tail, conv, normal, *tmp):
        normal[...] = front(tmpl, edges, flipped, band, weight, tail, conv, tmp)

    conv, normal = pl.pallas_call(
        first,
        out_shape=[result(conv_shape), result((size, size))],
        in_specs=[vmem] * 6,
        out_specs=[vmem] * 2,
        scratch_shapes=scratch,
        compiler_params=params,
        name="fit_normal",
    )(tile.astype(F32), edge.astype(F32), flipped, band, weight, tail)
    normal = lax.psum(normal, "sky")

    def second(normal, conv, sci, inverse, diff, coef, out):
        back(normal[...], conv, sci, inverse, diff, coef, out)

    return pl.pallas_call(
        second,
        out_shape=out_shapes,
        in_specs=[vmem] * 4,
        out_specs=[vmem] * 3,
        compiler_params=params,
        name="fit_solve",
    )(normal, conv, image, inverse)


def sky_edges(tile, margin, sky):
    ends = sky - 1
    width = tile.shape[1]
    head = tile[:, 0:margin]
    tail = tile[:, width - margin :]
    after = lax.ppermute(head, "sky", [(i + 1, i) for i in range(ends)])
    before = lax.ppermute(tail, "sky", [(i, i + 1) for i in range(ends)])
    middle = jnp.zeros((tile.shape[0], width - 2 * margin), tile.dtype)
    return jnp.concatenate([after, middle, before], axis=1)


def solution(mesh):
    visits = mesh.shape["visit"]
    sky = mesh.shape["sky"]

    def on_device(template, science, variance, col_taps, row_taps, stamp_rows, stamp_cols):
        rows_each, width = template.shape
        margin = (col_taps.shape[1] - 1) // 2
        copies = jnp.broadcast_to(template[None], (visits, rows_each, width))
        tile = lax.all_to_all(copies, "visit", 0, 0, tiled=True).reshape(-1, width)
        edge = sky_edges(tile, margin, sky) if sky > 1 else None
        difference, coefficients, shares = fit(
            tile, edge, science, variance, col_taps, row_taps, stamp_rows, stamp_cols, rows_each, sky
        )
        shares = lax.all_to_all(shares, "visit", 0, 0, tiled=True)
        total = jnp.sum(shares, axis=0)
        detection = total[0:rows_each] / jnp.sqrt(total[rows_each:])
        return difference, coefficients, detection

    in_specs = (
        P(("group", "visit"), "sky"),
        P(("group", "visit"), None, "sky"),
        P(("group", "visit"), None, "sky"),
        P(),
        P(),
        P(("group", "visit"), "sky", None),
        P(("group", "visit"), "sky", None),
    )
    out_specs = (
        P(("group", "visit"), None, "sky"),
        P(("group", "visit"), None),
        P(("group", "visit"), "sky"),
    )
    return jax.shard_map(
        on_device, mesh=mesh, in_specs=in_specs, out_specs=out_specs, check_vma=False
    )
```

```python
import jax
import jax.numpy as jnp
from jax import lax
from jax.experimental import pallas as pl
from jax.experimental.pallas import tpu as pltpu
from jax.sharding import PartitionSpec as P

STAMP = 16
SUB = 8
LANE = 128
UNROLL = 32
CHUNK = 32
F32 = jnp.float32
BF16 = jnp.bfloat16


def ceil_to(value, step):
    return (value + step - 1) // step * step


def each(count, body):
    if count <= UNROLL:
        for index in range(count):
            body(index)
    else:
        lax.fori_loop(0, count, lambda index, carry: (body(index), carry)[1], 0)


def lanes_of(index, width):
    if isinstance(index, int):
        return slice(index * width, (index + 1) * width)
    return pl.ds(pl.multiple_of(index * width, width), width)


def split_bf16(value, pieces):
    out = []
    for piece in range(pieces):
        part = value.astype(BF16)
        out.append(part)
        if piece + 1 < pieces:
            value = value - part.astype(F32)
    return out


def load_taps(taps_ref, pad_ref):
    taps, kernels = taps_ref.shape
    pad_ref[...] = jnp.zeros(pad_ref.shape, F32)
    pad_ref[0:taps, 0:kernels] = taps_ref[...].astype(F32)
    return pad_ref[...].T


def chunk_rows(height):
    rows = min(CHUNK, height)
    return rows, (0 if rows == height else CHUNK // 2)


def taps_stage(col_taps_ref, row_taps_ref, pad_ref, flipped_ref, band_ref, height):
    tap_count = col_taps_ref.shape[0]
    margin = (tap_count - 1) // 2
    span = ceil_to(tap_count, SUB)
    groups = band_ref.shape[0]
    rows, side = chunk_rows(height)
    wide = SUB * (rows + 2 * side)
    taps = load_taps(col_taps_ref, pad_ref)[0 : flipped_ref.shape[0]]
    flip = (
        lax.broadcasted_iota(jnp.int32, (span, span), 0)
        + lax.broadcasted_iota(jnp.int32, (span, span), 1)
        == tap_count - 1
    ).astype(BF16)
    flipped_ref[...] = jnp.dot(
        taps[:, 0:span].astype(BF16), flip, preferred_element_type=F32
    ).astype(BF16)
    taps = load_taps(row_taps_ref, pad_ref)[0 : groups * SUB]
    repeat = (
        lax.broadcasted_iota(jnp.int32, (span, wide), 1) // SUB
        == lax.broadcasted_iota(jnp.int32, (span, wide), 0)
    ).astype(BF16)
    spread = jnp.dot(
        taps[:, 0:span].astype(BF16), repeat, preferred_element_type=F32
    )
    tall = groups * SUB
    lane = lax.broadcasted_iota(jnp.int32, (tall, wide), 1)
    own = lane % SUB == lax.broadcasted_iota(jnp.int32, (tall, wide), 0) % SUB
    spread = jnp.where(own, spread, 0.0)
    place = lane // SUB - side

    def line(row):
        moved = pltpu.roll(spread, (SUB * (row - margin + side)) % wide, 1)
        return jnp.where((place >= row - margin) & (place <= row + margin), moved, 0.0)

    for row in range(0, rows, 2):
        first, second = line(row), line(row + 1)
        for group in range(groups):
            here = slice(SUB * group, SUB * (group + 1))
            both = jnp.concatenate([first[here], second[here]], axis=0)
            band_ref[group, SUB * row : SUB * (row + 2), :] = both.astype(BF16)


def column_stage(tmpl_ref, edge_ref, flipped_ref, cols_ref, height, tap_count):
    width = tmpl_ref.shape[1]
    margin = (tap_count - 1) // 2
    span = ceil_to(tap_count, SUB)
    groups = cols_ref.shape[0]
    _, side = chunk_rows(height)
    taps = flipped_ref[...]
    place = lax.broadcasted_iota(jnp.int32, (span, width), 1) + (
        margin - lax.broadcasted_iota(jnp.int32, (span, width), 0)
    )
    inside = (place >= 0) & (place < width)
    if side:
        nothing = jnp.zeros((groups, SUB * side, width), BF16)
        cols_ref[:, 0 : SUB * side, :] = nothing
        cols_ref[:, SUB * (side + height) :, :] = nothing

    def shifted(row):
        line = jnp.broadcast_to(tmpl_ref[pl.ds(row, 1), :].astype(F32), (span, width))
        line = pltpu.roll(line, width - margin, 1, stride=1, stride_axis=0)
        if edge_ref is None:
            return jnp.where(inside, line, 0.0).astype(BF16)
        other = jnp.broadcast_to(edge_ref[pl.ds(row, 1), :].astype(F32), (span, width))
        other = pltpu.roll(other, width - margin, 1, stride=1, stride_axis=0)
        return jnp.where(inside, line, other).astype(BF16)

    def pair(index):
        both = jnp.concatenate([shifted(2 * index), shifted(2 * index + 1)], axis=1)
        result = jnp.dot(taps, both, preferred_element_type=F32)
        start = SUB * (2 * index + side)
        if not isinstance(start, int):
            start = pl.multiple_of(start, 2 * SUB)
        for group in range(groups):
            here = result[SUB * group : SUB * (group + 1)]
            two = jnp.concatenate([here[:, 0:width], here[:, width:]], axis=0)
            cols_ref[group, pl.ds(start, 2 * SUB), :] = two.astype(BF16)

    each(height // 2, pair)


def row_stage(band_ref, cols_ref, tail_ref, conv_ref):
    height, groups, _, width = conv_ref.shape
    rows, side = chunk_rows(height)

    def chunk(index):
        first = index * rows
        start = SUB * first
        if not isinstance(start, int):
            start = pl.multiple_of(start, SUB * rows)
        for group in range(groups):
            result = jnp.dot(
                band_ref[group],
                cols_ref[group, pl.ds(start, SUB * (rows + 2 * side)), :],
                preferred_element_type=F32,
            )
            for row in range(rows):
                value = result[SUB * row : SUB * (row + 1)].astype(BF16).astype(F32)
                if group == groups - 1:
                    value = value + tail_ref[first + row]
                conv_ref[first + row, group] = value

    each(height // rows, chunk)


def weight_stage(sci_ref, var_ref, rows_ref, cols_ref, weight_ref, inverse_ref, tail_ref, kernels):
    height, width = weight_ref.shape
    stamps = rows_ref.shape[-1]
    sub = lax.broadcasted_iota(jnp.int32, (SUB, width), 0)
    col = lax.broadcasted_iota(jnp.int32, (SUB, width), 1)
    ones = kernels % SUB

    def block(index):
        first = index * SUB
        row = sub + first
        count = jnp.zeros((SUB, width), F32)
        for stamp in range(stamps):
            down = row - rows_ref[0, 0, stamp]
            along = col - cols_ref[0, 0, stamp]
            held = (down >= 0) & (down < STAMP) & (along >= 0) & (along < STAMP)
            count = count + jnp.where(held, 1.0, 0.0)
        if not isinstance(first, int):
            first = pl.multiple_of(first, SUB)
        inverse = 1.0 / var_ref[0, pl.ds(first, SUB), :]
        inverse_ref[pl.ds(first, SUB), :] = inverse
        weight_ref[pl.ds(first, SUB), :] = inverse * count
        pieces = [p.astype(F32) for p in split_bf16(sci_ref[0, pl.ds(first, SUB), :], 3)]
        for line in range(SUB):
            value = jnp.where(sub == ones, 1.0, 0.0)
            for piece, part in enumerate(pieces):
                spread = jnp.broadcast_to(part[line : line + 1, :], (SUB, width))
                value = jnp.where(sub == ones + 1 + piece, spread, value)
            tail_ref[first + line] = value

    each(height // SUB, block)


def normal_stage(weight_ref, conv_ref, left_ref, right_ref):
    height, groups, _, width = conv_ref.shape
    size = right_ref.shape[0]
    tall = groups * SUB

    def one(row):
        design = conv_ref[row].reshape(tall, width)
        if size > tall:
            design = jnp.concatenate([design, jnp.zeros((size - tall, width), F32)], axis=0)
        weight = jnp.broadcast_to(weight_ref[pl.ds(row, 1), :], (size, width))
        high, low = split_bf16(design * weight, 2)
        where = lanes_of(row, width)
        left_ref[0:size, where] = high
        left_ref[size : 2 * size, where] = low
        right_ref[:, where] = design.astype(BF16)

    each(height, one)
    product = lax.dot_general(
        left_ref[...],
        right_ref[...],
        (((1,), (1,)), ((), ())),
        preferred_element_type=F32,
    )
    return product[0:size] + product[size : 2 * size]


def solve_stage(normal, kernels):
    unknowns = kernels + 1
    width = LANE
    groups = ceil_to(unknowns, SUB) // SUB
    size = normal.shape[1]
    parts = [normal[SUB * g : SUB * (g + 1)] for g in range(groups)]
    if size < width:
        parts = [
            jnp.concatenate([part, jnp.zeros((SUB, width - size), F32)], axis=1)
            for part in parts
        ]

    def pick(value, index, axis):
        where = jnp.full((SUB, width), index, jnp.int32)
        return jnp.take_along_axis(value, where, axis, mode="promise_in_bounds")

    def lane(value, index):
        return pick(value, index, 1)

    def sub(value, index):
        return pick(value, index, 0)

    total = [
        lane(p, unknowns) + (lane(p, unknowns + 1) + lane(p, unknowns + 2)) for p in parts
    ]
    column = lax.broadcasted_iota(jnp.int32, (SUB, width), 1)
    row = lax.broadcasted_iota(jnp.int32, (SUB, width), 0)
    parts = [jnp.where(column == unknowns, t, p) for p, t in zip(parts, total)]
    step = 0
    while step < unknowns:
        if step + 1 < unknowns:
            first, second = step, step + 1
            g0, s0, g1, s1 = first // SUB, first % SUB, second // SUB, second % SUB
            c0 = [lane(p, first) for p in parts]
            c1 = [lane(p, second) for p in parts]
            r0, r1 = sub(parts[g0], s0), sub(parts[g1], s1)
            a, b = lane(r0, first), lane(r0, second)
            e, d = lane(r1, first), lane(r1, second)
            inverse = 1.0 / (a * d - b * e)
            q0 = (d * inverse) * r0 - (b * inverse) * r1
            q1 = (a * inverse) * r1 - (e * inverse) * r0
            parts = [p - x * q0 - y * q1 for p, x, y in zip(parts, c0, c1)]
            parts[g0] = jnp.where(row == s0, q0, parts[g0])
            parts[g1] = jnp.where(row == s1, q1, parts[g1])
            step += 2
        else:
            g0, s0 = step // SUB, step % SUB
            c0 = [lane(p, step) for p in parts]
            r0 = sub(parts[g0], s0)
            q0 = r0 * (1.0 / lane(r0, step))
            parts = [p - x * q0 for p, x in zip(parts, c0)]
            parts[g0] = jnp.where(row == s0, q0, parts[g0])
            step += 1
    values = [lane(p, unknowns) for p in parts]
    last = [jnp.where(row + SUB * g < unknowns, v, 0.0) for g, v in enumerate(values)]
    return last


def residual_stage(values, conv_ref, sci_ref, inverse_ref, diff_ref, out_ref, rows_each):
    height, groups, _, width = conv_ref.shape

    def block(index):
        first = index * SUB
        if not isinstance(first, int):
            first = pl.multiple_of(first, SUB)
        lines = []
        for row in range(SUB):
            total = conv_ref[first + row, 0] * values[0]
            for group in range(1, groups):
                total = total + conv_ref[first + row, group] * values[group]
            lines.append(jnp.sum(total, axis=0, keepdims=True))
        model = jnp.concatenate(lines, axis=0)
        here = pl.ds(first, SUB)
        residual = sci_ref[here, :] - model
        inverse = inverse_ref[here, :]
        diff_ref[0, here, :] = residual * jnp.sqrt(inverse)
        weighted = residual * inverse
        for start in range(0, SUB, rows_each):
            target = (first + start) // rows_each
            out_ref[target, 0:rows_each, :] = weighted[start : start + rows_each]
            out_ref[target, rows_each : 2 * rows_each, :] = inverse[start : start + rows_each]

    each(height // SUB, block)


def store_coefficients(values, coef_ref, unknowns):
    row = lax.broadcasted_iota(jnp.int32, (SUB, LANE), 0)
    column = lax.broadcasted_iota(jnp.int32, (SUB, LANE), 1)
    total = jnp.zeros((SUB, LANE), F32)
    for group, value in enumerate(values):
        total = total + jnp.where(column == row + SUB * group, value, 0.0)
    coef_ref[...] = jnp.sum(total, axis=0, keepdims=True)[:, 0:unknowns]


def fit(tile, edge, science, variance, col_taps, row_taps, stamp_rows, stamp_cols, rows_each, sky):
    height, width = science.shape[1:]
    kernels, tap_count = col_taps.shape
    unknowns = kernels + 1
    groups = ceil_to(unknowns + 3, SUB) // SUB
    size = ceil_to(unknowns + 3, 2 * SUB)
    tall = ceil_to(kernels, 2 * SUB)
    rows, side = chunk_rows(height)
    local = sky == 1
    vmem = pl.BlockSpec(memory_space=pltpu.VMEM)
    smem = pl.BlockSpec(memory_space=pltpu.SMEM)
    params = pltpu.CompilerParams(vmem_limit_bytes=56 * 1024 * 1024)

    def result(shape, dtype=F32):
        return pltpu.VMEM(shape, dtype) if local else jax.ShapeDtypeStruct(shape, dtype)

    def operand(value):
        return pltpu.with_memory_space_constraint(value, pltpu.VMEM) if local else value

    def before(sci, var, ct, rt, sr, sc, flipped, band, weight, inverse, tail, image, pad):
        taps_stage(ct, rt, pad, flipped, band, height)
        weight_stage(sci, var, sr, sc, weight, inverse, tail, kernels)
        image[...] = sci[0]

    flipped, band, weight, inverse, tail, image = pl.pallas_call(
        before,
        out_shape=[
            result((tall, ceil_to(tap_count, SUB)), BF16),
            result((groups, SUB * rows, SUB * (rows + 2 * side)), BF16),
            result((height, width)),
            result((height, width)),
            result((height, SUB, width)),
            result((height, width)),
        ],
        in_specs=[vmem] * 4 + [smem] * 2,
        out_specs=[vmem] * 6,
        scratch_shapes=[pltpu.VMEM((LANE, LANE), F32)],
        compiler_params=params,
        name="before",
    )(science, variance, col_taps.T, row_taps.T, stamp_rows, stamp_cols)

    conv_shape = (height, groups, SUB, width)
    out_shapes = [
        result((1, height, width)),
        result((1, unknowns)),
        result((height // rows_each, 2 * rows_each, width)),
    ]
    scratch = [
        pltpu.VMEM((groups, SUB * (height + 2 * side), width), BF16),
        pltpu.VMEM((2 * size, height * width), BF16),
        pltpu.VMEM((size, height * width), BF16),
    ]

    def front(tmpl, edges, flipped, band, weight, tail, conv, tmp):
        cols, left, right = tmp
        column_stage(tmpl, edges, flipped, cols, height, tap_count)
        row_stage(band, cols, tail, conv)
        return normal_stage(weight, conv, left, right)

    def back(normal, conv, sci, inverse, diff, coef, out):
        values = solve_stage(normal, kernels)
        store_coefficients(values, coef, unknowns)
        residual_stage(values, conv, sci, inverse, diff, out, rows_each)

    if local:

        def kernel(tmpl, flipped, band, weight, inverse, tail, image, diff, coef, out, conv, *tmp):
            normal = front(tmpl, None, flipped, band, weight, tail, conv, tmp)
            back(normal, conv, image, inverse, diff, coef, out)

        args = (tile, flipped, band, weight, inverse, tail, image)
        return pl.pallas_call(
            kernel,
            out_shape=out_shapes,
            in_specs=[vmem] * 7,
            out_specs=[vmem] * 3,
            scratch_shapes=[pltpu.VMEM(conv_shape, F32)] + scratch,
            compiler_params=params,
            name="fit",
        )(*[operand(arg) for arg in args])

    def first(tmpl, edges, flipped, band, weight, tail, conv, normal, *tmp):
        normal[...] = front(tmpl, edges, flipped, band, weight, tail, conv, tmp)

    conv, normal = pl.pallas_call(
        first,
        out_shape=[result(conv_shape), result((size, size))],
        in_specs=[vmem] * 6,
        out_specs=[vmem] * 2,
        scratch_shapes=scratch,
        compiler_params=params,
        name="fit_normal",
    )(tile.astype(F32), edge.astype(F32), flipped, band, weight, tail)
    normal = lax.psum(normal, "sky")

    def second(normal, conv, sci, inverse, diff, coef, out):
        back(normal[...], conv, sci, inverse, diff, coef, out)

    return pl.pallas_call(
        second,
        out_shape=out_shapes,
        in_specs=[vmem] * 4,
        out_specs=[vmem] * 3,
        compiler_params=params,
        name="fit_solve",
    )(normal, conv, image, inverse)


def sky_edges(tile, margin, sky):
    ends = sky - 1
    width = tile.shape[1]
    head = tile[:, 0:margin]
    tail = tile[:, width - margin :]
    after = lax.ppermute(head, "sky", [(i + 1, i) for i in range(ends)])
    before = lax.ppermute(tail, "sky", [(i, i + 1) for i in range(ends)])
    middle = jnp.zeros((tile.shape[0], width - 2 * margin), tile.dtype)
    return jnp.concatenate([after, middle, before], axis=1)


def gather_results(shares, difference, coefficients):
    rows_each = shares.shape[1] // 2

    def kernel(shares_ref, diff_ref, coef_ref, diff_out, coef_out, out_ref):
        diff_out[...] = diff_ref[...]
        coef_out[...] = coef_ref[...]
        total = jnp.sum(shares_ref[...], axis=0)
        out_ref[...] = total[0:rows_each] / jnp.sqrt(total[rows_each:])

    vmem = pl.BlockSpec(memory_space=pltpu.VMEM)
    args = (shares, difference, coefficients)
    return pl.pallas_call(
        kernel,
        out_shape=[
            jax.ShapeDtypeStruct(difference.shape, F32),
            jax.ShapeDtypeStruct(coefficients.shape, F32),
            jax.ShapeDtypeStruct((rows_each, shares.shape[2]), F32),
        ],
        in_specs=[vmem] * 3,
        out_specs=[vmem] * 3,
        name="results",
    )(*[pltpu.with_memory_space_constraint(arg, pltpu.VMEM) for arg in args])


def solution(mesh):
    visits = mesh.shape["visit"]
    sky = mesh.shape["sky"]

    def on_device(template, science, variance, col_taps, row_taps, stamp_rows, stamp_cols):
        rows_each, width = template.shape
        margin = (col_taps.shape[1] - 1) // 2
        copies = jnp.broadcast_to(template[None], (visits, rows_each, width))
        tile = lax.all_to_all(copies, "visit", 0, 0, tiled=True).reshape(-1, width)
        edge = sky_edges(tile, margin, sky) if sky > 1 else None
        difference, coefficients, shares = fit(
            tile, edge, science, variance, col_taps, row_taps, stamp_rows, stamp_cols, rows_each, sky
        )
        shares = lax.all_to_all(shares, "visit", 0, 0, tiled=True)
        if sky == 1:
            return gather_results(shares, difference, coefficients)
        total = jnp.sum(shares, axis=0)
        detection = total[0:rows_each] / jnp.sqrt(total[rows_each:])
        return difference, coefficients, detection

    in_specs = (
        P(("group", "visit"), "sky"),
        P(("group", "visit"), None, "sky"),
        P(("group", "visit"), None, "sky"),
        P(),
        P(),
        P(("group", "visit"), "sky", None),
        P(("group", "visit"), "sky", None),
    )
    out_specs = (
        P(("group", "visit"), None, "sky"),
        P(("group", "visit"), None),
        P(("group", "visit"), "sky"),
    )
    return jax.shard_map(
        on_device, mesh=mesh, in_specs=in_specs, out_specs=out_specs, check_vma=False
    )
```

```python
import jax
import jax.numpy as jnp
from jax import lax
from jax.experimental import pallas as pl
from jax.experimental.pallas import tpu as pltpu
from jax.sharding import PartitionSpec as P

STAMP = 16
SUB = 8
LANE = 128
UNROLL = 32
CHUNK = 32
F32 = jnp.float32
BF16 = jnp.bfloat16


def ceil_to(value, step):
    return (value + step - 1) // step * step


def each(count, body):
    if count <= UNROLL:
        for index in range(count):
            body(index)
    else:
        lax.fori_loop(0, count, lambda index, carry: (body(index), carry)[1], 0)


def lanes_of(index, width):
    if isinstance(index, int):
        return slice(index * width, (index + 1) * width)
    return pl.ds(pl.multiple_of(index * width, width), width)


def split_bf16(value, pieces):
    out = []
    for piece in range(pieces):
        part = value.astype(BF16)
        out.append(part)
        if piece + 1 < pieces:
            value = value - part.astype(F32)
    return out


def load_taps(taps_ref, pad_ref):
    taps, kernels = taps_ref.shape
    pad_ref[...] = jnp.zeros(pad_ref.shape, F32)
    pad_ref[0:taps, 0:kernels] = taps_ref[...].astype(F32)
    return pad_ref[...].T


def chunk_rows(height):
    rows = min(CHUNK, height)
    return rows, (0 if rows == height else CHUNK // 2)


def taps_stage(col_taps_ref, row_taps_ref, pad_ref, flipped_ref, band_ref, height):
    tap_count = col_taps_ref.shape[0]
    margin = (tap_count - 1) // 2
    span = ceil_to(tap_count, SUB)
    groups = band_ref.shape[0]
    rows, side = chunk_rows(height)
    wide = SUB * (rows + 2 * side)
    taps = load_taps(col_taps_ref, pad_ref)[0 : flipped_ref.shape[0]]
    flip = (
        lax.broadcasted_iota(jnp.int32, (span, span), 0)
        + lax.broadcasted_iota(jnp.int32, (span, span), 1)
        == tap_count - 1
    ).astype(BF16)
    flipped_ref[...] = jnp.dot(
        taps[:, 0:span].astype(BF16), flip, preferred_element_type=F32
    ).astype(BF16)
    taps = load_taps(row_taps_ref, pad_ref)[0 : groups * SUB]
    repeat = (
        lax.broadcasted_iota(jnp.int32, (span, wide), 1) // SUB
        == lax.broadcasted_iota(jnp.int32, (span, wide), 0)
    ).astype(BF16)
    spread = jnp.dot(
        taps[:, 0:span].astype(BF16), repeat, preferred_element_type=F32
    )
    tall = groups * SUB
    lane = lax.broadcasted_iota(jnp.int32, (tall, wide), 1)
    own = lane % SUB == lax.broadcasted_iota(jnp.int32, (tall, wide), 0) % SUB
    spread = jnp.where(own, spread, 0.0)
    place = lane // SUB - side

    def line(row):
        moved = pltpu.roll(spread, (SUB * (row - margin + side)) % wide, 1)
        return jnp.where((place >= row - margin) & (place <= row + margin), moved, 0.0)

    for row in range(0, rows, 2):
        first, second = line(row), line(row + 1)
        for group in range(groups):
            here = slice(SUB * group, SUB * (group + 1))
            both = jnp.concatenate([first[here], second[here]], axis=0)
            band_ref[group, SUB * row : SUB * (row + 2), :] = both.astype(BF16)


def column_stage(tmpl_ref, edge_ref, flipped_ref, cols_ref, height, tap_count):
    width = tmpl_ref.shape[1]
    margin = (tap_count - 1) // 2
    span = ceil_to(tap_count, SUB)
    groups = cols_ref.shape[0]
    _, side = chunk_rows(height)
    taps = flipped_ref[...]
    place = lax.broadcasted_iota(jnp.int32, (span, width), 1) + (
        margin - lax.broadcasted_iota(jnp.int32, (span, width), 0)
    )
    inside = (place >= 0) & (place < width)
    if side:
        nothing = jnp.zeros((groups, SUB * side, width), BF16)
        cols_ref[:, 0 : SUB * side, :] = nothing
        cols_ref[:, SUB * (side + height) :, :] = nothing

    def shifted(row):
        line = jnp.broadcast_to(tmpl_ref[pl.ds(row, 1), :].astype(F32), (span, width))
        line = pltpu.roll(line, width - margin, 1, stride=1, stride_axis=0)
        if edge_ref is None:
            return jnp.where(inside, line, 0.0).astype(BF16)
        other = jnp.broadcast_to(edge_ref[pl.ds(row, 1), :].astype(F32), (span, width))
        other = pltpu.roll(other, width - margin, 1, stride=1, stride_axis=0)
        return jnp.where(inside, line, other).astype(BF16)

    def pair(index):
        both = jnp.concatenate([shifted(2 * index), shifted(2 * index + 1)], axis=1)
        result = jnp.dot(taps, both, preferred_element_type=F32)
        start = SUB * (2 * index + side)
        if not isinstance(start, int):
            start = pl.multiple_of(start, 2 * SUB)
        for group in range(groups):
            here = result[SUB * group : SUB * (group + 1)]
            two = jnp.concatenate([here[:, 0:width], here[:, width:]], axis=0)
            cols_ref[group, pl.ds(start, 2 * SUB), :] = two.astype(BF16)

    each(height // 2, pair)


def row_stage(band_ref, cols_ref, tail_ref, conv_ref):
    height, groups, _, width = conv_ref.shape
    rows, side = chunk_rows(height)

    def chunk(index):
        first = index * rows
        start = SUB * first
        if not isinstance(start, int):
            start = pl.multiple_of(start, SUB * rows)
        for group in range(groups):
            result = jnp.dot(
                band_ref[group],
                cols_ref[group, pl.ds(start, SUB * (rows + 2 * side)), :],
                preferred_element_type=F32,
            )
            for row in range(rows):
                value = result[SUB * row : SUB * (row + 1)].astype(BF16).astype(F32)
                if group == groups - 1:
                    value = value + tail_ref[first + row]
                conv_ref[first + row, group] = value

    each(height // rows, chunk)


def weight_stage(sci_ref, var_ref, rows_ref, cols_ref, weight_ref, inverse_ref, tail_ref, kernels):
    height, width = weight_ref.shape
    stamps = rows_ref.shape[-1]
    sub = lax.broadcasted_iota(jnp.int32, (SUB, width), 0)
    col = lax.broadcasted_iota(jnp.int32, (SUB, width), 1)
    ones = kernels % SUB

    def block(index):
        first = index * SUB
        row = sub + first
        count = jnp.zeros((SUB, width), F32)
        for stamp in range(stamps):
            down = row - rows_ref[0, 0, stamp]
            along = col - cols_ref[0, 0, stamp]
            held = (down >= 0) & (down < STAMP) & (along >= 0) & (along < STAMP)
            count = count + jnp.where(held, 1.0, 0.0)
        if not isinstance(first, int):
            first = pl.multiple_of(first, SUB)
        inverse = 1.0 / var_ref[0, pl.ds(first, SUB), :]
        inverse_ref[pl.ds(first, SUB), :] = inverse
        weight_ref[pl.ds(first, SUB), :] = inverse * count
        pieces = [p.astype(F32) for p in split_bf16(sci_ref[0, pl.ds(first, SUB), :], 3)]
        for line in range(SUB):
            value = jnp.where(sub == ones, 1.0, 0.0)
            for piece, part in enumerate(pieces):
                spread = jnp.broadcast_to(part[line : line + 1, :], (SUB, width))
                value = jnp.where(sub == ones + 1 + piece, spread, value)
            tail_ref[first + line] = value

    each(height // SUB, block)


def normal_stage(weight_ref, conv_ref, left_ref, right_ref):
    height, groups, _, width = conv_ref.shape
    size = right_ref.shape[0]
    tall = groups * SUB

    def one(row):
        design = conv_ref[row].reshape(tall, width)
        if size > tall:
            design = jnp.concatenate([design, jnp.zeros((size - tall, width), F32)], axis=0)
        weight = jnp.broadcast_to(weight_ref[pl.ds(row, 1), :], (size, width))
        high, low = split_bf16(design * weight, 2)
        where = lanes_of(row, width)
        left_ref[0:size, where] = high
        left_ref[size : 2 * size, where] = low
        right_ref[:, where] = design.astype(BF16)

    each(height, one)
    product = lax.dot_general(
        left_ref[...],
        right_ref[...],
        (((1,), (1,)), ((), ())),
        preferred_element_type=F32,
    )
    return product[0:size] + product[size : 2 * size]


def solve_stage(normal, kernels):
    unknowns = kernels + 1
    width = LANE
    groups = ceil_to(unknowns, SUB) // SUB
    size = normal.shape[1]
    parts = [normal[SUB * g : SUB * (g + 1)] for g in range(groups)]
    if size < width:
        parts = [
            jnp.concatenate([part, jnp.zeros((SUB, width - size), F32)], axis=1)
            for part in parts
        ]

    def pick(value, index, axis):
        where = jnp.full((SUB, width), index, jnp.int32)
        return jnp.take_along_axis(value, where, axis, mode="promise_in_bounds")

    row = lax.broadcasted_iota(jnp.int32, (SUB, width), 0)

    def reduce_pair(values, at, first, second):
        own, line = at // SUB, at % SUB
        a, b = pick(first[own], line, 0), pick(second[own], line, 0)
        d = pick(second[own], line + 1, 0)
        inverse = 1.0 / (a * d - b * b)
        a, b, d = a * inverse, b * inverse, d * inverse

        def update(value):
            r0, r1 = pick(value[own], line, 0), pick(value[own], line + 1, 0)
            q0 = d * r0 - b * r1
            q1 = a * r1 - b * r0
            value = [v - x * q0 - y * q1 for v, x, y in zip(value, first, second)]
            value[own] = jnp.where(row == line, q0, jnp.where(row == line + 1, q1, value[own]))
            return value

        return [update(value) for value in values]

    def reduce_last(values, at, first):
        own, line = at // SUB, at % SUB
        inverse = 1.0 / pick(first[own], line, 0)

        def update(value):
            q0 = pick(value[own], line, 0) * inverse
            value = [v - x * q0 for v, x in zip(value, first)]
            value[own] = jnp.where(row == line, q0, value[own])
            return value

        return [update(value) for value in values]

    edges = [0] + list(range(2 - groups % 2, groups + 1, 2))
    for low, high in zip(edges[:-1], edges[1:]):
        members = range(low, high)
        count = min(SUB * high, unknowns) - SUB * low
        copied = [
            [pick(part, SUB * low + index, 1) for part in parts] for index in range(count)
        ]
        columns = [[one[g] for g in members] for one in copied]
        block = [parts[g] for g in members]
        at = 0
        while at < count:
            if at + 1 < count:
                rest = reduce_pair(columns[at + 2 :] + [block], at, columns[at], columns[at + 1])
                at += 2
            else:
                rest = reduce_last(columns[at + 1 :] + [block], at, columns[at])
                at += 1
            columns[at:], block = rest[:-1], rest[-1]
        lines = [pick(block[index // SUB], index % SUB, 0) for index in range(count)]
        for group in range(groups):
            if group in members:
                parts[group] = block[group - low]
                continue
            terms = [copied[index][group] * lines[index] for index in range(count)]
            while len(terms) > 1:
                terms = [sum(terms[i : i + 2][1:], terms[i]) for i in range(0, len(terms), 2)]
            parts[group] = parts[group] - terms[0]
    values = [
        pick(p, unknowns, 1) + (pick(p, unknowns + 1, 1) + pick(p, unknowns + 2, 1))
        for p in parts
    ]
    return [jnp.where(row + SUB * g < unknowns, v, 0.0) for g, v in enumerate(values)]


def residual_stage(values, conv_ref, sci_ref, inverse_ref, diff_ref, out_ref, rows_each):
    height, groups, _, width = conv_ref.shape

    def block(index):
        first = index * SUB
        if not isinstance(first, int):
            first = pl.multiple_of(first, SUB)
        lines = []
        for row in range(SUB):
            total = conv_ref[first + row, 0] * values[0]
            for group in range(1, groups):
                total = total + conv_ref[first + row, group] * values[group]
            lines.append(jnp.sum(total, axis=0, keepdims=True))
        model = jnp.concatenate(lines, axis=0)
        here = pl.ds(first, SUB)
        residual = sci_ref[here, :] - model
        inverse = inverse_ref[here, :]
        diff_ref[0, here, :] = residual * jnp.sqrt(inverse)
        weighted = residual * inverse
        for start in range(0, SUB, rows_each):
            target = (first + start) // rows_each
            out_ref[target, 0:rows_each, :] = weighted[start : start + rows_each]
            out_ref[target, rows_each : 2 * rows_each, :] = inverse[start : start + rows_each]

    each(height // SUB, block)


def store_coefficients(values, coef_ref, unknowns):
    row = lax.broadcasted_iota(jnp.int32, (SUB, LANE), 0)
    column = lax.broadcasted_iota(jnp.int32, (SUB, LANE), 1)
    total = jnp.zeros((SUB, LANE), F32)
    for group, value in enumerate(values):
        total = total + jnp.where(column == row + SUB * group, value, 0.0)
    coef_ref[...] = jnp.sum(total, axis=0, keepdims=True)[:, 0:unknowns]


def fit(tile, edge, science, variance, col_taps, row_taps, stamp_rows, stamp_cols, rows_each, sky):
    height, width = science.shape[1:]
    kernels, tap_count = col_taps.shape
    unknowns = kernels + 1
    groups = ceil_to(unknowns + 3, SUB) // SUB
    size = ceil_to(unknowns + 3, 2 * SUB)
    tall = ceil_to(kernels, 2 * SUB)
    rows, side = chunk_rows(height)
    local = sky == 1
    vmem = pl.BlockSpec(memory_space=pltpu.VMEM)
    smem = pl.BlockSpec(memory_space=pltpu.SMEM)
    params = pltpu.CompilerParams(vmem_limit_bytes=56 * 1024 * 1024)

    def result(shape, dtype=F32):
        return pltpu.VMEM(shape, dtype) if local else jax.ShapeDtypeStruct(shape, dtype)

    def operand(value):
        return pltpu.with_memory_space_constraint(value, pltpu.VMEM) if local else value

    def before(sci, var, ct, rt, sr, sc, flipped, band, weight, inverse, tail, image, pad):
        taps_stage(ct, rt, pad, flipped, band, height)
        weight_stage(sci, var, sr, sc, weight, inverse, tail, kernels)
        image[...] = sci[0]

    flipped, band, weight, inverse, tail, image = pl.pallas_call(
        before,
        out_shape=[
            result((tall, ceil_to(tap_count, SUB)), BF16),
            result((groups, SUB * rows, SUB * (rows + 2 * side)), BF16),
            result((height, width)),
            result((height, width)),
            result((height, SUB, width)),
            result((height, width)),
        ],
        in_specs=[vmem] * 4 + [smem] * 2,
        out_specs=[vmem] * 6,
        scratch_shapes=[pltpu.VMEM((LANE, LANE), F32)],
        compiler_params=params,
        name="before",
    )(science, variance, col_taps.T, row_taps.T, stamp_rows, stamp_cols)

    conv_shape = (height, groups, SUB, width)
    out_shapes = [
        result((1, height, width)),
        result((1, unknowns)),
        result((height // rows_each, 2 * rows_each, width)),
    ]
    scratch = [
        pltpu.VMEM((groups, SUB * (height + 2 * side), width), BF16),
        pltpu.VMEM((2 * size, height * width), BF16),
        pltpu.VMEM((size, height * width), BF16),
    ]

    def front(tmpl, edges, flipped, band, weight, tail, conv, tmp):
        cols, left, right = tmp
        column_stage(tmpl, edges, flipped, cols, height, tap_count)
        row_stage(band, cols, tail, conv)
        return normal_stage(weight, conv, left, right)

    def back(normal, conv, sci, inverse, diff, coef, out):
        values = solve_stage(normal, kernels)
        store_coefficients(values, coef, unknowns)
        residual_stage(values, conv, sci, inverse, diff, out, rows_each)

    if local:

        def kernel(tmpl, flipped, band, weight, inverse, tail, image, diff, coef, out, conv, *tmp):
            normal = front(tmpl, None, flipped, band, weight, tail, conv, tmp)
            back(normal, conv, image, inverse, diff, coef, out)

        args = (tile, flipped, band, weight, inverse, tail, image)
        return pl.pallas_call(
            kernel,
            out_shape=out_shapes,
            in_specs=[vmem] * 7,
            out_specs=[vmem] * 3,
            scratch_shapes=[pltpu.VMEM(conv_shape, F32)] + scratch,
            compiler_params=params,
            name="fit",
        )(*[operand(arg) for arg in args])

    def first(tmpl, edges, flipped, band, weight, tail, conv, normal, *tmp):
        normal[...] = front(tmpl, edges, flipped, band, weight, tail, conv, tmp)

    conv, normal = pl.pallas_call(
        first,
        out_shape=[result(conv_shape), result((size, size))],
        in_specs=[vmem] * 6,
        out_specs=[vmem] * 2,
        scratch_shapes=scratch,
        compiler_params=params,
        name="fit_normal",
    )(tile.astype(F32), edge.astype(F32), flipped, band, weight, tail)
    normal = lax.psum(normal, "sky")

    def second(normal, conv, sci, inverse, diff, coef, out):
        back(normal[...], conv, sci, inverse, diff, coef, out)

    return pl.pallas_call(
        second,
        out_shape=out_shapes,
        in_specs=[vmem] * 4,
        out_specs=[vmem] * 3,
        compiler_params=params,
        name="fit_solve",
    )(normal, conv, image, inverse)


def sky_edges(tile, margin, sky):
    ends = sky - 1
    width = tile.shape[1]
    head = tile[:, 0:margin]
    tail = tile[:, width - margin :]
    after = lax.ppermute(head, "sky", [(i + 1, i) for i in range(ends)])
    before = lax.ppermute(tail, "sky", [(i, i + 1) for i in range(ends)])
    middle = jnp.zeros((tile.shape[0], width - 2 * margin), tile.dtype)
    return jnp.concatenate([after, middle, before], axis=1)


def gather_results(shares, difference, coefficients):
    rows_each = shares.shape[1] // 2

    def kernel(shares_ref, diff_ref, coef_ref, diff_out, coef_out, out_ref):
        diff_out[...] = diff_ref[...]
        coef_out[...] = coef_ref[...]
        total = jnp.sum(shares_ref[...], axis=0)
        out_ref[...] = total[0:rows_each] / jnp.sqrt(total[rows_each:])

    vmem = pl.BlockSpec(memory_space=pltpu.VMEM)
    args = (shares, difference, coefficients)
    return pl.pallas_call(
        kernel,
        out_shape=[
            jax.ShapeDtypeStruct(difference.shape, F32),
            jax.ShapeDtypeStruct(coefficients.shape, F32),
            jax.ShapeDtypeStruct((rows_each, shares.shape[2]), F32),
        ],
        in_specs=[vmem] * 3,
        out_specs=[vmem] * 3,
        name="results",
    )(*[pltpu.with_memory_space_constraint(arg, pltpu.VMEM) for arg in args])


def solution(mesh):
    visits = mesh.shape["visit"]
    sky = mesh.shape["sky"]

    def on_device(template, science, variance, col_taps, row_taps, stamp_rows, stamp_cols):
        rows_each, width = template.shape
        margin = (col_taps.shape[1] - 1) // 2
        copies = jnp.broadcast_to(template[None], (visits, rows_each, width))
        tile = lax.all_to_all(copies, "visit", 0, 0, tiled=True).reshape(-1, width)
        edge = sky_edges(tile, margin, sky) if sky > 1 else None
        difference, coefficients, shares = fit(
            tile, edge, science, variance, col_taps, row_taps, stamp_rows, stamp_cols, rows_each, sky
        )
        shares = lax.all_to_all(shares, "visit", 0, 0, tiled=True)
        if sky == 1:
            return gather_results(shares, difference, coefficients)
        total = jnp.sum(shares, axis=0)
        detection = total[0:rows_each] / jnp.sqrt(total[rows_each:])
        return difference, coefficients, detection

    in_specs = (
        P(("group", "visit"), "sky"),
        P(("group", "visit"), None, "sky"),
        P(("group", "visit"), None, "sky"),
        P(),
        P(),
        P(("group", "visit"), "sky", None),
        P(("group", "visit"), "sky", None),
    )
    out_specs = (
        P(("group", "visit"), None, "sky"),
        P(("group", "visit"), None),
        P(("group", "visit"), "sky"),
    )
    return jax.shard_map(
        on_device, mesh=mesh, in_specs=in_specs, out_specs=out_specs, check_vma=False
    )
```

```python
import jax
import jax.numpy as jnp
from jax import lax
from jax.experimental import pallas as pl
from jax.experimental.pallas import tpu as pltpu
from jax.sharding import PartitionSpec as P

STAMP = 16
SUB = 8
LANE = 128
UNROLL = 32
CHUNK = 32
F32 = jnp.float32
BF16 = jnp.bfloat16


def ceil_to(value, step):
    return (value + step - 1) // step * step


def each(count, body):
    if count <= UNROLL:
        for index in range(count):
            body(index)
    else:
        lax.fori_loop(0, count, lambda index, carry: (body(index), carry)[1], 0)


def lanes_of(index, width):
    if isinstance(index, int):
        return slice(index * width, (index + 1) * width)
    return pl.ds(pl.multiple_of(index * width, width), width)


def split_bf16(value, pieces):
    out = []
    for piece in range(pieces):
        part = value.astype(BF16)
        out.append(part)
        if piece + 1 < pieces:
            value = value - part.astype(F32)
    return out


def load_taps(taps_ref, pad_ref):
    taps, kernels = taps_ref.shape
    pad_ref[...] = jnp.zeros(pad_ref.shape, F32)
    pad_ref[0:taps, 0:kernels] = taps_ref[...].astype(F32)
    return pad_ref[...].T


def chunk_rows(height):
    rows = min(CHUNK, height)
    return rows, (0 if rows == height else CHUNK // 2)


def taps_stage(col_taps_ref, row_taps_ref, pad_ref, flipped_ref, band_ref, height):
    tap_count = col_taps_ref.shape[0]
    margin = (tap_count - 1) // 2
    span = ceil_to(tap_count, SUB)
    groups = band_ref.shape[0]
    rows, side = chunk_rows(height)
    wide = SUB * (rows + 2 * side)
    taps = load_taps(col_taps_ref, pad_ref)[0 : flipped_ref.shape[0]]
    flip = (
        lax.broadcasted_iota(jnp.int32, (span, span), 0)
        + lax.broadcasted_iota(jnp.int32, (span, span), 1)
        == tap_count - 1
    ).astype(BF16)
    flipped_ref[...] = jnp.dot(
        taps[:, 0:span].astype(BF16), flip, preferred_element_type=F32
    ).astype(BF16)
    taps = load_taps(row_taps_ref, pad_ref)[0 : groups * SUB]
    repeat = (
        lax.broadcasted_iota(jnp.int32, (span, wide), 1) // SUB
        == lax.broadcasted_iota(jnp.int32, (span, wide), 0)
    ).astype(BF16)
    spread = jnp.dot(
        taps[:, 0:span].astype(BF16), repeat, preferred_element_type=F32
    )
    tall = groups * SUB
    lane = lax.broadcasted_iota(jnp.int32, (tall, wide), 1)
    own = lane % SUB == lax.broadcasted_iota(jnp.int32, (tall, wide), 0) % SUB
    spread = jnp.where(own, spread, 0.0)
    place = lane // SUB - side

    def line(row):
        moved = pltpu.roll(spread, (SUB * (row - margin + side)) % wide, 1)
        return jnp.where((place >= row - margin) & (place <= row + margin), moved, 0.0)

    for row in range(0, rows, 2):
        first, second = line(row), line(row + 1)
        for group in range(groups):
            here = slice(SUB * group, SUB * (group + 1))
            both = jnp.concatenate([first[here], second[here]], axis=0)
            band_ref[group, SUB * row : SUB * (row + 2), :] = both.astype(BF16)


def column_stage(tmpl_ref, edge_ref, flipped_ref, cols_ref, height, tap_count):
    width = tmpl_ref.shape[1]
    margin = (tap_count - 1) // 2
    span = ceil_to(tap_count, SUB)
    groups = cols_ref.shape[0]
    _, side = chunk_rows(height)
    taps = flipped_ref[...]
    place = lax.broadcasted_iota(jnp.int32, (span, width), 1) + (
        margin - lax.broadcasted_iota(jnp.int32, (span, width), 0)
    )
    inside = (place >= 0) & (place < width)
    if side:
        nothing = jnp.zeros((groups, SUB * side, width), BF16)
        cols_ref[:, 0 : SUB * side, :] = nothing
        cols_ref[:, SUB * (side + height) :, :] = nothing

    def shifted(row):
        line = jnp.broadcast_to(tmpl_ref[pl.ds(row, 1), :].astype(F32), (span, width))
        line = pltpu.roll(line, width - margin, 1, stride=1, stride_axis=0)
        if edge_ref is None:
            return jnp.where(inside, line, 0.0).astype(BF16)
        other = jnp.broadcast_to(edge_ref[pl.ds(row, 1), :].astype(F32), (span, width))
        other = pltpu.roll(other, width - margin, 1, stride=1, stride_axis=0)
        return jnp.where(inside, line, other).astype(BF16)

    def pair(index):
        both = jnp.concatenate([shifted(2 * index), shifted(2 * index + 1)], axis=1)
        result = jnp.dot(taps, both, preferred_element_type=F32)
        start = SUB * (2 * index + side)
        if not isinstance(start, int):
            start = pl.multiple_of(start, 2 * SUB)
        for group in range(groups):
            here = result[SUB * group : SUB * (group + 1)]
            two = jnp.concatenate([here[:, 0:width], here[:, width:]], axis=0)
            cols_ref[group, pl.ds(start, 2 * SUB), :] = two.astype(BF16)

    each(height // 2, pair)


def row_stage(band_ref, cols_ref, tail_ref, conv_ref):
    height, groups, _, width = conv_ref.shape
    rows, side = chunk_rows(height)

    def chunk(index):
        first = index * rows
        start = SUB * first
        if not isinstance(start, int):
            start = pl.multiple_of(start, SUB * rows)
        for group in range(groups):
            result = jnp.dot(
                band_ref[group],
                cols_ref[group, pl.ds(start, SUB * (rows + 2 * side)), :],
                preferred_element_type=F32,
            )
            for row in range(rows):
                value = result[SUB * row : SUB * (row + 1)].astype(BF16).astype(F32)
                if group == groups - 1:
                    value = value + tail_ref[first + row]
                conv_ref[first + row, group] = value

    each(height // rows, chunk)


def weight_stage(sci_ref, var_ref, rows_ref, cols_ref, weight_ref, inverse_ref, tail_ref, kernels):
    height, width = weight_ref.shape
    stamps = rows_ref.shape[-1]
    sub = lax.broadcasted_iota(jnp.int32, (SUB, width), 0)
    ones = kernels % SUB

    def held(starts_ref, length):
        place = lax.broadcasted_iota(jnp.int32, (length, stamps), 0) - starts_ref[0]
        return jnp.where((place >= 0) & (place < STAMP), 1.0, 0.0).astype(BF16)

    weight_ref[...] = lax.dot_general(
        held(rows_ref, height),
        held(cols_ref, width),
        (((1,), (1,)), ((), ())),
        preferred_element_type=F32,
    )

    def block(index):
        first = index * SUB
        if not isinstance(first, int):
            first = pl.multiple_of(first, SUB)
        here = pl.ds(first, SUB)
        inverse = 1.0 / var_ref[0, here, :]
        inverse_ref[here, :] = inverse
        weight_ref[here, :] = inverse * weight_ref[here, :]
        pieces = [p.astype(F32) for p in split_bf16(sci_ref[0, here, :], 3)]
        for line in range(SUB):
            value = jnp.where(sub == ones, 1.0, 0.0)
            for piece, part in enumerate(pieces):
                spread = jnp.broadcast_to(part[line : line + 1, :], (SUB, width))
                value = jnp.where(sub == ones + 1 + piece, spread, value)
            tail_ref[first + line] = value

    each(height // SUB, block)


def normal_stage(weight_ref, conv_ref, size):
    height, groups, _, width = conv_ref.shape
    tall = groups * SUB
    rows = 2

    def chunk(first):
        left, right = [], []
        for row in range(rows):
            design = conv_ref[first + row].reshape(tall, width)
            if size > tall:
                design = jnp.concatenate([design, jnp.zeros((size - tall, width), F32)], axis=0)
            weight = jnp.broadcast_to(weight_ref[pl.ds(first + row, 1), :], (size, width))
            left.append(jnp.concatenate(split_bf16(design * weight, 2), axis=0))
            right.append(design.astype(BF16))
        return lax.dot_general(
            jnp.concatenate(left, axis=1),
            jnp.concatenate(right, axis=1),
            (((1,), (1,)), ((), ())),
            preferred_element_type=F32,
        )

    if height <= UNROLL:
        product = chunk(0)
        for first in range(rows, height, rows):
            product = product + chunk(first)
    else:
        product = lax.fori_loop(
            0,
            height // rows,
            lambda index, total: total + chunk(index * rows),
            jnp.zeros((2 * size, size), F32),
        )
    return product[0:size] + product[size : 2 * size]


def solve_stage(normal, kernels):
    unknowns = kernels + 1
    width = LANE
    groups = ceil_to(unknowns, SUB) // SUB
    size = normal.shape[1]
    parts = [normal[SUB * g : SUB * (g + 1)] for g in range(groups)]
    if size < width:
        parts = [
            jnp.concatenate([part, jnp.zeros((SUB, width - size), F32)], axis=1)
            for part in parts
        ]

    def pick(value, index, axis):
        where = jnp.full((SUB, width), index, jnp.int32)
        return jnp.take_along_axis(value, where, axis, mode="promise_in_bounds")

    row = lax.broadcasted_iota(jnp.int32, (SUB, width), 0)

    nothing = jnp.zeros((SUB, width), F32)
    straight, across = [nothing] * groups, [nothing] * groups
    edges = [2 * e for e in range(groups // 2)] + [groups]
    for low, high in zip(edges[:-1], edges[1:]):
        members = range(low, high)
        count = ceil_to(min(SUB * high, unknowns) - SUB * low, 2)
        copied = [
            [pick(part, SUB * low + index, 1) for part in parts] for index in range(count)
        ]
        columns = [[one[g] for g in members] for one in copied]
        block = [parts[g] for g in members]
        pivots = []
        for at in range(0, count, 2):
            own, line = at // SUB, at % SUB
            first, second = columns[at], columns[at + 1]
            a, b = pick(first[own], line, 0), pick(second[own], line, 0)
            d = pick(second[own], line + 1, 0)
            inverse = 1.0 / (a * d - b * b)
            a, b, d = a * inverse, b * inverse, d * inverse
            pivots.append((own, line, a, b, d))
            here = (row == line) | (row == line + 1)
            near = [x * d - y * b for x, y in zip(first, second)]
            far = [y * a - x * b for x, y in zip(first, second)]
            near[own] = jnp.where(here, 0.0, near[own])
            far[own] = jnp.where(here, 0.0, far[own])

            def update(value):
                r0, r1 = pick(value[own], line, 0), pick(value[own], line + 1, 0)
                return [v - x * r0 - y * r1 for v, x, y in zip(value, near, far)]

            columns[at + 2 :] = [update(value) for value in columns[at + 2 :]]
            block = update(block)
            group = low + own
            diagonal = jnp.where(row == line + 1, a, straight[group])
            straight[group] = jnp.where(row == line, d, diagonal)
            across[group] = jnp.where(here, b, across[group])
        lines = []
        for own, line, a, b, d in pivots:
            r0, r1 = pick(block[own], line, 0), pick(block[own], line + 1, 0)
            lines += [d * r0 - b * r1, a * r1 - b * r0]
        for group in range(groups):
            if group in members:
                parts[group] = block[group - low]
                continue
            terms = [copied[index][group] * lines[index] for index in range(count)]
            while len(terms) > 1:
                terms = [sum(terms[i : i + 2][1:], terms[i]) for i in range(0, len(terms), 2)]
            parts[group] = parts[group] - terms[0]
    other = jnp.where(row % 2 == 0, row + 1, row - 1)
    parts = [
        x * p - y * jnp.take_along_axis(p, other, 0, mode="promise_in_bounds")
        for x, y, p in zip(straight, across, parts)
    ]
    values = [
        pick(p, unknowns, 1) + (pick(p, unknowns + 1, 1) + pick(p, unknowns + 2, 1))
        for p in parts
    ]
    return [jnp.where(row + SUB * g < unknowns, v, 0.0) for g, v in enumerate(values)]


def residual_stage(values, conv_ref, sci_ref, inverse_ref, diff_ref, out_ref, rows_each):
    height, groups, _, width = conv_ref.shape

    def block(index):
        first = index * SUB
        if not isinstance(first, int):
            first = pl.multiple_of(first, SUB)
        lines = []
        for row in range(SUB):
            total = conv_ref[first + row, 0] * values[0]
            for group in range(1, groups):
                total = total + conv_ref[first + row, group] * values[group]
            lines.append(jnp.sum(total, axis=0, keepdims=True))
        model = jnp.concatenate(lines, axis=0)
        here = pl.ds(first, SUB)
        residual = sci_ref[0, here, :] - model
        inverse = inverse_ref[here, :]
        diff_ref[0, here, :] = residual * jnp.sqrt(inverse)
        weighted = residual * inverse
        for start in range(0, SUB, rows_each):
            target = (first + start) // rows_each
            out_ref[target, 0:rows_each, :] = weighted[start : start + rows_each]
            out_ref[target, rows_each : 2 * rows_each, :] = inverse[start : start + rows_each]

    each(height // SUB, block)


def store_coefficients(values, coef_ref, unknowns):
    row = lax.broadcasted_iota(jnp.int32, (SUB, LANE), 0)
    column = lax.broadcasted_iota(jnp.int32, (SUB, LANE), 1)
    total = jnp.zeros((SUB, LANE), F32)
    for group, value in enumerate(values):
        total = total + jnp.where(column == row + SUB * group, value, 0.0)
    coef_ref[...] = jnp.sum(total, axis=0, keepdims=True)[:, 0:unknowns]


def fit(tile, edge, science, variance, col_taps, row_taps, stamp_rows, stamp_cols, rows_each, sky):
    height, width = science.shape[1:]
    tap_count, kernels = col_taps.shape
    unknowns = kernels + 1
    groups = ceil_to(unknowns + 3, SUB) // SUB
    size = ceil_to(unknowns + 3, 2 * SUB)
    tall = ceil_to(kernels, 2 * SUB)
    rows, side = chunk_rows(height)
    local = sky == 1
    vmem = pl.BlockSpec(memory_space=pltpu.VMEM)
    params = pltpu.CompilerParams(vmem_limit_bytes=56 * 1024 * 1024)
    taps = (col_taps, row_taps)

    def result(shape, dtype=F32):
        return pltpu.VMEM(shape, dtype) if local else jax.ShapeDtypeStruct(shape, dtype)

    prepared = [
        ((tall, ceil_to(tap_count, SUB)), BF16),
        ((groups, SUB * rows, SUB * (rows + 2 * side)), BF16),
        ((height, width), F32),
        ((height, width), F32),
        ((height, SUB, width), F32),
    ]
    pad_shape = pltpu.VMEM((LANE, LANE), F32)
    conv_shape = (height, groups, SUB, width)
    cols_shape = pltpu.VMEM((groups, SUB * (height + 2 * side), width), BF16)
    out_shapes = [
        result((1, height, width)),
        result((1, unknowns)),
        result((height // rows_each, 2 * rows_each, width)),
    ]

    def before(sci, var, ct, rt, sr, sc, flipped, band, weight, inverse, tail, pad):
        taps_stage(ct, rt, pad, flipped, band, height)
        weight_stage(sci, var, sr, sc, weight, inverse, tail, kernels)

    def front(tmpl, edges, flipped, band, weight, tail, conv, cols):
        column_stage(tmpl, edges, flipped, cols, height, tap_count)
        row_stage(band, cols, tail, conv)
        return normal_stage(weight, conv, size)

    def back(normal, conv, sci, inverse, diff, coef, out):
        values = solve_stage(normal, kernels)
        store_coefficients(values, coef, unknowns)
        residual_stage(values, conv, sci, inverse, diff, out, rows_each)

    if local:

        def kernel(tmpl, sci, var, ct, rt, sr, sc, diff, coef, out, conv, cols, pad, *tables):
            before(sci, var, ct, rt, sr, sc, *tables, pad)
            flipped, band, weight, inverse, tail = tables
            normal = front(tmpl, None, flipped, band, weight, tail, conv, cols)
            back(normal, conv, sci, inverse, diff, coef, out)

        args = (tile, science, variance) + taps + (stamp_rows, stamp_cols)
        return pl.pallas_call(
            kernel,
            out_shape=out_shapes,
            in_specs=[vmem] * 7,
            out_specs=[vmem] * 3,
            scratch_shapes=[pltpu.VMEM(conv_shape, F32), cols_shape, pad_shape]
            + [pltpu.VMEM(shape, dtype) for shape, dtype in prepared],
            compiler_params=params,
            name="fit",
        )(*[pltpu.with_memory_space_constraint(arg, pltpu.VMEM) for arg in args])

    flipped, band, weight, inverse, tail = pl.pallas_call(
        before,
        out_shape=[result(shape, dtype) for shape, dtype in prepared],
        in_specs=[vmem] * 6,
        out_specs=[vmem] * 5,
        scratch_shapes=[pad_shape],
        compiler_params=params,
        name="before",
    )(science, variance, *taps, stamp_rows, stamp_cols)

    def first(tmpl, edges, flipped, band, weight, tail, conv, normal, cols):
        normal[...] = front(tmpl, edges, flipped, band, weight, tail, conv, cols)

    conv, normal = pl.pallas_call(
        first,
        out_shape=[result(conv_shape), result((size, size))],
        in_specs=[vmem] * 6,
        out_specs=[vmem] * 2,
        scratch_shapes=[cols_shape],
        compiler_params=params,
        name="fit_normal",
    )(tile.astype(F32), edge.astype(F32), flipped, band, weight, tail)
    normal = lax.psum(normal, "sky")

    def second(normal, conv, sci, inverse, diff, coef, out):
        back(normal[...], conv, sci, inverse, diff, coef, out)

    return pl.pallas_call(
        second,
        out_shape=out_shapes,
        in_specs=[vmem] * 4,
        out_specs=[vmem] * 3,
        compiler_params=params,
        name="fit_solve",
    )(normal, conv, science, inverse)


def sky_edges(tile, margin, sky):
    ends = sky - 1
    width = tile.shape[1]
    head = tile[:, 0:margin]
    tail = tile[:, width - margin :]
    after = lax.ppermute(head, "sky", [(i + 1, i) for i in range(ends)])
    before = lax.ppermute(tail, "sky", [(i, i + 1) for i in range(ends)])
    middle = jnp.zeros((tile.shape[0], width - 2 * margin), tile.dtype)
    return jnp.concatenate([after, middle, before], axis=1)


def stage_inputs(lines, count, others):
    def kernel(*refs):
        taken, given = refs[: len(refs) // 2], refs[len(refs) // 2 :]
        given[0][...] = jnp.broadcast_to(taken[0][...][None], given[0].shape)
        for source, target in zip(taken[1:], given[1:]):
            target[...] = source[...]

    vmem = pl.BlockSpec(memory_space=pltpu.VMEM)
    return pl.pallas_call(
        kernel,
        out_shape=[pltpu.VMEM((count,) + lines.shape, lines.dtype)]
        + [pltpu.VMEM(other.shape, other.dtype) for other in others],
        in_specs=[vmem] * (1 + len(others)),
        out_specs=[vmem] * (1 + len(others)),
        name="stage_inputs",
    )(lines, *others)


def gather_results(shares, difference, coefficients):
    rows_each = shares.shape[1] // 2

    def kernel(shares_ref, diff_ref, coef_ref, diff_out, coef_out, out_ref):
        diff_out[...] = diff_ref[...]
        coef_out[...] = coef_ref[...]
        total = jnp.sum(shares_ref[...], axis=0)
        out_ref[...] = total[0:rows_each] / jnp.sqrt(total[rows_each:])

    vmem = pl.BlockSpec(memory_space=pltpu.VMEM)
    args = (shares, difference, coefficients)
    return pl.pallas_call(
        kernel,
        out_shape=[
            jax.ShapeDtypeStruct(difference.shape, F32),
            jax.ShapeDtypeStruct(coefficients.shape, F32),
            jax.ShapeDtypeStruct((rows_each, shares.shape[2]), F32),
        ],
        in_specs=[vmem] * 3,
        out_specs=[vmem] * 3,
        name="results",
    )(*[pltpu.with_memory_space_constraint(arg, pltpu.VMEM) for arg in args])


def solution(mesh):
    visits = mesh.shape["visit"]
    sky = mesh.shape["sky"]

    def on_device(template, science, variance, col_taps, row_taps, stamp_rows, stamp_cols):
        rows_each, width = template.shape
        margin = (col_taps.shape[1] - 1) // 2
        others = (science, variance, col_taps.T, row_taps.T, stamp_rows, stamp_cols)
        if sky == 1:
            copies, *others = stage_inputs(template, visits, others)
        else:
            copies = jnp.broadcast_to(template[None], (visits, rows_each, width))
        tile = lax.all_to_all(copies, "visit", 0, 0, tiled=True).reshape(-1, width)
        edge = sky_edges(tile, margin, sky) if sky > 1 else None
        difference, coefficients, shares = fit(tile, edge, *others, rows_each, sky)
        shares = lax.all_to_all(shares, "visit", 0, 0, tiled=True)
        if sky == 1:
            return gather_results(shares, difference, coefficients)
        total = jnp.sum(shares, axis=0)
        detection = total[0:rows_each] / jnp.sqrt(total[rows_each:])
        return difference, coefficients, detection

    in_specs = (
        P(("group", "visit"), "sky"),
        P(("group", "visit"), None, "sky"),
        P(("group", "visit"), None, "sky"),
        P(),
        P(),
        P(("group", "visit"), "sky", None),
        P(("group", "visit"), "sky", None),
    )
    out_specs = (
        P(("group", "visit"), None, "sky"),
        P(("group", "visit"), None),
        P(("group", "visit"), "sky"),
    )
    return jax.shard_map(
        on_device, mesh=mesh, in_specs=in_specs, out_specs=out_specs, check_vma=False
    )
```

```python
import jax
import jax.numpy as jnp
from jax import lax
from jax.experimental import pallas as pl
from jax.experimental.pallas import tpu as pltpu
from jax.sharding import PartitionSpec as P

STAMP = 16
SUB = 8
LANE = 128
UNROLL = 32
CHUNK = 32
F32 = jnp.float32
BF16 = jnp.bfloat16


def ceil_to(value, step):
    return (value + step - 1) // step * step


def each(count, body):
    if count <= UNROLL:
        for index in range(count):
            body(index)
    else:
        lax.fori_loop(0, count, lambda index, carry: (body(index), carry)[1], 0)


def lanes_of(index, width):
    if isinstance(index, int):
        return slice(index * width, (index + 1) * width)
    return pl.ds(pl.multiple_of(index * width, width), width)


def split_bf16(value, pieces):
    out = []
    for piece in range(pieces):
        part = value.astype(BF16)
        out.append(part)
        if piece + 1 < pieces:
            value = value - part.astype(F32)
    return out


def load_taps(taps_ref, pad_ref):
    taps, kernels = taps_ref.shape
    pad_ref[...] = jnp.zeros(pad_ref.shape, F32)
    pad_ref[0:taps, 0:kernels] = taps_ref[...].astype(F32)
    return pad_ref[...].T


def chunk_rows(height):
    rows = min(CHUNK, height)
    return rows, (0 if rows == height else CHUNK // 2)


def halves(shape):
    return lax.broadcasted_iota(jnp.int32, shape, 0) % SUB < SUB // 2


def turned(value):
    tiles = [value[at : at + SUB] for at in range(0, value.shape[0], SUB)]
    return jnp.concatenate([pltpu.roll(tile, SUB // 2, 0) for tile in tiles], axis=0)


def taps_stage(col_taps_ref, row_taps_ref, pad_ref, flipped_ref, band_ref, height):
    tap_count = col_taps_ref.shape[0]
    margin = (tap_count - 1) // 2
    span = ceil_to(tap_count, SUB)
    groups = band_ref.shape[0]
    rows, side = chunk_rows(height)
    reach = rows + 2 * side
    wide = SUB // 2 * reach
    tall = groups * SUB
    taps = load_taps(col_taps_ref, pad_ref)[0 : flipped_ref.shape[1], 0:span]
    flip = (
        lax.broadcasted_iota(jnp.int32, (span, span), 0)
        + lax.broadcasted_iota(jnp.int32, (span, span), 1)
        == tap_count - 1
    ).astype(BF16)
    reversed_taps = jnp.dot(taps.astype(BF16), flip, preferred_element_type=F32)
    flipped_ref[0] = reversed_taps.astype(BF16)
    flipped_ref[1] = turned(reversed_taps).astype(BF16)
    taps = load_taps(row_taps_ref, pad_ref)[0:tall, 0:span]
    other = turned(taps)
    lower = halves((tall, span))
    tap = lax.broadcasted_iota(jnp.int32, (span, wide), 0)
    lane = lax.broadcasted_iota(jnp.int32, (span, wide), 1)
    line = lax.broadcasted_iota(jnp.int32, (tall, wide), 0)
    along = lax.broadcasted_iota(jnp.int32, (tall, wide), 1)
    for half in range(2):
        four = jnp.where(lower, taps, other) if half == 0 else jnp.where(lower, other, taps)

        def second(index):
            late = index % SUB >= SUB // 2
            return jnp.where(late, 1 - half, half)

        def base(shift):
            source = 2 * (lane // SUB) + second(lane) - shift - side + margin
            repeat = ((source + reach) % reach == tap).astype(BF16)
            return jnp.dot(four.astype(BF16), repeat, preferred_element_type=F32)

        spread = jnp.where(second(line) == 1, base(1), base(0))
        spread = jnp.where(line % (SUB // 2) == along % (SUB // 2), spread, 0.0)
        place = 2 * (along // SUB) + second(along) - second(line) - side

        def pair(index):
            moved = pltpu.roll(spread, SUB * index, 1) if index else spread
            offset = place - 2 * index
            return jnp.where((offset >= -margin) & (offset <= margin), moved, 0.0)

        for index in range(0, rows // 2, 2):
            first, next_one = pair(index), pair(index + 1)
            for group in range(groups):
                here = slice(SUB * group, SUB * (group + 1))
                both = jnp.concatenate([first[here], next_one[here]], axis=0)
                band_ref[group, half, SUB * index : SUB * (index + 2), :] = both.astype(BF16)


def column_stage(tmpl_ref, edge_ref, flipped_ref, cols_ref, height, tap_count):
    width = tmpl_ref.shape[1]
    margin = (tap_count - 1) // 2
    span = ceil_to(tap_count, SUB)
    groups = cols_ref.shape[0]
    _, side = chunk_rows(height)
    place = lax.broadcasted_iota(jnp.int32, (span, width), 1) + (
        margin - lax.broadcasted_iota(jnp.int32, (span, width), 0)
    )
    inside = (place >= 0) & (place < width)
    lower = halves((SUB, width))
    if side:
        nothing = jnp.zeros((groups, 2, SUB // 2 * side, width), BF16)
        cols_ref[:, :, 0 : SUB // 2 * side, :] = nothing
        cols_ref[:, :, SUB // 2 * (side + height) :, :] = nothing

    def shifted(row):
        line = jnp.broadcast_to(tmpl_ref[pl.ds(row, 1), :].astype(F32), (span, width))
        line = pltpu.roll(line, width - margin, 1, stride=1, stride_axis=0)
        if edge_ref is None:
            return jnp.where(inside, line, 0.0).astype(BF16)
        other = jnp.broadcast_to(edge_ref[pl.ds(row, 1), :].astype(F32), (span, width))
        other = pltpu.roll(other, width - margin, 1, stride=1, stride_axis=0)
        return jnp.where(inside, line, other).astype(BF16)

    def quad(index):
        results = []
        for odd in range(2):
            row = 4 * index + odd
            both = jnp.concatenate([shifted(row), shifted(row + 2)], axis=1)
            results.append(jnp.dot(flipped_ref[odd], both, preferred_element_type=F32))
        start = 2 * SUB * index + SUB // 2 * side
        if not isinstance(start, int):
            start = pl.multiple_of(start, 2 * SUB)
        for group in range(groups):
            even, odd = [value[SUB * group : SUB * (group + 1)] for value in results]
            even, odd = [[v[:, 0:width], v[:, width:]] for v in (even, odd)]
            for half in range(2):
                tiles = [
                    jnp.where(lower, e, o) if half == 0 else jnp.where(lower, o, e)
                    for e, o in zip(even, odd)
                ]
                two = jnp.concatenate(tiles, axis=0)
                cols_ref[group, half, pl.ds(start, 2 * SUB), :] = two.astype(BF16)

    each(height // 4, quad)


def row_stage(band_ref, cols_ref, tail_ref, conv_ref):
    height, groups, _, width = conv_ref.shape
    rows, side = chunk_rows(height)
    lower = halves((SUB, width))

    def chunk(index):
        first = index * rows
        start = SUB // 2 * first
        if not isinstance(start, int):
            start = pl.multiple_of(start, SUB // 2 * rows)
        for group in range(groups):
            near, far = [
                jnp.dot(
                    band_ref[group, half],
                    cols_ref[group, half, pl.ds(start, SUB // 2 * (rows + 2 * side)), :],
                    preferred_element_type=F32,
                )
                for half in range(2)
            ]
            for pair in range(rows // 2):
                here = slice(SUB * pair, SUB * (pair + 1))
                even = jnp.where(lower, near[here], far[here])
                odd = pltpu.roll(jnp.where(lower, far[here], near[here]), SUB // 2, 0)
                for row, value in ((2 * pair, even), (2 * pair + 1, odd)):
                    value = value.astype(BF16).astype(F32)
                    if group == groups - 1:
                        value = value + tail_ref[first + row]
                    conv_ref[first + row, group] = value

    each(height // rows, chunk)


def weight_stage(sci_ref, var_ref, rows_ref, cols_ref, weight_ref, inverse_ref, tail_ref, kernels):
    height, width = weight_ref.shape
    stamps = rows_ref.shape[-1]
    sub = lax.broadcasted_iota(jnp.int32, (SUB, width), 0)
    ones = kernels % SUB

    def held(starts_ref, length):
        place = lax.broadcasted_iota(jnp.int32, (length, stamps), 0) - starts_ref[0]
        return jnp.where((place >= 0) & (place < STAMP), 1.0, 0.0).astype(BF16)

    weight_ref[...] = lax.dot_general(
        held(rows_ref, height),
        held(cols_ref, width),
        (((1,), (1,)), ((), ())),
        preferred_element_type=F32,
    )

    def block(index):
        first = index * SUB
        if not isinstance(first, int):
            first = pl.multiple_of(first, SUB)
        here = pl.ds(first, SUB)
        inverse = 1.0 / var_ref[0, here, :]
        inverse_ref[here, :] = inverse
        weight_ref[here, :] = inverse * weight_ref[here, :]
        pieces = [p.astype(F32) for p in split_bf16(sci_ref[0, here, :], 3)]
        for line in range(SUB):
            value = jnp.where(sub == ones, 1.0, 0.0)
            for piece, part in enumerate(pieces):
                spread = jnp.broadcast_to(part[line : line + 1, :], (SUB, width))
                value = jnp.where(sub == ones + 1 + piece, spread, value)
            tail_ref[first + line] = value

    each(height // SUB, block)


def normal_stage(weight_ref, conv_ref, size):
    height, groups, _, width = conv_ref.shape
    tall = groups * SUB
    rows = 2

    def chunk(first):
        left, right = [], []
        for row in range(rows):
            design = conv_ref[first + row].reshape(tall, width)
            if size > tall:
                design = jnp.concatenate([design, jnp.zeros((size - tall, width), F32)], axis=0)
            weight = jnp.broadcast_to(weight_ref[pl.ds(first + row, 1), :], (size, width))
            left.append(jnp.concatenate(split_bf16(design * weight, 2), axis=0))
            right.append(design.astype(BF16))
        return lax.dot_general(
            jnp.concatenate(left, axis=1),
            jnp.concatenate(right, axis=1),
            (((1,), (1,)), ((), ())),
            preferred_element_type=F32,
        )

    if height <= UNROLL:
        product = chunk(0)
        for first in range(rows, height, rows):
            product = product + chunk(first)
    else:
        product = lax.fori_loop(
            0,
            height // rows,
            lambda index, total: total + chunk(index * rows),
            jnp.zeros((2 * size, size), F32),
        )
    return product[0:size] + product[size : 2 * size]


def solve_stage(normal, kernels):
    unknowns = kernels + 1
    width = LANE
    groups = ceil_to(unknowns, SUB) // SUB
    size = normal.shape[1]
    parts = [normal[SUB * g : SUB * (g + 1)] for g in range(groups)]
    if size < width:
        parts = [
            jnp.concatenate([part, jnp.zeros((SUB, width - size), F32)], axis=1)
            for part in parts
        ]

    def pick(value, index, axis):
        where = jnp.full((SUB, width), index, jnp.int32)
        return jnp.take_along_axis(value, where, axis, mode="promise_in_bounds")

    row = lax.broadcasted_iota(jnp.int32, (SUB, width), 0)

    nothing = jnp.zeros((SUB, width), F32)
    straight, across = [nothing] * groups, [nothing] * groups
    edges = [2 * e for e in range(groups // 2)] + [groups]
    for low, high in zip(edges[:-1], edges[1:]):
        members = range(low, high)
        count = ceil_to(min(SUB * high, unknowns) - SUB * low, 2)
        copied = [
            [pick(part, SUB * low + index, 1) for part in parts] for index in range(count)
        ]
        columns = [[one[g] for g in members] for one in copied]
        block = [parts[g] for g in members]
        pivots = []
        for at in range(0, count, 2):
            own, line = at // SUB, at % SUB
            first, second = columns[at], columns[at + 1]
            a, b = pick(first[own], line, 0), pick(second[own], line, 0)
            d = pick(second[own], line + 1, 0)
            inverse = 1.0 / (a * d - b * b)
            a, b, d = a * inverse, b * inverse, d * inverse
            pivots.append((own, line, a, b, d))
            here = (row == line) | (row == line + 1)
            near = [x * d - y * b for x, y in zip(first, second)]
            far = [y * a - x * b for x, y in zip(first, second)]
            near[own] = jnp.where(here, 0.0, near[own])
            far[own] = jnp.where(here, 0.0, far[own])

            def update(value):
                r0, r1 = pick(value[own], line, 0), pick(value[own], line + 1, 0)
                return [v - x * r0 - y * r1 for v, x, y in zip(value, near, far)]

            columns[at + 2 :] = [update(value) for value in columns[at + 2 :]]
            block = update(block)
            group = low + own
            diagonal = jnp.where(row == line + 1, a, straight[group])
            straight[group] = jnp.where(row == line, d, diagonal)
            across[group] = jnp.where(here, b, across[group])
        lines = []
        for own, line, a, b, d in pivots:
            r0, r1 = pick(block[own], line, 0), pick(block[own], line + 1, 0)
            lines += [d * r0 - b * r1, a * r1 - b * r0]
        for group in range(groups):
            if group in members:
                parts[group] = block[group - low]
                continue
            terms = [copied[index][group] * lines[index] for index in range(count)]
            while len(terms) > 1:
                terms = [sum(terms[i : i + 2][1:], terms[i]) for i in range(0, len(terms), 2)]
            parts[group] = parts[group] - terms[0]
    other = jnp.where(row % 2 == 0, row + 1, row - 1)
    parts = [
        x * p - y * jnp.take_along_axis(p, other, 0, mode="promise_in_bounds")
        for x, y, p in zip(straight, across, parts)
    ]
    values = [
        pick(p, unknowns, 1) + (pick(p, unknowns + 1, 1) + pick(p, unknowns + 2, 1))
        for p in parts
    ]
    return [jnp.where(row + SUB * g < unknowns, v, 0.0) for g, v in enumerate(values)]


def residual_stage(values, conv_ref, sci_ref, inverse_ref, diff_ref, out_ref, rows_each):
    height, groups, _, width = conv_ref.shape

    def block(index):
        first = index * SUB
        if not isinstance(first, int):
            first = pl.multiple_of(first, SUB)
        lines = []
        for row in range(SUB):
            total = conv_ref[first + row, 0] * values[0]
            for group in range(1, groups):
                total = total + conv_ref[first + row, group] * values[group]
            lines.append(jnp.sum(total, axis=0, keepdims=True))
        model = jnp.concatenate(lines, axis=0)
        here = pl.ds(first, SUB)
        residual = sci_ref[0, here, :] - model
        inverse = inverse_ref[here, :]
        diff_ref[0, here, :] = residual * jnp.sqrt(inverse)
        weighted = residual * inverse
        for start in range(0, SUB, rows_each):
            target = (first + start) // rows_each
            out_ref[target, 0:rows_each, :] = weighted[start : start + rows_each]
            out_ref[target, rows_each : 2 * rows_each, :] = inverse[start : start + rows_each]

    each(height // SUB, block)


def store_coefficients(values, coef_ref, unknowns):
    row = lax.broadcasted_iota(jnp.int32, (SUB, LANE), 0)
    column = lax.broadcasted_iota(jnp.int32, (SUB, LANE), 1)
    total = jnp.zeros((SUB, LANE), F32)
    for group, value in enumerate(values):
        total = total + jnp.where(column == row + SUB * group, value, 0.0)
    coef_ref[...] = jnp.sum(total, axis=0, keepdims=True)[:, 0:unknowns]


def fit(tile, edge, science, variance, col_taps, row_taps, stamp_rows, stamp_cols, rows_each, sky):
    height, width = science.shape[1:]
    tap_count, kernels = col_taps.shape
    unknowns = kernels + 1
    groups = ceil_to(unknowns + 3, SUB) // SUB
    size = ceil_to(unknowns + 3, 2 * SUB)
    tall = ceil_to(kernels, 2 * SUB)
    rows, side = chunk_rows(height)
    local = sky == 1
    vmem = pl.BlockSpec(memory_space=pltpu.VMEM)
    params = pltpu.CompilerParams(vmem_limit_bytes=56 * 1024 * 1024)
    taps = (col_taps, row_taps)

    def result(shape, dtype=F32):
        return pltpu.VMEM(shape, dtype) if local else jax.ShapeDtypeStruct(shape, dtype)

    prepared = [
        ((2, tall, ceil_to(tap_count, SUB)), BF16),
        ((groups, 2, SUB // 2 * rows, SUB // 2 * (rows + 2 * side)), BF16),
        ((height, width), F32),
        ((height, width), F32),
        ((height, SUB, width), F32),
    ]
    pad_shape = pltpu.VMEM((LANE, LANE), F32)
    conv_shape = (height, groups, SUB, width)
    cols_shape = pltpu.VMEM((groups, 2, SUB // 2 * (height + 2 * side), width), BF16)
    out_shapes = [
        result((1, height, width)),
        result((1, unknowns)),
        result((height // rows_each, 2 * rows_each, width)),
    ]

    def before(sci, var, ct, rt, sr, sc, flipped, band, weight, inverse, tail, pad):
        taps_stage(ct, rt, pad, flipped, band, height)
        weight_stage(sci, var, sr, sc, weight, inverse, tail, kernels)

    def front(tmpl, edges, flipped, band, weight, tail, conv, cols):
        column_stage(tmpl, edges, flipped, cols, height, tap_count)
        row_stage(band, cols, tail, conv)
        return normal_stage(weight, conv, size)

    def back(normal, conv, sci, inverse, diff, coef, out):
        values = solve_stage(normal, kernels)
        store_coefficients(values, coef, unknowns)
        residual_stage(values, conv, sci, inverse, diff, out, rows_each)

    if local:

        def kernel(tmpl, sci, var, ct, rt, sr, sc, diff, coef, out, conv, cols, pad, *tables):
            before(sci, var, ct, rt, sr, sc, *tables, pad)
            flipped, band, weight, inverse, tail = tables
            normal = front(tmpl, None, flipped, band, weight, tail, conv, cols)
            back(normal, conv, sci, inverse, diff, coef, out)

        args = (tile, science, variance) + taps + (stamp_rows, stamp_cols)
        return pl.pallas_call(
            kernel,
            out_shape=out_shapes,
            in_specs=[vmem] * 7,
            out_specs=[vmem] * 3,
            scratch_shapes=[pltpu.VMEM(conv_shape, F32), cols_shape, pad_shape]
            + [pltpu.VMEM(shape, dtype) for shape, dtype in prepared],
            compiler_params=params,
            name="fit",
        )(*[pltpu.with_memory_space_constraint(arg, pltpu.VMEM) for arg in args])

    flipped, band, weight, inverse, tail = pl.pallas_call(
        before,
        out_shape=[result(shape, dtype) for shape, dtype in prepared],
        in_specs=[vmem] * 6,
        out_specs=[vmem] * 5,
        scratch_shapes=[pad_shape],
        compiler_params=params,
        name="before",
    )(science, variance, *taps, stamp_rows, stamp_cols)

    def first(tmpl, edges, flipped, band, weight, tail, conv, normal, cols):
        normal[...] = front(tmpl, edges, flipped, band, weight, tail, conv, cols)

    conv, normal = pl.pallas_call(
        first,
        out_shape=[result(conv_shape), result((size, size))],
        in_specs=[vmem] * 6,
        out_specs=[vmem] * 2,
        scratch_shapes=[cols_shape],
        compiler_params=params,
        name="fit_normal",
    )(tile.astype(F32), edge.astype(F32), flipped, band, weight, tail)
    normal = lax.psum(normal, "sky")

    def second(normal, conv, sci, inverse, diff, coef, out):
        back(normal[...], conv, sci, inverse, diff, coef, out)

    return pl.pallas_call(
        second,
        out_shape=out_shapes,
        in_specs=[vmem] * 4,
        out_specs=[vmem] * 3,
        compiler_params=params,
        name="fit_solve",
    )(normal, conv, science, inverse)


def sky_edges(tile, margin, sky):
    ends = sky - 1
    width = tile.shape[1]
    head = tile[:, 0:margin]
    tail = tile[:, width - margin :]
    after = lax.ppermute(head, "sky", [(i + 1, i) for i in range(ends)])
    before = lax.ppermute(tail, "sky", [(i, i + 1) for i in range(ends)])
    middle = jnp.zeros((tile.shape[0], width - 2 * margin), tile.dtype)
    return jnp.concatenate([after, middle, before], axis=1)


def stage_inputs(lines, count, others):
    def kernel(*refs):
        taken, given = refs[: len(refs) // 2], refs[len(refs) // 2 :]
        given[0][...] = jnp.broadcast_to(taken[0][...][None], given[0].shape)
        for source, target in zip(taken[1:], given[1:]):
            target[...] = source[...]

    vmem = pl.BlockSpec(memory_space=pltpu.VMEM)
    return pl.pallas_call(
        kernel,
        out_shape=[pltpu.VMEM((count,) + lines.shape, lines.dtype)]
        + [pltpu.VMEM(other.shape, other.dtype) for other in others],
        in_specs=[vmem] * (1 + len(others)),
        out_specs=[vmem] * (1 + len(others)),
        name="stage_inputs",
    )(lines, *others)


def gather_results(shares, difference, coefficients):
    rows_each = shares.shape[1] // 2

    def kernel(shares_ref, diff_ref, coef_ref, diff_out, coef_out, out_ref):
        diff_out[...] = diff_ref[...]
        coef_out[...] = coef_ref[...]
        total = jnp.sum(shares_ref[...], axis=0)
        out_ref[...] = total[0:rows_each] / jnp.sqrt(total[rows_each:])

    vmem = pl.BlockSpec(memory_space=pltpu.VMEM)
    args = (shares, difference, coefficients)
    return pl.pallas_call(
        kernel,
        out_shape=[
            jax.ShapeDtypeStruct(difference.shape, F32),
            jax.ShapeDtypeStruct(coefficients.shape, F32),
            jax.ShapeDtypeStruct((rows_each, shares.shape[2]), F32),
        ],
        in_specs=[vmem] * 3,
        out_specs=[vmem] * 3,
        name="results",
    )(*[pltpu.with_memory_space_constraint(arg, pltpu.VMEM) for arg in args])


def solution(mesh):
    visits = mesh.shape["visit"]
    sky = mesh.shape["sky"]

    def on_device(template, science, variance, col_taps, row_taps, stamp_rows, stamp_cols):
        rows_each, width = template.shape
        margin = (col_taps.shape[1] - 1) // 2
        others = (science, variance, col_taps.T, row_taps.T, stamp_rows, stamp_cols)
        if sky == 1:
            copies, *others = stage_inputs(template, visits, others)
        else:
            copies = jnp.broadcast_to(template[None], (visits, rows_each, width))
        tile = lax.all_to_all(copies, "visit", 0, 0, tiled=True).reshape(-1, width)
        edge = sky_edges(tile, margin, sky) if sky > 1 else None
        difference, coefficients, shares = fit(tile, edge, *others, rows_each, sky)
        shares = lax.all_to_all(shares, "visit", 0, 0, tiled=True)
        if sky == 1:
            return gather_results(shares, difference, coefficients)
        total = jnp.sum(shares, axis=0)
        detection = total[0:rows_each] / jnp.sqrt(total[rows_each:])
        return difference, coefficients, detection

    in_specs = (
        P(("group", "visit"), "sky"),
        P(("group", "visit"), None, "sky"),
        P(("group", "visit"), None, "sky"),
        P(),
        P(),
        P(("group", "visit"), "sky", None),
        P(("group", "visit"), "sky", None),
    )
    out_specs = (
        P(("group", "visit"), None, "sky"),
        P(("group", "visit"), None),
        P(("group", "visit"), "sky"),
    )
    return jax.shard_map(
        on_device, mesh=mesh, in_specs=in_specs, out_specs=out_specs, check_vma=False
    )
```

```python
import jax
import jax.numpy as jnp
from jax import lax
from jax.experimental import pallas as pl
from jax.experimental.pallas import tpu as pltpu
from jax.sharding import PartitionSpec as P

STAMP = 16
SUB = 8
LANE = 128
UNROLL = 32
CHUNK = 32
F32 = jnp.float32
BF16 = jnp.bfloat16


def ceil_to(value, step):
    return (value + step - 1) // step * step


def each(count, body):
    if count <= UNROLL:
        for index in range(count):
            body(index)
    else:
        lax.fori_loop(0, count, lambda index, carry: (body(index), carry)[1], 0)


def lanes_of(index, width):
    if isinstance(index, int):
        return slice(index * width, (index + 1) * width)
    return pl.ds(pl.multiple_of(index * width, width), width)


def split_bf16(value, pieces):
    out = []
    for piece in range(pieces):
        part = value.astype(BF16)
        out.append(part)
        if piece + 1 < pieces:
            value = value - part.astype(F32)
    return out


def load_taps(taps_ref, pad_ref):
    taps, kernels = taps_ref.shape
    pad_ref[...] = jnp.zeros(pad_ref.shape, F32)
    pad_ref[0:taps, 0:kernels] = taps_ref[...].astype(F32)
    return pad_ref[...].T


def chunk_rows(height):
    rows = min(CHUNK, height)
    return rows, (0 if rows == height else CHUNK // 2)


def halves(shape):
    return (lax.broadcasted_iota(jnp.int32, shape, 0) & (SUB - 1)) < SUB // 2


def turned(value):
    tiles = [value[at : at + SUB] for at in range(0, value.shape[0], SUB)]
    return jnp.concatenate([pltpu.roll(tile, SUB // 2, 0) for tile in tiles], axis=0)


def taps_stage(col_taps_ref, row_taps_ref, pad_ref, flipped_ref, band_ref, height):
    tap_count = col_taps_ref.shape[0]
    margin = (tap_count - 1) // 2
    span = ceil_to(tap_count, SUB)
    groups = band_ref.shape[0]
    rows, side = chunk_rows(height)
    reach = rows + 2 * side
    wide = SUB // 2 * reach
    tall = groups * SUB
    taps = load_taps(col_taps_ref, pad_ref)[0 : flipped_ref.shape[1], 0:span]
    flip = (
        lax.broadcasted_iota(jnp.int32, (span, span), 0)
        + lax.broadcasted_iota(jnp.int32, (span, span), 1)
        == tap_count - 1
    ).astype(BF16)
    reversed_taps = jnp.dot(taps.astype(BF16), flip, preferred_element_type=F32)
    flipped_ref[0] = reversed_taps.astype(BF16)
    flipped_ref[1] = turned(reversed_taps).astype(BF16)
    taps = load_taps(row_taps_ref, pad_ref)[0:tall, 0:span]
    other = turned(taps)
    lower = halves((tall, span))
    tap = lax.broadcasted_iota(jnp.int32, (span, wide), 0)
    lane = lax.broadcasted_iota(jnp.int32, (span, wide), 1)
    sub = lax.broadcasted_iota(jnp.int32, (SUB, wide), 0)
    along = lax.broadcasted_iota(jnp.int32, (SUB, wide), 1)
    own = (sub & (SUB // 2 - 1)) == (along & (SUB // 2 - 1))
    bit = (SUB // 2).bit_length() - 1
    for half in range(2):
        four = jnp.where(lower, taps, other) if half == 0 else jnp.where(lower, other, taps)

        def line_of(index):
            return 2 * (index >> (bit + 1)) + (((index >> bit) & 1) ^ half)

        def base(shift):
            source = line_of(lane) - shift - side + margin
            source = jnp.where(source >= reach, source - reach, source)
            source = jnp.where(source < 0, source + reach, source)
            repeat = jnp.where(source == tap, 1.0, 0.0).astype(BF16)
            return jnp.dot(four.astype(BF16), repeat, preferred_element_type=F32)

        first, second = base(0), base(1)
        place = line_of(along) - line_of(sub) - side
        late = line_of(sub) == 1
        spread = []
        for group in range(groups):
            here = slice(SUB * group, SUB * (group + 1))
            spread.append(jnp.where(own, jnp.where(late, second[here], first[here]), 0.0))

        for index in range(0, rows // 2, 2):
            inside = [
                (place >= 2 * pair - margin) & (place <= 2 * pair + margin)
                for pair in (index, index + 1)
            ]
            for group in range(groups):
                both = [
                    jnp.where(inside[pair], pltpu.roll(spread[group], SUB * (index + pair), 1), 0.0)
                    for pair in range(2)
                ]
                both = jnp.concatenate(both, axis=0).astype(BF16)
                band_ref[group, half, SUB * index : SUB * (index + 2), :] = both


def column_stage(tmpl_ref, edge_ref, flipped_ref, cols_ref, height, tap_count):
    width = tmpl_ref.shape[1]
    margin = (tap_count - 1) // 2
    span = ceil_to(tap_count, SUB)
    groups = cols_ref.shape[0]
    _, side = chunk_rows(height)
    place = lax.broadcasted_iota(jnp.int32, (span, width), 1) + (
        margin - lax.broadcasted_iota(jnp.int32, (span, width), 0)
    )
    inside = (place >= 0) & (place < width)
    lower = halves((SUB, width))
    if side:
        nothing = jnp.zeros((groups, 2, SUB // 2 * side, width), BF16)
        cols_ref[:, :, 0 : SUB // 2 * side, :] = nothing
        cols_ref[:, :, SUB // 2 * (side + height) :, :] = nothing

    def shifted(row):
        line = jnp.broadcast_to(tmpl_ref[pl.ds(row, 1), :].astype(F32), (span, width))
        line = pltpu.roll(line, width - margin, 1, stride=1, stride_axis=0)
        if edge_ref is None:
            return jnp.where(inside, line, 0.0).astype(BF16)
        other = jnp.broadcast_to(edge_ref[pl.ds(row, 1), :].astype(F32), (span, width))
        other = pltpu.roll(other, width - margin, 1, stride=1, stride_axis=0)
        return jnp.where(inside, line, other).astype(BF16)

    def quad(index):
        results = []
        for odd in range(2):
            row = 4 * index + odd
            both = jnp.concatenate([shifted(row), shifted(row + 2)], axis=1)
            results.append(jnp.dot(flipped_ref[odd], both, preferred_element_type=F32))
        start = 2 * SUB * index + SUB // 2 * side
        if not isinstance(start, int):
            start = pl.multiple_of(start, 2 * SUB)
        for group in range(groups):
            even, odd = [value[SUB * group : SUB * (group + 1)] for value in results]
            even, odd = [[v[:, 0:width], v[:, width:]] for v in (even, odd)]
            for half in range(2):
                tiles = [
                    jnp.where(lower, e, o) if half == 0 else jnp.where(lower, o, e)
                    for e, o in zip(even, odd)
                ]
                two = jnp.concatenate(tiles, axis=0)
                cols_ref[group, half, pl.ds(start, 2 * SUB), :] = two.astype(BF16)

    each(height // 4, quad)


def row_stage(band_ref, cols_ref, tail_ref, conv_ref):
    height, _, width = conv_ref.shape
    groups = band_ref.shape[0]
    rows, side = chunk_rows(height)
    lower = halves((SUB, width))

    def chunk(index):
        first = index * rows
        start = SUB // 2 * first
        if not isinstance(start, int):
            start = pl.multiple_of(start, SUB // 2 * rows)
        for group in range(0, groups, 2):
            members = range(group, min(group + 2, groups))
            pairs = [
                [
                    jnp.dot(
                        band_ref[g, half],
                        cols_ref[g, half, pl.ds(start, SUB // 2 * (rows + 2 * side)), :],
                        preferred_element_type=F32,
                    )
                    for half in range(2)
                ]
                for g in members
            ]
            for pair in range(rows // 2):
                here = slice(SUB * pair, SUB * (pair + 1))
                both = []
                for near, far in pairs:
                    even = jnp.where(lower, near[here], far[here])
                    odd = pltpu.roll(jnp.where(lower, far[here], near[here]), SUB // 2, 0)
                    both.append((even, odd))
                for half in range(2):
                    row = first + 2 * pair + half
                    tiles = [one[half] for one in both]
                    if members[-1] == groups - 1:
                        tiles[-1] = tiles[-1] + tail_ref[row]
                    if len(tiles) == 1:
                        tiles.append(jnp.zeros((SUB, width), F32))
                    conv_ref[row, SUB * group : SUB * (group + 2), :] = jnp.concatenate(
                        tiles, axis=0
                    ).astype(BF16)

    each(height // rows, chunk)


def weight_stage(sci_ref, var_ref, rows_ref, cols_ref, weight_ref, inverse_ref, tail_ref, kernels):
    height, width = weight_ref.shape
    stamps = rows_ref.shape[-1]
    sub = lax.broadcasted_iota(jnp.int32, (SUB, width), 0)
    ones = kernels % SUB

    def held(starts_ref, length):
        place = lax.broadcasted_iota(jnp.int32, (length, stamps), 0) - starts_ref[0]
        return jnp.where((place >= 0) & (place < STAMP), 1.0, 0.0).astype(BF16)

    weight_ref[...] = lax.dot_general(
        held(rows_ref, height),
        held(cols_ref, width),
        (((1,), (1,)), ((), ())),
        preferred_element_type=F32,
    )

    def block(index):
        first = index * SUB
        if not isinstance(first, int):
            first = pl.multiple_of(first, SUB)
        here = pl.ds(first, SUB)
        inverse = 1.0 / var_ref[0, here, :]
        inverse_ref[here, :] = inverse
        weight_ref[here, :] = inverse * weight_ref[here, :]
        pieces = [p.astype(F32) for p in split_bf16(sci_ref[0, here, :], 3)]
        for line in range(SUB):
            value = jnp.where(sub == ones, 1.0, 0.0)
            for piece, part in enumerate(pieces):
                spread = jnp.broadcast_to(part[line : line + 1, :], (SUB, width))
                value = jnp.where(sub == ones + 1 + piece, spread, value)
            tail_ref[first + line] = value

    each(height // SUB, block)


def normal_stage(weight_ref, conv_ref, size):
    height, _, width = conv_ref.shape
    rows = 2

    def chunk(first):
        left, right = [], []
        for row in range(rows):
            design = conv_ref[first + row]
            weight = jnp.broadcast_to(weight_ref[pl.ds(first + row, 1), :], (size, width))
            left.append(jnp.concatenate(split_bf16(design.astype(F32) * weight, 2), axis=0))
            right.append(design)
        return lax.dot_general(
            jnp.concatenate(left, axis=1),
            jnp.concatenate(right, axis=1),
            (((1,), (1,)), ((), ())),
            preferred_element_type=F32,
        )

    if height <= UNROLL:
        product = chunk(0)
        for first in range(rows, height, rows):
            product = product + chunk(first)
    else:
        product = lax.fori_loop(
            0,
            height // rows,
            lambda index, total: total + chunk(index * rows),
            jnp.zeros((2 * size, size), F32),
        )
    return product[0:size] + product[size : 2 * size]


def solve_stage(normal, kernels):
    unknowns = kernels + 1
    width = LANE
    groups = ceil_to(unknowns, SUB) // SUB
    size = normal.shape[1]
    parts = [normal[SUB * g : SUB * (g + 1)] for g in range(groups)]
    if size < width:
        parts = [
            jnp.concatenate([part, jnp.zeros((SUB, width - size), F32)], axis=1)
            for part in parts
        ]

    def pick(value, index, axis):
        where = jnp.full((SUB, width), index, jnp.int32)
        return jnp.take_along_axis(value, where, axis, mode="promise_in_bounds")

    row = lax.broadcasted_iota(jnp.int32, (SUB, width), 0)

    nothing = jnp.zeros((SUB, width), F32)
    straight, across = [nothing] * groups, [nothing] * groups
    edges = [2 * e for e in range(groups // 2)] + [groups]
    for low, high in zip(edges[:-1], edges[1:]):
        members = range(low, high)
        count = ceil_to(min(SUB * high, unknowns) - SUB * low, 2)
        copied = [
            [pick(part, SUB * low + index, 1) for part in parts] for index in range(count)
        ]
        columns = [[one[g] for g in members] for one in copied]
        block = [parts[g] for g in members]
        pivots = []
        for at in range(0, count, 2):
            own, line = at // SUB, at % SUB
            first, second = columns[at], columns[at + 1]
            a, b = pick(first[own], line, 0), pick(second[own], line, 0)
            d = pick(second[own], line + 1, 0)
            inverse = 1.0 / (a * d - b * b)
            a, b, d = a * inverse, b * inverse, d * inverse
            pivots.append((own, line, a, b, d))
            here = (row == line) | (row == line + 1)
            near = [x * d - y * b for x, y in zip(first, second)]
            far = [y * a - x * b for x, y in zip(first, second)]
            near[own] = jnp.where(here, 0.0, near[own])
            far[own] = jnp.where(here, 0.0, far[own])

            def update(value):
                r0, r1 = pick(value[own], line, 0), pick(value[own], line + 1, 0)
                return [v - x * r0 - y * r1 for v, x, y in zip(value, near, far)]

            columns[at + 2 :] = [update(value) for value in columns[at + 2 :]]
            block = update(block)
            group = low + own
            diagonal = jnp.where(row == line + 1, a, straight[group])
            straight[group] = jnp.where(row == line, d, diagonal)
            across[group] = jnp.where(here, b, across[group])
        lines = []
        for own, line, a, b, d in pivots:
            r0, r1 = pick(block[own], line, 0), pick(block[own], line + 1, 0)
            lines += [d * r0 - b * r1, a * r1 - b * r0]
        for group in range(groups):
            if group in members:
                parts[group] = block[group - low]
                continue
            terms = [copied[index][group] * lines[index] for index in range(count)]
            while len(terms) > 1:
                terms = [sum(terms[i : i + 2][1:], terms[i]) for i in range(0, len(terms), 2)]
            parts[group] = parts[group] - terms[0]
    other = row ^ 1
    parts = [
        x * p - y * jnp.take_along_axis(p, other, 0, mode="promise_in_bounds")
        for x, y, p in zip(straight, across, parts)
    ]
    values = [
        pick(p, unknowns, 1) + (pick(p, unknowns + 1, 1) + pick(p, unknowns + 2, 1))
        for p in parts
    ]
    return [jnp.where(row + SUB * g < unknowns, v, 0.0) for g, v in enumerate(values)]


def residual_stage(values, conv_ref, sci_ref, inverse_ref, diff_ref, out_ref, rows_each):
    height, _, width = conv_ref.shape

    def block(index):
        first = index * SUB
        if not isinstance(first, int):
            first = pl.multiple_of(first, SUB)
        lines = []
        for row in range(SUB):
            design = conv_ref[first + row].astype(F32)
            total = design[0:SUB] * values[0]
            for group in range(1, len(values)):
                total = total + design[SUB * group : SUB * (group + 1)] * values[group]
            lines.append(jnp.sum(total, axis=0, keepdims=True))
        model = jnp.concatenate(lines, axis=0)
        here = pl.ds(first, SUB)
        residual = sci_ref[0, here, :] - model
        inverse = inverse_ref[here, :]
        diff_ref[0, here, :] = residual * jnp.sqrt(inverse)
        weighted = residual * inverse
        for start in range(0, SUB, rows_each):
            target = (first + start) // rows_each
            out_ref[target, 0:rows_each, :] = weighted[start : start + rows_each]
            out_ref[target, rows_each : 2 * rows_each, :] = inverse[start : start + rows_each]

    each(height // SUB, block)


def store_coefficients(values, coef_ref, unknowns):
    row = lax.broadcasted_iota(jnp.int32, (SUB, LANE), 0)
    column = lax.broadcasted_iota(jnp.int32, (SUB, LANE), 1)
    total = jnp.zeros((SUB, LANE), F32)
    for group, value in enumerate(values):
        total = total + jnp.where(column == row + SUB * group, value, 0.0)
    coef_ref[...] = jnp.sum(total, axis=0, keepdims=True)[:, 0:unknowns]


def fit(tile, edge, science, variance, col_taps, row_taps, stamp_rows, stamp_cols, rows_each, sky):
    height, width = science.shape[1:]
    tap_count, kernels = col_taps.shape
    unknowns = kernels + 1
    groups = ceil_to(unknowns + 3, SUB) // SUB
    size = ceil_to(unknowns + 3, 2 * SUB)
    tall = ceil_to(kernels, 2 * SUB)
    rows, side = chunk_rows(height)
    local = sky == 1
    vmem = pl.BlockSpec(memory_space=pltpu.VMEM)
    params = pltpu.CompilerParams(vmem_limit_bytes=56 * 1024 * 1024)
    taps = (col_taps, row_taps)

    def result(shape, dtype=F32):
        return pltpu.VMEM(shape, dtype) if local else jax.ShapeDtypeStruct(shape, dtype)

    prepared = [
        ((2, tall, ceil_to(tap_count, SUB)), BF16),
        ((groups, 2, SUB // 2 * rows, SUB // 2 * (rows + 2 * side)), BF16),
        ((height, width), F32),
        ((height, width), F32),
        ((height, SUB, width), F32),
    ]
    pad_shape = pltpu.VMEM((LANE, LANE), F32)
    conv_shape = (height, size, width)
    cols_shape = pltpu.VMEM((groups, 2, SUB // 2 * (height + 2 * side), width), BF16)
    out_shapes = [
        result((1, height, width)),
        result((1, unknowns)),
        result((height // rows_each, 2 * rows_each, width)),
    ]

    def before(sci, var, ct, rt, sr, sc, flipped, band, weight, inverse, tail, pad):
        taps_stage(ct, rt, pad, flipped, band, height)
        weight_stage(sci, var, sr, sc, weight, inverse, tail, kernels)

    def front(tmpl, edges, flipped, band, weight, tail, conv, cols):
        column_stage(tmpl, edges, flipped, cols, height, tap_count)
        row_stage(band, cols, tail, conv)
        return normal_stage(weight, conv, size)

    def back(normal, conv, sci, inverse, diff, coef, out):
        values = solve_stage(normal, kernels)
        store_coefficients(values, coef, unknowns)
        residual_stage(values, conv, sci, inverse, diff, out, rows_each)

    if local:

        def kernel(tmpl, sci, var, ct, rt, sr, sc, diff, coef, out, conv, cols, pad, *tables):
            before(sci, var, ct, rt, sr, sc, *tables, pad)
            flipped, band, weight, inverse, tail = tables
            normal = front(tmpl, None, flipped, band, weight, tail, conv, cols)
            back(normal, conv, sci, inverse, diff, coef, out)

        args = (tile, science, variance) + taps + (stamp_rows, stamp_cols)
        return pl.pallas_call(
            kernel,
            out_shape=out_shapes,
            in_specs=[vmem] * 7,
            out_specs=[vmem] * 3,
            scratch_shapes=[pltpu.VMEM(conv_shape, BF16), cols_shape, pad_shape]
            + [pltpu.VMEM(shape, dtype) for shape, dtype in prepared],
            compiler_params=params,
            name="fit",
        )(*[pltpu.with_memory_space_constraint(arg, pltpu.VMEM) for arg in args])

    flipped, band, weight, inverse, tail = pl.pallas_call(
        before,
        out_shape=[result(shape, dtype) for shape, dtype in prepared],
        in_specs=[vmem] * 6,
        out_specs=[vmem] * 5,
        scratch_shapes=[pad_shape],
        compiler_params=params,
        name="before",
    )(science, variance, *taps, stamp_rows, stamp_cols)

    def first(tmpl, edges, flipped, band, weight, tail, conv, normal, cols):
        normal[...] = front(tmpl, edges, flipped, band, weight, tail, conv, cols)

    conv, normal = pl.pallas_call(
        first,
        out_shape=[result(conv_shape, BF16), result((size, size))],
        in_specs=[vmem] * 6,
        out_specs=[vmem] * 2,
        scratch_shapes=[cols_shape],
        compiler_params=params,
        name="fit_normal",
    )(tile.astype(F32), edge.astype(F32), flipped, band, weight, tail)
    normal = lax.psum(normal, "sky")

    def second(normal, conv, sci, inverse, diff, coef, out):
        back(normal[...], conv, sci, inverse, diff, coef, out)

    return pl.pallas_call(
        second,
        out_shape=out_shapes,
        in_specs=[vmem] * 4,
        out_specs=[vmem] * 3,
        compiler_params=params,
        name="fit_solve",
    )(normal, conv, science, inverse)


def sky_edges(tile, margin, sky):
    ends = sky - 1
    width = tile.shape[1]
    head = tile[:, 0:margin]
    tail = tile[:, width - margin :]
    after = lax.ppermute(head, "sky", [(i + 1, i) for i in range(ends)])
    before = lax.ppermute(tail, "sky", [(i, i + 1) for i in range(ends)])
    middle = jnp.zeros((tile.shape[0], width - 2 * margin), tile.dtype)
    return jnp.concatenate([after, middle, before], axis=1)


def stage_inputs(lines, count, others):
    def kernel(*refs):
        taken, given = refs[: len(refs) // 2], refs[len(refs) // 2 :]
        given[0][...] = jnp.broadcast_to(taken[0][...][None], given[0].shape)
        for source, target in zip(taken[1:], given[1:]):
            target[...] = source[...]

    vmem = pl.BlockSpec(memory_space=pltpu.VMEM)
    return pl.pallas_call(
        kernel,
        out_shape=[pltpu.VMEM((count,) + lines.shape, lines.dtype)]
        + [pltpu.VMEM(other.shape, other.dtype) for other in others],
        in_specs=[vmem] * (1 + len(others)),
        out_specs=[vmem] * (1 + len(others)),
        name="stage_inputs",
    )(lines, *others)


def gather_results(shares, difference, coefficients):
    rows_each = shares.shape[1] // 2

    def kernel(shares_ref, diff_ref, coef_ref, diff_out, coef_out, out_ref):
        diff_out[...] = diff_ref[...]
        coef_out[...] = coef_ref[...]
        total = jnp.sum(shares_ref[...], axis=0)
        out_ref[...] = total[0:rows_each] / jnp.sqrt(total[rows_each:])

    vmem = pl.BlockSpec(memory_space=pltpu.VMEM)
    args = (shares, difference, coefficients)
    return pl.pallas_call(
        kernel,
        out_shape=[
            jax.ShapeDtypeStruct(difference.shape, F32),
            jax.ShapeDtypeStruct(coefficients.shape, F32),
            jax.ShapeDtypeStruct((rows_each, shares.shape[2]), F32),
        ],
        in_specs=[vmem] * 3,
        out_specs=[vmem] * 3,
        name="results",
    )(*[pltpu.with_memory_space_constraint(arg, pltpu.VMEM) for arg in args])


def solution(mesh):
    visits = mesh.shape["visit"]
    sky = mesh.shape["sky"]

    def on_device(template, science, variance, col_taps, row_taps, stamp_rows, stamp_cols):
        rows_each, width = template.shape
        margin = (col_taps.shape[1] - 1) // 2
        others = (science, variance, col_taps.T, row_taps.T, stamp_rows, stamp_cols)
        if sky == 1:
            copies, *others = stage_inputs(template, visits, others)
        else:
            copies = jnp.broadcast_to(template[None], (visits, rows_each, width))
        tile = lax.all_to_all(copies, "visit", 0, 0, tiled=True).reshape(-1, width)
        edge = sky_edges(tile, margin, sky) if sky > 1 else None
        difference, coefficients, shares = fit(tile, edge, *others, rows_each, sky)
        shares = lax.all_to_all(shares, "visit", 0, 0, tiled=True)
        if sky == 1:
            return gather_results(shares, difference, coefficients)
        total = jnp.sum(shares, axis=0)
        detection = total[0:rows_each] / jnp.sqrt(total[rows_each:])
        return difference, coefficients, detection

    in_specs = (
        P(("group", "visit"), "sky"),
        P(("group", "visit"), None, "sky"),
        P(("group", "visit"), None, "sky"),
        P(),
        P(),
        P(("group", "visit"), "sky", None),
        P(("group", "visit"), "sky", None),
    )
    out_specs = (
        P(("group", "visit"), None, "sky"),
        P(("group", "visit"), None),
        P(("group", "visit"), "sky"),
    )
    return jax.shard_map(
        on_device, mesh=mesh, in_specs=in_specs, out_specs=out_specs, check_vma=False
    )
```

```python
import jax
import jax.numpy as jnp
from jax import lax
from jax.experimental import pallas as pl
from jax.experimental.pallas import tpu as pltpu
from jax.sharding import PartitionSpec as P

STAMP = 16
SUB = 8
LANE = 128
UNROLL = 32
CHUNK = 32
F32 = jnp.float32
BF16 = jnp.bfloat16


def ceil_to(value, step):
    return (value + step - 1) // step * step


def each(count, body):
    if count <= UNROLL:
        for index in range(count):
            body(index)
    else:
        lax.fori_loop(0, count, lambda index, carry: (body(index), carry)[1], 0)


def lanes_of(index, width):
    if isinstance(index, int):
        return slice(index * width, (index + 1) * width)
    return pl.ds(pl.multiple_of(index * width, width), width)


def split_bf16(value, pieces):
    out = []
    for piece in range(pieces):
        part = value.astype(BF16)
        out.append(part)
        if piece + 1 < pieces:
            value = value - part.astype(F32)
    return out


def load_taps(taps_ref, pad_ref):
    taps, kernels = taps_ref.shape
    pad_ref[...] = jnp.zeros(pad_ref.shape, F32)
    pad_ref[0:taps, 0:kernels] = taps_ref[...].astype(F32)
    return pad_ref[...].T


def chunk_rows(height):
    rows = min(CHUNK, height)
    return rows, (0 if rows == height else CHUNK // 2)


def halves(shape):
    return (lax.broadcasted_iota(jnp.int32, shape, 0) & (SUB - 1)) < SUB // 2


def turned(value):
    tiles = [value[at : at + SUB] for at in range(0, value.shape[0], SUB)]
    return jnp.concatenate([pltpu.roll(tile, SUB // 2, 0) for tile in tiles], axis=0)


def taps_stage(col_taps_ref, row_taps_ref, pad_ref, flipped_ref, band_ref, height):
    tap_count = col_taps_ref.shape[0]
    margin = (tap_count - 1) // 2
    span = ceil_to(tap_count, SUB)
    groups = band_ref.shape[0]
    rows, side = chunk_rows(height)
    reach = rows + 2 * side
    wide = SUB // 2 * reach
    tall = groups * SUB
    taps = load_taps(col_taps_ref, pad_ref)[0 : flipped_ref.shape[1], 0:span]
    flip = (
        lax.broadcasted_iota(jnp.int32, (span, span), 0)
        + lax.broadcasted_iota(jnp.int32, (span, span), 1)
        == tap_count - 1
    ).astype(BF16)
    reversed_taps = jnp.dot(taps.astype(BF16), flip, preferred_element_type=F32)
    flipped_ref[0] = reversed_taps.astype(BF16)
    flipped_ref[1] = turned(reversed_taps).astype(BF16)
    taps = load_taps(row_taps_ref, pad_ref)[0:tall, 0:span]
    other = turned(taps)
    lower = halves((tall, span))
    tap = lax.broadcasted_iota(jnp.int32, (span, wide), 0)
    lane = lax.broadcasted_iota(jnp.int32, (span, wide), 1)
    sub = lax.broadcasted_iota(jnp.int32, (SUB, wide), 0)
    along = lax.broadcasted_iota(jnp.int32, (SUB, wide), 1)
    own = (sub & (SUB // 2 - 1)) == (along & (SUB // 2 - 1))
    bit = (SUB // 2).bit_length() - 1
    for half in range(2):
        four = jnp.where(lower, taps, other) if half == 0 else jnp.where(lower, other, taps)

        def line_of(index):
            return 2 * (index >> (bit + 1)) + (((index >> bit) & 1) ^ half)

        def base(shift):
            source = line_of(lane) - shift - side + margin
            source = jnp.where(source >= reach, source - reach, source)
            source = jnp.where(source < 0, source + reach, source)
            repeat = jnp.where(source == tap, 1.0, 0.0).astype(BF16)
            return jnp.dot(four.astype(BF16), repeat, preferred_element_type=F32)

        first, second = base(0), base(1)
        place = line_of(along) - line_of(sub) - side
        late = line_of(sub) == 1
        spread = []
        for group in range(groups):
            here = slice(SUB * group, SUB * (group + 1))
            spread.append(jnp.where(own, jnp.where(late, second[here], first[here]), 0.0))

        for index in range(0, rows // 2, 2):
            inside = [
                (place >= 2 * pair - margin) & (place <= 2 * pair + margin)
                for pair in (index, index + 1)
            ]
            for group in range(groups):
                both = [
                    jnp.where(inside[pair], pltpu.roll(spread[group], SUB * (index + pair), 1), 0.0)
                    for pair in range(2)
                ]
                both = jnp.concatenate(both, axis=0).astype(BF16)
                band_ref[group, half, SUB * index : SUB * (index + 2), :] = both


def column_stage(tmpl_ref, edge_ref, flipped_ref, cols_ref, height, tap_count):
    width = tmpl_ref.shape[1]
    margin = (tap_count - 1) // 2
    span = ceil_to(tap_count, SUB)
    groups = cols_ref.shape[0]
    _, side = chunk_rows(height)
    place = lax.broadcasted_iota(jnp.int32, (span, width), 1) + (
        margin - lax.broadcasted_iota(jnp.int32, (span, width), 0)
    )
    inside = (place >= 0) & (place < width)
    lower = halves((SUB, width))
    if side:
        nothing = jnp.zeros((groups, 2, SUB // 2 * side, width), BF16)
        cols_ref[:, :, 0 : SUB // 2 * side, :] = nothing
        cols_ref[:, :, SUB // 2 * (side + height) :, :] = nothing

    def shifted(row):
        line = jnp.broadcast_to(tmpl_ref[pl.ds(row, 1), :].astype(F32), (span, width))
        line = pltpu.roll(line, width - margin, 1, stride=1, stride_axis=0)
        if edge_ref is None:
            return jnp.where(inside, line, 0.0).astype(BF16)
        other = jnp.broadcast_to(edge_ref[pl.ds(row, 1), :].astype(F32), (span, width))
        other = pltpu.roll(other, width - margin, 1, stride=1, stride_axis=0)
        return jnp.where(inside, line, other).astype(BF16)

    def quad(index):
        results = []
        for odd in range(2):
            row = 4 * index + odd
            both = jnp.concatenate([shifted(row), shifted(row + 2)], axis=1)
            results.append(jnp.dot(flipped_ref[odd], both, preferred_element_type=F32))
        start = 2 * SUB * index + SUB // 2 * side
        if not isinstance(start, int):
            start = pl.multiple_of(start, 2 * SUB)
        for group in range(groups):
            even, odd = [value[SUB * group : SUB * (group + 1)] for value in results]
            even, odd = [[v[:, 0:width], v[:, width:]] for v in (even, odd)]
            for half in range(2):
                tiles = [
                    jnp.where(lower, e, o) if half == 0 else jnp.where(lower, o, e)
                    for e, o in zip(even, odd)
                ]
                two = jnp.concatenate(tiles, axis=0)
                cols_ref[group, half, pl.ds(start, 2 * SUB), :] = two.astype(BF16)

    each(height // 4, quad)


def row_stage(band_ref, cols_ref, tail_ref, conv_ref):
    height, _, width = conv_ref.shape
    groups = band_ref.shape[0]
    rows, side = chunk_rows(height)
    lower = halves((SUB, width))

    def chunk(index):
        first = index * rows
        start = SUB // 2 * first
        if not isinstance(start, int):
            start = pl.multiple_of(start, SUB // 2 * rows)
        for group in range(0, groups, 2):
            members = range(group, min(group + 2, groups))
            pairs = [
                [
                    jnp.dot(
                        band_ref[g, half],
                        cols_ref[g, half, pl.ds(start, SUB // 2 * (rows + 2 * side)), :],
                        preferred_element_type=F32,
                    )
                    for half in range(2)
                ]
                for g in members
            ]
            for pair in range(rows // 2):
                here = slice(SUB * pair, SUB * (pair + 1))
                both = []
                for near, far in pairs:
                    even = jnp.where(lower, near[here], far[here])
                    odd = pltpu.roll(jnp.where(lower, far[here], near[here]), SUB // 2, 0)
                    both.append((even, odd))
                for half in range(2):
                    row = first + 2 * pair + half
                    tiles = [one[half] for one in both]
                    if members[-1] == groups - 1:
                        tiles[-1] = tiles[-1] + tail_ref[row]
                    if len(tiles) == 1:
                        tiles.append(jnp.zeros((SUB, width), F32))
                    conv_ref[row, SUB * group : SUB * (group + 2), :] = jnp.concatenate(
                        tiles, axis=0
                    ).astype(BF16)

    each(height // rows, chunk)


def weight_stage(sci_ref, var_ref, rows_ref, cols_ref, weight_ref, inverse_ref, tail_ref, kernels):
    height, width = weight_ref.shape
    stamps = rows_ref.shape[-1]
    sub = lax.broadcasted_iota(jnp.int32, (SUB, width), 0)
    ones = kernels % SUB

    def held(starts_ref, length):
        place = lax.broadcasted_iota(jnp.int32, (length, stamps), 0) - starts_ref[0]
        return jnp.where((place >= 0) & (place < STAMP), 1.0, 0.0).astype(BF16)

    weight_ref[...] = lax.dot_general(
        held(rows_ref, height),
        held(cols_ref, width),
        (((1,), (1,)), ((), ())),
        preferred_element_type=F32,
    )

    def block(index):
        first = index * SUB
        if not isinstance(first, int):
            first = pl.multiple_of(first, SUB)
        here = pl.ds(first, SUB)
        inverse = 1.0 / var_ref[0, here, :]
        inverse_ref[here, :] = inverse
        weight_ref[here, :] = inverse * weight_ref[here, :]
        pieces = [p.astype(F32) for p in split_bf16(sci_ref[0, here, :], 3)]
        for line in range(SUB):
            value = jnp.where(sub == ones, 1.0, 0.0)
            for piece, part in enumerate(pieces):
                spread = jnp.broadcast_to(part[line : line + 1, :], (SUB, width))
                value = jnp.where(sub == ones + 1 + piece, spread, value)
            tail_ref[first + line] = value

    each(height // SUB, block)


def normal_stage(weight_ref, conv_ref, size):
    height, _, width = conv_ref.shape
    rows = 2

    def chunk(first):
        left, right = [], []
        for row in range(rows):
            design = conv_ref[first + row]
            weight = jnp.broadcast_to(weight_ref[pl.ds(first + row, 1), :], (size, width))
            left.append(jnp.concatenate(split_bf16(design.astype(F32) * weight, 2), axis=0))
            right.append(design)
        return lax.dot_general(
            jnp.concatenate(left, axis=1),
            jnp.concatenate(right, axis=1),
            (((1,), (1,)), ((), ())),
            preferred_element_type=F32,
        )

    if height <= UNROLL:
        product = chunk(0)
        for first in range(rows, height, rows):
            product = product + chunk(first)
    else:
        product = lax.fori_loop(
            0,
            height // rows,
            lambda index, total: total + chunk(index * rows),
            jnp.zeros((2 * size, size), F32),
        )
    return product[0:size] + product[size : 2 * size]


def solve_stage(normal, kernels):
    unknowns = kernels + 1
    width = LANE
    groups = ceil_to(unknowns, SUB) // SUB
    size = normal.shape[1]
    parts = [normal[SUB * g : SUB * (g + 1)] for g in range(groups)]
    if size < width:
        parts = [
            jnp.concatenate([part, jnp.zeros((SUB, width - size), F32)], axis=1)
            for part in parts
        ]

    def pick(value, index, axis):
        where = jnp.full((SUB, width), index, jnp.int32)
        return jnp.take_along_axis(value, where, axis, mode="promise_in_bounds")

    row = lax.broadcasted_iota(jnp.int32, (SUB, width), 0)

    nothing = jnp.zeros((SUB, width), F32)
    straight, across = [nothing] * groups, [nothing] * groups
    edges = [2 * e for e in range(groups // 2)] + [groups]
    for low, high in zip(edges[:-1], edges[1:]):
        members = range(low, high)
        count = ceil_to(min(SUB * high, unknowns) - SUB * low, 2)
        copied = [
            [pick(part, SUB * low + index, 1) for part in parts] for index in range(count)
        ]
        columns = [[one[g] for g in members] for one in copied]
        block = [parts[g] for g in members]
        pivots = []
        for at in range(0, count, 2):
            own, line = at // SUB, at % SUB
            first, second = columns[at], columns[at + 1]
            a, b = pick(first[own], line, 0), pick(second[own], line, 0)
            d = pick(second[own], line + 1, 0)
            inverse = 1.0 / (a * d - b * b)
            a, b, d = a * inverse, b * inverse, d * inverse
            pivots.append((own, line, a, b, d))
            here = (row == line) | (row == line + 1)
            near = [x * d - y * b for x, y in zip(first, second)]
            far = [y * a - x * b for x, y in zip(first, second)]
            near[own] = jnp.where(here, 0.0, near[own])
            far[own] = jnp.where(here, 0.0, far[own])

            def update(value):
                r0, r1 = pick(value[own], line, 0), pick(value[own], line + 1, 0)
                return [v - x * r0 - y * r1 for v, x, y in zip(value, near, far)]

            columns[at + 2 :] = [update(value) for value in columns[at + 2 :]]
            block = update(block)
            group = low + own
            diagonal = jnp.where(row == line + 1, a, straight[group])
            straight[group] = jnp.where(row == line, d, diagonal)
            across[group] = jnp.where(here, b, across[group])
        lines = []
        for own, line, a, b, d in pivots:
            r0, r1 = pick(block[own], line, 0), pick(block[own], line + 1, 0)
            lines += [d * r0 - b * r1, a * r1 - b * r0]
        for group in range(groups):
            if group in members:
                parts[group] = block[group - low]
                continue
            terms = [copied[index][group] * lines[index] for index in range(count)]
            while len(terms) > 1:
                terms = [sum(terms[i : i + 2][1:], terms[i]) for i in range(0, len(terms), 2)]
            parts[group] = parts[group] - terms[0]
    other = row ^ 1
    parts = [
        x * p - y * jnp.take_along_axis(p, other, 0, mode="promise_in_bounds")
        for x, y, p in zip(straight, across, parts)
    ]
    values = [
        pick(p, unknowns, 1) + (pick(p, unknowns + 1, 1) + pick(p, unknowns + 2, 1))
        for p in parts
    ]
    return [jnp.where(row + SUB * g < unknowns, v, 0.0) for g, v in enumerate(values)]


def residual_stage(values, conv_ref, sci_ref, inverse_ref, diff_ref, out_ref, rows_each):
    height, _, width = conv_ref.shape

    def block(index):
        first = index * SUB
        if not isinstance(first, int):
            first = pl.multiple_of(first, SUB)
        lines = []
        for row in range(SUB):
            design = conv_ref[first + row].astype(F32)
            total = design[0:SUB] * values[0]
            for group in range(1, len(values)):
                total = total + design[SUB * group : SUB * (group + 1)] * values[group]
            lines.append(jnp.sum(total, axis=0, keepdims=True))
        model = jnp.concatenate(lines, axis=0)
        here = pl.ds(first, SUB)
        residual = sci_ref[0, here, :] - model
        inverse = inverse_ref[here, :]
        diff_ref[0, here, :] = residual * jnp.sqrt(inverse)
        weighted = residual * inverse
        for start in range(0, SUB, rows_each):
            target = (first + start) // rows_each
            out_ref[target, 0:rows_each, :] = weighted[start : start + rows_each]
            out_ref[target, rows_each : 2 * rows_each, :] = inverse[start : start + rows_each]

    each(height // SUB, block)


def store_coefficients(values, coef_ref, unknowns):
    row = lax.broadcasted_iota(jnp.int32, (SUB, LANE), 0)
    column = lax.broadcasted_iota(jnp.int32, (SUB, LANE), 1)
    total = jnp.zeros((SUB, LANE), F32)
    for group, value in enumerate(values):
        total = total + jnp.where(column == row + SUB * group, value, 0.0)
    coef_ref[...] = jnp.sum(total, axis=0, keepdims=True)[:, 0:unknowns]


def fit(tile, edge, science, variance, col_taps, row_taps, stamp_rows, stamp_cols, rows_each, sky):
    height, width = science.shape[1:]
    tap_count, kernels = col_taps.shape
    unknowns = kernels + 1
    groups = ceil_to(unknowns + 3, SUB) // SUB
    size = ceil_to(unknowns + 3, 2 * SUB)
    tall = ceil_to(kernels, 2 * SUB)
    rows, side = chunk_rows(height)
    local = sky == 1
    vmem = pl.BlockSpec(memory_space=pltpu.VMEM)
    params = pltpu.CompilerParams(vmem_limit_bytes=56 * 1024 * 1024)
    taps = (col_taps, row_taps)

    def result(shape, dtype=F32):
        return pltpu.VMEM(shape, dtype) if local else jax.ShapeDtypeStruct(shape, dtype)

    prepared = [
        ((2, tall, ceil_to(tap_count, SUB)), BF16),
        ((groups, 2, SUB // 2 * rows, SUB // 2 * (rows + 2 * side)), BF16),
        ((height, width), F32),
        ((height, width), F32),
        ((height, SUB, width), F32),
    ]
    pad_shape = pltpu.VMEM((LANE, LANE), F32)
    conv_shape = (height, size, width)
    cols_shape = pltpu.VMEM((groups, 2, SUB // 2 * (height + 2 * side), width), BF16)
    out_shapes = [
        result((1, height, width)),
        result((1, unknowns)),
        result((height // rows_each, 2 * rows_each, width)),
    ]

    def before(sci, var, ct, rt, sr, sc, flipped, band, weight, inverse, tail, pad):
        taps_stage(ct, rt, pad, flipped, band, height)
        weight_stage(sci, var, sr, sc, weight, inverse, tail, kernels)

    def front(tmpl, edges, flipped, band, weight, tail, conv, cols):
        column_stage(tmpl, edges, flipped, cols, height, tap_count)
        row_stage(band, cols, tail, conv)
        return normal_stage(weight, conv, size)

    def back(normal, conv, sci, inverse, diff, coef, out):
        values = solve_stage(normal, kernels)
        store_coefficients(values, coef, unknowns)
        residual_stage(values, conv, sci, inverse, diff, out, rows_each)

    if local:

        def kernel(tmpl, sci, var, ct, rt, sr, sc, diff, coef, out, conv, cols, pad, *tables):
            before(sci, var, ct, rt, sr, sc, *tables, pad)
            flipped, band, weight, inverse, tail = tables
            normal = front(tmpl, None, flipped, band, weight, tail, conv, cols)
            back(normal, conv, sci, inverse, diff, coef, out)

        args = (tile, science, variance) + taps + (stamp_rows, stamp_cols)
        return pl.pallas_call(
            kernel,
            out_shape=out_shapes,
            in_specs=[vmem] * 7,
            out_specs=[vmem] * 3,
            scratch_shapes=[pltpu.VMEM(conv_shape, BF16), cols_shape, pad_shape]
            + [pltpu.VMEM(shape, dtype) for shape, dtype in prepared],
            compiler_params=params,
            name="fit",
        )(*[pltpu.with_memory_space_constraint(arg, pltpu.VMEM) for arg in args])

    flipped, band, weight, inverse, tail = pl.pallas_call(
        before,
        out_shape=[result(shape, dtype) for shape, dtype in prepared],
        in_specs=[vmem] * 6,
        out_specs=[vmem] * 5,
        scratch_shapes=[pad_shape],
        compiler_params=params,
        name="before",
    )(science, variance, *taps, stamp_rows, stamp_cols)

    def first(tmpl, edges, flipped, band, weight, tail, conv, normal, cols):
        normal[...] = front(tmpl, edges, flipped, band, weight, tail, conv, cols)

    conv, normal = pl.pallas_call(
        first,
        out_shape=[result(conv_shape, BF16), result((size, size))],
        in_specs=[vmem] * 6,
        out_specs=[vmem] * 2,
        scratch_shapes=[cols_shape],
        compiler_params=params,
        name="fit_normal",
    )(tile.astype(F32), edge.astype(F32), flipped, band, weight, tail)
    normal = lax.psum(normal, "sky")

    def second(normal, conv, sci, inverse, diff, coef, out):
        back(normal[...], conv, sci, inverse, diff, coef, out)

    return pl.pallas_call(
        second,
        out_shape=out_shapes,
        in_specs=[vmem] * 4,
        out_specs=[vmem] * 3,
        compiler_params=params,
        name="fit_solve",
    )(normal, conv, science, inverse)


def sky_edges(tile, margin, sky):
    ends = sky - 1
    width = tile.shape[1]
    head = tile[:, 0:margin]
    tail = tile[:, width - margin :]
    after = lax.ppermute(head, "sky", [(i + 1, i) for i in range(ends)])
    before = lax.ppermute(tail, "sky", [(i, i + 1) for i in range(ends)])
    middle = jnp.zeros((tile.shape[0], width - 2 * margin), tile.dtype)
    return jnp.concatenate([after, middle, before], axis=1)


def stage_inputs(lines, count, others):
    def kernel(*refs):
        taken, given = refs[: len(refs) // 2], refs[len(refs) // 2 :]
        given[0][...] = jnp.broadcast_to(taken[0][...][None], given[0].shape)
        for source, target in zip(taken[1:], given[1:]):
            target[...] = source[...]

    vmem = pl.BlockSpec(memory_space=pltpu.VMEM)
    return pl.pallas_call(
        kernel,
        out_shape=[pltpu.VMEM((count,) + lines.shape, lines.dtype)]
        + [pltpu.VMEM(other.shape, other.dtype) for other in others],
        in_specs=[vmem] * (1 + len(others)),
        out_specs=[vmem] * (1 + len(others)),
        name="stage_inputs",
    )(lines, *others)


def gather_results(shares, difference, coefficients):
    rows_each = shares.shape[1] // 2

    def kernel(shares_ref, diff_ref, coef_ref, diff_out, coef_out, out_ref):
        diff_out[...] = diff_ref[...]
        coef_out[...] = coef_ref[...]
        total = jnp.sum(shares_ref[...], axis=0)
        out_ref[...] = total[0:rows_each] / jnp.sqrt(total[rows_each:])

    vmem = pl.BlockSpec(memory_space=pltpu.VMEM)
    args = (shares, difference, coefficients)
    return pl.pallas_call(
        kernel,
        out_shape=[
            jax.ShapeDtypeStruct(difference.shape, F32),
            jax.ShapeDtypeStruct(coefficients.shape, F32),
            jax.ShapeDtypeStruct((rows_each, shares.shape[2]), F32),
        ],
        in_specs=[vmem] * 3,
        out_specs=[vmem] * 3,
        name="results",
    )(*[pltpu.with_memory_space_constraint(arg, pltpu.VMEM) for arg in args])


def solution(mesh):
    visits = mesh.shape["visit"]
    sky = mesh.shape["sky"]

    def on_device(template, science, variance, col_taps, row_taps, stamp_rows, stamp_cols):
        rows_each, width = template.shape
        margin = (col_taps.shape[1] - 1) // 2
        others = (science, variance, col_taps.T, row_taps.T, stamp_rows, stamp_cols)
        if sky == 1:
            copies, *rest = stage_inputs(template, visits, others[2:])
            others = others[:2] + tuple(rest)
        else:
            copies = jnp.broadcast_to(template[None], (visits, rows_each, width))
        tile = lax.all_to_all(copies, "visit", 0, 0, tiled=True).reshape(-1, width)
        edge = sky_edges(tile, margin, sky) if sky > 1 else None
        difference, coefficients, shares = fit(tile, edge, *others, rows_each, sky)
        shares = lax.all_to_all(shares, "visit", 0, 0, tiled=True)
        if sky == 1:
            return gather_results(shares, difference, coefficients)
        total = jnp.sum(shares, axis=0)
        detection = total[0:rows_each] / jnp.sqrt(total[rows_each:])
        return difference, coefficients, detection

    in_specs = (
        P(("group", "visit"), "sky"),
        P(("group", "visit"), None, "sky"),
        P(("group", "visit"), None, "sky"),
        P(),
        P(),
        P(("group", "visit"), "sky", None),
        P(("group", "visit"), "sky", None),
    )
    out_specs = (
        P(("group", "visit"), None, "sky"),
        P(("group", "visit"), None),
        P(("group", "visit"), "sky"),
    )
    return jax.shard_map(
        on_device, mesh=mesh, in_specs=in_specs, out_specs=out_specs, check_vma=False
    )
```

```python
import jax
import jax.numpy as jnp
from jax import lax
from jax.experimental import pallas as pl
from jax.experimental.pallas import tpu as pltpu
from jax.sharding import PartitionSpec as P

STAMP = 16
SUB = 8
LANE = 128
UNROLL = 32
CHUNK = 32
F32 = jnp.float32
BF16 = jnp.bfloat16


def ceil_to(value, step):
    return (value + step - 1) // step * step


def each(count, body):
    if count <= UNROLL:
        for index in range(count):
            body(index)
    else:
        lax.fori_loop(0, count, lambda index, carry: (body(index), carry)[1], 0)


def lanes_of(index, width):
    if isinstance(index, int):
        return slice(index * width, (index + 1) * width)
    return pl.ds(pl.multiple_of(index * width, width), width)


def split_bf16(value, pieces):
    out = []
    for piece in range(pieces):
        part = value.astype(BF16)
        out.append(part)
        if piece + 1 < pieces:
            value = value - part.astype(F32)
    return out


def load_taps(taps_ref, pad_ref):
    taps, kernels = taps_ref.shape
    pad_ref[...] = jnp.zeros(pad_ref.shape, F32)
    pad_ref[0:taps, 0:kernels] = taps_ref[...].astype(F32)
    return pad_ref[...].T


def chunk_rows(height):
    rows = min(CHUNK, height)
    return rows, (0 if rows == height else CHUNK // 2)


def halves(shape):
    return (lax.broadcasted_iota(jnp.int32, shape, 0) & (SUB - 1)) < SUB // 2


def turned(value):
    tiles = [value[at : at + SUB] for at in range(0, value.shape[0], SUB)]
    return jnp.concatenate([pltpu.roll(tile, SUB // 2, 0) for tile in tiles], axis=0)


def taps_stage(col_taps_ref, row_taps_ref, pad_ref, flipped_ref, band_ref, height):
    tap_count = col_taps_ref.shape[0]
    margin = (tap_count - 1) // 2
    span = ceil_to(tap_count, SUB)
    groups = band_ref.shape[0]
    rows, side = chunk_rows(height)
    reach = rows + 2 * side
    wide = SUB // 2 * reach
    tall = groups * SUB
    taps = load_taps(col_taps_ref, pad_ref)[0 : flipped_ref.shape[1], 0:span]
    flip = (
        lax.broadcasted_iota(jnp.int32, (span, span), 0)
        + lax.broadcasted_iota(jnp.int32, (span, span), 1)
        == tap_count - 1
    ).astype(BF16)
    reversed_taps = jnp.dot(taps.astype(BF16), flip, preferred_element_type=F32)
    flipped_ref[0] = reversed_taps.astype(BF16)
    flipped_ref[1] = turned(reversed_taps).astype(BF16)
    taps = load_taps(row_taps_ref, pad_ref)[0:tall, 0:span]
    other = turned(taps)
    lower = halves((tall, span))
    tap = lax.broadcasted_iota(jnp.int32, (span, wide), 0)
    lane = lax.broadcasted_iota(jnp.int32, (span, wide), 1)
    sub = lax.broadcasted_iota(jnp.int32, (SUB, wide), 0)
    along = lax.broadcasted_iota(jnp.int32, (SUB, wide), 1)
    own = (sub & (SUB // 2 - 1)) == (along & (SUB // 2 - 1))
    bit = (SUB // 2).bit_length() - 1
    for half in range(2):
        four = jnp.where(lower, taps, other) if half == 0 else jnp.where(lower, other, taps)

        def line_of(index):
            return 2 * (index >> (bit + 1)) + (((index >> bit) & 1) ^ half)

        def base(shift):
            source = line_of(lane) - shift - side + margin
            source = jnp.where(source >= reach, source - reach, source)
            source = jnp.where(source < 0, source + reach, source)
            repeat = jnp.where(source == tap, 1.0, 0.0).astype(BF16)
            return jnp.dot(four.astype(BF16), repeat, preferred_element_type=F32)

        first, second = base(0), base(1)
        place = line_of(along) - line_of(sub) - side
        late = line_of(sub) == 1
        spread = []
        for group in range(groups):
            here = slice(SUB * group, SUB * (group + 1))
            spread.append(jnp.where(own, jnp.where(late, second[here], first[here]), 0.0))

        for index in range(0, rows // 2, 2):
            inside = [
                (place >= 2 * pair - margin) & (place <= 2 * pair + margin)
                for pair in (index, index + 1)
            ]
            for group in range(groups):
                both = [
                    jnp.where(inside[pair], pltpu.roll(spread[group], SUB * (index + pair), 1), 0.0)
                    for pair in range(2)
                ]
                both = jnp.concatenate(both, axis=0).astype(BF16)
                band_ref[group, half, SUB * index : SUB * (index + 2), :] = both


def column_stage(tmpl_ref, edge_ref, flipped_ref, cols_ref, height, tap_count):
    width = tmpl_ref.shape[1]
    margin = (tap_count - 1) // 2
    span = ceil_to(tap_count, SUB)
    groups = cols_ref.shape[0]
    _, side = chunk_rows(height)
    place = lax.broadcasted_iota(jnp.int32, (span, width), 1) + (
        margin - lax.broadcasted_iota(jnp.int32, (span, width), 0)
    )
    inside = (place >= 0) & (place < width)
    lower = halves((SUB, width))
    if side:
        nothing = jnp.zeros((groups, 2, SUB // 2 * side, width), BF16)
        cols_ref[:, :, 0 : SUB // 2 * side, :] = nothing
        cols_ref[:, :, SUB // 2 * (side + height) :, :] = nothing

    def shifted(row):
        line = jnp.broadcast_to(tmpl_ref[pl.ds(row, 1), :].astype(F32), (span, width))
        line = pltpu.roll(line, width - margin, 1, stride=1, stride_axis=0)
        if edge_ref is None:
            return jnp.where(inside, line, 0.0).astype(BF16)
        other = jnp.broadcast_to(edge_ref[pl.ds(row, 1), :].astype(F32), (span, width))
        other = pltpu.roll(other, width - margin, 1, stride=1, stride_axis=0)
        return jnp.where(inside, line, other).astype(BF16)

    def quad(index):
        results = []
        for odd in range(2):
            row = 4 * index + odd
            both = jnp.concatenate([shifted(row), shifted(row + 2)], axis=1)
            results.append(jnp.dot(flipped_ref[odd], both, preferred_element_type=F32))
        start = 2 * SUB * index + SUB // 2 * side
        if not isinstance(start, int):
            start = pl.multiple_of(start, 2 * SUB)
        for group in range(groups):
            even, odd = [value[SUB * group : SUB * (group + 1)] for value in results]
            even, odd = [[v[:, 0:width], v[:, width:]] for v in (even, odd)]
            for half in range(2):
                tiles = [
                    jnp.where(lower, e, o) if half == 0 else jnp.where(lower, o, e)
                    for e, o in zip(even, odd)
                ]
                two = jnp.concatenate(tiles, axis=0)
                cols_ref[group, half, pl.ds(start, 2 * SUB), :] = two.astype(BF16)

    each(height // 4, quad)


def row_stage(band_ref, cols_ref, tail_ref, conv_ref):
    height, _, width = conv_ref.shape
    groups = band_ref.shape[0]
    rows, side = chunk_rows(height)
    lower = halves((SUB, width))

    def chunk(index):
        first = index * rows
        start = SUB // 2 * first
        if not isinstance(start, int):
            start = pl.multiple_of(start, SUB // 2 * rows)
        for group in range(0, groups, 2):
            members = range(group, min(group + 2, groups))
            pairs = [
                [
                    jnp.dot(
                        band_ref[g, half],
                        cols_ref[g, half, pl.ds(start, SUB // 2 * (rows + 2 * side)), :],
                        preferred_element_type=F32,
                    )
                    for half in range(2)
                ]
                for g in members
            ]
            for pair in range(rows // 2):
                here = slice(SUB * pair, SUB * (pair + 1))
                both = []
                for near, far in pairs:
                    even = jnp.where(lower, near[here], far[here])
                    odd = pltpu.roll(jnp.where(lower, far[here], near[here]), SUB // 2, 0)
                    both.append((even, odd))
                for half in range(2):
                    row = first + 2 * pair + half
                    tiles = [one[half] for one in both]
                    if members[-1] == groups - 1:
                        tiles[-1] = tiles[-1] + tail_ref[row]
                    if len(tiles) == 1:
                        tiles.append(jnp.zeros((SUB, width), F32))
                    conv_ref[row, SUB * group : SUB * (group + 2), :] = jnp.concatenate(
                        tiles, axis=0
                    ).astype(BF16)

    each(height // rows, chunk)


def weight_stage(sci_ref, var_ref, rows_ref, cols_ref, weight_ref, inverse_ref, tail_ref, kernels):
    height, width = weight_ref.shape
    stamps = rows_ref.shape[-1]
    sub = lax.broadcasted_iota(jnp.int32, (SUB, width), 0)
    ones = kernels % SUB

    def held(starts_ref, length):
        place = lax.broadcasted_iota(jnp.int32, (length, stamps), 0) - starts_ref[0]
        return jnp.where((place >= 0) & (place < STAMP), 1.0, 0.0).astype(BF16)

    weight_ref[...] = lax.dot_general(
        held(rows_ref, height),
        held(cols_ref, width),
        (((1,), (1,)), ((), ())),
        preferred_element_type=F32,
    )

    def block(index):
        first = index * SUB
        if not isinstance(first, int):
            first = pl.multiple_of(first, SUB)
        here = pl.ds(first, SUB)
        inverse = 1.0 / var_ref[0, here, :]
        inverse_ref[here, :] = inverse
        weight_ref[here, :] = inverse * weight_ref[here, :]
        pieces = [p.astype(F32) for p in split_bf16(sci_ref[0, here, :], 3)]
        for line in range(SUB):
            value = jnp.where(sub == ones, 1.0, 0.0)
            for piece, part in enumerate(pieces):
                spread = jnp.broadcast_to(part[line : line + 1, :], (SUB, width))
                value = jnp.where(sub == ones + 1 + piece, spread, value)
            tail_ref[first + line] = value

    each(height // SUB, block)


def normal_stage(weight_ref, conv_ref, size):
    height, _, width = conv_ref.shape
    rows = 8

    def chunk(first):
        left, right = [], []
        for row in range(rows):
            design = conv_ref[first + row]
            weight = jnp.broadcast_to(weight_ref[pl.ds(first + row, 1), :], (size, width))
            left.append(jnp.concatenate(split_bf16(design.astype(F32) * weight, 2), axis=0))
            right.append(design)
        return lax.dot_general(
            jnp.concatenate(left, axis=1),
            jnp.concatenate(right, axis=1),
            (((1,), (1,)), ((), ())),
            preferred_element_type=F32,
        )

    if height <= UNROLL:
        product = chunk(0)
        for first in range(rows, height, rows):
            product = product + chunk(first)
    else:
        product = lax.fori_loop(
            0,
            height // rows,
            lambda index, total: total + chunk(index * rows),
            jnp.zeros((2 * size, size), F32),
        )
    return product[0:size] + product[size : 2 * size]


def solve_stage(normal, kernels):
    unknowns = kernels + 1
    width = LANE
    groups = ceil_to(unknowns, SUB) // SUB
    size = normal.shape[1]
    parts = [normal[SUB * g : SUB * (g + 1)] for g in range(groups)]
    if size < width:
        parts = [
            jnp.concatenate([part, jnp.zeros((SUB, width - size), F32)], axis=1)
            for part in parts
        ]

    def pick(value, index, axis):
        where = jnp.full((SUB, width), index, jnp.int32)
        return jnp.take_along_axis(value, where, axis, mode="promise_in_bounds")

    row = lax.broadcasted_iota(jnp.int32, (SUB, width), 0)

    nothing = jnp.zeros((SUB, width), F32)
    straight, across = [nothing] * groups, [nothing] * groups
    edges = [2 * e for e in range(groups // 2)] + [groups]
    for low, high in zip(edges[:-1], edges[1:]):
        members = range(low, high)
        count = ceil_to(min(SUB * high, unknowns) - SUB * low, 2)
        copied = [
            [pick(part, SUB * low + index, 1) for part in parts] for index in range(count)
        ]
        columns = [[one[g] for g in members] for one in copied]
        block = [parts[g] for g in members]
        pivots = []
        for at in range(0, count, 2):
            own, line = at // SUB, at % SUB
            first, second = columns[at], columns[at + 1]
            a, b = pick(first[own], line, 0), pick(second[own], line, 0)
            d = pick(second[own], line + 1, 0)
            inverse = 1.0 / (a * d - b * b)
            a, b, d = a * inverse, b * inverse, d * inverse
            pivots.append((own, line, a, b, d))
            here = (row == line) | (row == line + 1)
            near = [x * d - y * b for x, y in zip(first, second)]
            far = [y * a - x * b for x, y in zip(first, second)]
            near[own] = jnp.where(here, 0.0, near[own])
            far[own] = jnp.where(here, 0.0, far[own])

            def update(value):
                r0, r1 = pick(value[own], line, 0), pick(value[own], line + 1, 0)
                return [v - x * r0 - y * r1 for v, x, y in zip(value, near, far)]

            columns[at + 2 :] = [update(value) for value in columns[at + 2 :]]
            block = update(block)
            group = low + own
            diagonal = jnp.where(row == line + 1, a, straight[group])
            straight[group] = jnp.where(row == line, d, diagonal)
            across[group] = jnp.where(here, b, across[group])
        lines = []
        for own, line, a, b, d in pivots:
            r0, r1 = pick(block[own], line, 0), pick(block[own], line + 1, 0)
            lines += [d * r0 - b * r1, a * r1 - b * r0]
        for group in range(groups):
            if group in members:
                parts[group] = block[group - low]
                continue
            terms = [copied[index][group] * lines[index] for index in range(count)]
            while len(terms) > 1:
                terms = [sum(terms[i : i + 2][1:], terms[i]) for i in range(0, len(terms), 2)]
            parts[group] = parts[group] - terms[0]
    other = row ^ 1
    parts = [
        x * p - y * jnp.take_along_axis(p, other, 0, mode="promise_in_bounds")
        for x, y, p in zip(straight, across, parts)
    ]
    values = [
        pick(p, unknowns, 1) + (pick(p, unknowns + 1, 1) + pick(p, unknowns + 2, 1))
        for p in parts
    ]
    return [jnp.where(row + SUB * g < unknowns, v, 0.0) for g, v in enumerate(values)]


def residual_stage(values, conv_ref, sci_ref, inverse_ref, diff_ref, out_ref, rows_each):
    height, _, width = conv_ref.shape

    def block(index):
        first = index * SUB
        if not isinstance(first, int):
            first = pl.multiple_of(first, SUB)
        lines = []
        for row in range(SUB):
            design = conv_ref[first + row].astype(F32)
            total = design[0:SUB] * values[0]
            for group in range(1, len(values)):
                total = total + design[SUB * group : SUB * (group + 1)] * values[group]
            lines.append(jnp.sum(total, axis=0, keepdims=True))
        model = jnp.concatenate(lines, axis=0)
        here = pl.ds(first, SUB)
        residual = sci_ref[0, here, :] - model
        inverse = inverse_ref[here, :]
        diff_ref[0, here, :] = residual * jnp.sqrt(inverse)
        weighted = residual * inverse
        for start in range(0, SUB, rows_each):
            target = (first + start) // rows_each
            out_ref[target, 0:rows_each, :] = weighted[start : start + rows_each]
            out_ref[target, rows_each : 2 * rows_each, :] = inverse[start : start + rows_each]

    each(height // SUB, block)


def store_coefficients(values, coef_ref, unknowns):
    row = lax.broadcasted_iota(jnp.int32, (SUB, LANE), 0)
    column = lax.broadcasted_iota(jnp.int32, (SUB, LANE), 1)
    total = jnp.zeros((SUB, LANE), F32)
    for group, value in enumerate(values):
        total = total + jnp.where(column == row + SUB * group, value, 0.0)
    coef_ref[...] = jnp.sum(total, axis=0, keepdims=True)[:, 0:unknowns]


def fit(tile, edge, science, variance, col_taps, row_taps, stamp_rows, stamp_cols, rows_each, sky):
    height, width = science.shape[1:]
    tap_count, kernels = col_taps.shape
    unknowns = kernels + 1
    groups = ceil_to(unknowns + 3, SUB) // SUB
    size = ceil_to(unknowns + 3, 2 * SUB)
    tall = ceil_to(kernels, 2 * SUB)
    rows, side = chunk_rows(height)
    local = sky == 1
    vmem = pl.BlockSpec(memory_space=pltpu.VMEM)
    params = pltpu.CompilerParams(vmem_limit_bytes=56 * 1024 * 1024)
    taps = (col_taps, row_taps)

    def result(shape, dtype=F32):
        return pltpu.VMEM(shape, dtype) if local else jax.ShapeDtypeStruct(shape, dtype)

    prepared = [
        ((2, tall, ceil_to(tap_count, SUB)), BF16),
        ((groups, 2, SUB // 2 * rows, SUB // 2 * (rows + 2 * side)), BF16),
        ((height, width), F32),
        ((height, width), F32),
        ((height, SUB, width), F32),
    ]
    pad_shape = pltpu.VMEM((LANE, LANE), F32)
    conv_shape = (height, size, width)
    cols_shape = pltpu.VMEM((groups, 2, SUB // 2 * (height + 2 * side), width), BF16)
    out_shapes = [
        result((1, height, width)),
        result((1, unknowns)),
        result((height // rows_each, 2 * rows_each, width)),
    ]

    def before(sci, var, ct, rt, sr, sc, flipped, band, weight, inverse, tail, pad):
        taps_stage(ct, rt, pad, flipped, band, height)
        weight_stage(sci, var, sr, sc, weight, inverse, tail, kernels)

    def front(tmpl, edges, flipped, band, weight, tail, conv, cols):
        column_stage(tmpl, edges, flipped, cols, height, tap_count)
        row_stage(band, cols, tail, conv)
        return normal_stage(weight, conv, size)

    def back(normal, conv, sci, inverse, diff, coef, out):
        values = solve_stage(normal, kernels)
        store_coefficients(values, coef, unknowns)
        residual_stage(values, conv, sci, inverse, diff, out, rows_each)

    if local:

        def kernel(tmpl, sci, var, ct, rt, sr, sc, diff, coef, out, conv, cols, pad, *tables):
            before(sci, var, ct, rt, sr, sc, *tables, pad)
            flipped, band, weight, inverse, tail = tables
            normal = front(tmpl, None, flipped, band, weight, tail, conv, cols)
            back(normal, conv, sci, inverse, diff, coef, out)

        args = (tile, science, variance) + taps + (stamp_rows, stamp_cols)
        return pl.pallas_call(
            kernel,
            out_shape=out_shapes,
            in_specs=[vmem] * 7,
            out_specs=[vmem] * 3,
            scratch_shapes=[pltpu.VMEM(conv_shape, BF16), cols_shape, pad_shape]
            + [pltpu.VMEM(shape, dtype) for shape, dtype in prepared],
            compiler_params=params,
            name="fit",
        )(*[pltpu.with_memory_space_constraint(arg, pltpu.VMEM) for arg in args])

    flipped, band, weight, inverse, tail = pl.pallas_call(
        before,
        out_shape=[result(shape, dtype) for shape, dtype in prepared],
        in_specs=[vmem] * 6,
        out_specs=[vmem] * 5,
        scratch_shapes=[pad_shape],
        compiler_params=params,
        name="before",
    )(science, variance, *taps, stamp_rows, stamp_cols)

    def first(tmpl, edges, flipped, band, weight, tail, conv, normal, cols):
        normal[...] = front(tmpl, edges, flipped, band, weight, tail, conv, cols)

    conv, normal = pl.pallas_call(
        first,
        out_shape=[result(conv_shape, BF16), result((size, size))],
        in_specs=[vmem] * 6,
        out_specs=[vmem] * 2,
        scratch_shapes=[cols_shape],
        compiler_params=params,
        name="fit_normal",
    )(tile.astype(F32), edge.astype(F32), flipped, band, weight, tail)
    normal = lax.psum(normal, "sky")

    def second(normal, conv, sci, inverse, diff, coef, out):
        back(normal[...], conv, sci, inverse, diff, coef, out)

    return pl.pallas_call(
        second,
        out_shape=out_shapes,
        in_specs=[vmem] * 4,
        out_specs=[vmem] * 3,
        compiler_params=params,
        name="fit_solve",
    )(normal, conv, science, inverse)


def sky_edges(tile, margin, sky):
    ends = sky - 1
    width = tile.shape[1]
    head = tile[:, 0:margin]
    tail = tile[:, width - margin :]
    after = lax.ppermute(head, "sky", [(i + 1, i) for i in range(ends)])
    before = lax.ppermute(tail, "sky", [(i, i + 1) for i in range(ends)])
    middle = jnp.zeros((tile.shape[0], width - 2 * margin), tile.dtype)
    return jnp.concatenate([after, middle, before], axis=1)


def stage_inputs(lines, count, others):
    def kernel(*refs):
        taken, given = refs[: len(refs) // 2], refs[len(refs) // 2 :]
        given[0][...] = jnp.broadcast_to(taken[0][...][None], given[0].shape)
        for source, target in zip(taken[1:], given[1:]):
            target[...] = source[...]

    vmem = pl.BlockSpec(memory_space=pltpu.VMEM)
    return pl.pallas_call(
        kernel,
        out_shape=[pltpu.VMEM((count,) + lines.shape, lines.dtype)]
        + [pltpu.VMEM(other.shape, other.dtype) for other in others],
        in_specs=[vmem] * (1 + len(others)),
        out_specs=[vmem] * (1 + len(others)),
        name="stage_inputs",
    )(lines, *others)


def gather_results(shares, difference, coefficients):
    rows_each = shares.shape[1] // 2

    def kernel(shares_ref, diff_ref, coef_ref, diff_out, coef_out, out_ref):
        diff_out[...] = diff_ref[...]
        coef_out[...] = coef_ref[...]
        total = jnp.sum(shares_ref[...], axis=0)
        out_ref[...] = total[0:rows_each] / jnp.sqrt(total[rows_each:])

    vmem = pl.BlockSpec(memory_space=pltpu.VMEM)
    args = (shares, difference, coefficients)
    return pl.pallas_call(
        kernel,
        out_shape=[
            jax.ShapeDtypeStruct(difference.shape, F32),
            jax.ShapeDtypeStruct(coefficients.shape, F32),
            jax.ShapeDtypeStruct((rows_each, shares.shape[2]), F32),
        ],
        in_specs=[vmem] * 3,
        out_specs=[vmem] * 3,
        name="results",
    )(*[pltpu.with_memory_space_constraint(arg, pltpu.VMEM) for arg in args])


def solution(mesh):
    visits = mesh.shape["visit"]
    sky = mesh.shape["sky"]

    def on_device(template, science, variance, col_taps, row_taps, stamp_rows, stamp_cols):
        rows_each, width = template.shape
        margin = (col_taps.shape[1] - 1) // 2
        others = (science, variance, col_taps.T, row_taps.T, stamp_rows, stamp_cols)
        if sky == 1:
            copies, *rest = stage_inputs(template, visits, others[2:])
            others = others[:2] + tuple(rest)
        else:
            copies = jnp.broadcast_to(template[None], (visits, rows_each, width))
        tile = lax.all_to_all(copies, "visit", 0, 0, tiled=True).reshape(-1, width)
        edge = sky_edges(tile, margin, sky) if sky > 1 else None
        difference, coefficients, shares = fit(tile, edge, *others, rows_each, sky)
        shares = lax.all_to_all(shares, "visit", 0, 0, tiled=True)
        if sky == 1:
            return gather_results(shares, difference, coefficients)
        total = jnp.sum(shares, axis=0)
        detection = total[0:rows_each] / jnp.sqrt(total[rows_each:])
        return difference, coefficients, detection

    in_specs = (
        P(("group", "visit"), "sky"),
        P(("group", "visit"), None, "sky"),
        P(("group", "visit"), None, "sky"),
        P(),
        P(),
        P(("group", "visit"), "sky", None),
        P(("group", "visit"), "sky", None),
    )
    out_specs = (
        P(("group", "visit"), None, "sky"),
        P(("group", "visit"), None),
        P(("group", "visit"), "sky"),
    )
    return jax.shard_map(
        on_device, mesh=mesh, in_specs=in_specs, out_specs=out_specs, check_vma=False
    )
```

```python
import jax
import jax.numpy as jnp
from jax import lax
from jax.experimental import pallas as pl
from jax.experimental.pallas import tpu as pltpu
from jax.sharding import PartitionSpec as P

STAMP = 16
SUB = 8
LANE = 128
UNROLL = 32
CHUNK = 32
F32 = jnp.float32
BF16 = jnp.bfloat16


def ceil_to(value, step):
    return (value + step - 1) // step * step


def each(count, body):
    if count <= UNROLL:
        for index in range(count):
            body(index)
    else:
        lax.fori_loop(0, count, lambda index, carry: (body(index), carry)[1], 0)


def lanes_of(index, width):
    if isinstance(index, int):
        return slice(index * width, (index + 1) * width)
    return pl.ds(pl.multiple_of(index * width, width), width)


def split_bf16(value, pieces):
    out = []
    for piece in range(pieces):
        part = value.astype(BF16)
        out.append(part)
        if piece + 1 < pieces:
            value = value - part.astype(F32)
    return out


def load_taps(taps_ref, pad_ref):
    taps, kernels = taps_ref.shape
    pad_ref[...] = jnp.zeros(pad_ref.shape, F32)
    pad_ref[0:taps, 0:kernels] = taps_ref[...].astype(F32)
    return pad_ref[...].T


def chunk_rows(height):
    rows = min(CHUNK, height)
    return rows, (0 if rows == height else CHUNK // 2)


def halves(shape):
    return (lax.broadcasted_iota(jnp.int32, shape, 0) & (SUB - 1)) < SUB // 2


def turned(value):
    tiles = [value[at : at + SUB] for at in range(0, value.shape[0], SUB)]
    return jnp.concatenate([pltpu.roll(tile, SUB // 2, 0) for tile in tiles], axis=0)


def taps_stage(col_taps_ref, row_taps_ref, pad_ref, flipped_ref, band_ref, height):
    tap_count = col_taps_ref.shape[0]
    margin = (tap_count - 1) // 2
    span = ceil_to(tap_count, SUB)
    groups = band_ref.shape[0]
    rows, side = chunk_rows(height)
    reach = rows + 2 * side
    wide = SUB // 2 * reach
    tall = groups * SUB
    taps = load_taps(col_taps_ref, pad_ref)[0 : flipped_ref.shape[1], 0:span]
    flip = (
        lax.broadcasted_iota(jnp.int32, (span, span), 0)
        + lax.broadcasted_iota(jnp.int32, (span, span), 1)
        == tap_count - 1
    ).astype(BF16)
    reversed_taps = jnp.dot(taps.astype(BF16), flip, preferred_element_type=F32)
    flipped_ref[0] = reversed_taps.astype(BF16)
    flipped_ref[1] = turned(reversed_taps).astype(BF16)
    taps = load_taps(row_taps_ref, pad_ref)[0:tall, 0:span]
    other = turned(taps)
    lower = halves((tall, span))
    tap = lax.broadcasted_iota(jnp.int32, (span, wide), 0)
    lane = lax.broadcasted_iota(jnp.int32, (span, wide), 1)
    sub = lax.broadcasted_iota(jnp.int32, (SUB, wide), 0)
    along = lax.broadcasted_iota(jnp.int32, (SUB, wide), 1)
    own = (sub & (SUB // 2 - 1)) == (along & (SUB // 2 - 1))
    bit = (SUB // 2).bit_length() - 1
    for half in range(2):
        four = jnp.where(lower, taps, other) if half == 0 else jnp.where(lower, other, taps)

        def line_of(index):
            return 2 * (index >> (bit + 1)) + (((index >> bit) & 1) ^ half)

        def base(shift):
            source = line_of(lane) - shift - side + margin
            source = jnp.where(source >= reach, source - reach, source)
            source = jnp.where(source < 0, source + reach, source)
            repeat = jnp.where(source == tap, 1.0, 0.0).astype(BF16)
            return jnp.dot(four.astype(BF16), repeat, preferred_element_type=F32)

        first, second = base(0), base(1)
        place = line_of(along) - line_of(sub) - side
        late = line_of(sub) == 1
        spread = []
        for group in range(groups):
            here = slice(SUB * group, SUB * (group + 1))
            spread.append(jnp.where(own, jnp.where(late, second[here], first[here]), 0.0))

        for index in range(0, rows // 2, 2):
            inside = [
                (place >= 2 * pair - margin) & (place <= 2 * pair + margin)
                for pair in (index, index + 1)
            ]
            for group in range(groups):
                both = [
                    jnp.where(inside[pair], pltpu.roll(spread[group], SUB * (index + pair), 1), 0.0)
                    for pair in range(2)
                ]
                both = jnp.concatenate(both, axis=0).astype(BF16)
                band_ref[group, half, SUB * index : SUB * (index + 2), :] = both


def column_stage(tmpl_ref, edge_ref, flipped_ref, cols_ref, height, tap_count):
    width = tmpl_ref.shape[1]
    margin = (tap_count - 1) // 2
    span = ceil_to(tap_count, SUB)
    groups = cols_ref.shape[0]
    _, side = chunk_rows(height)
    place = lax.broadcasted_iota(jnp.int32, (span, width), 1) + (
        margin - lax.broadcasted_iota(jnp.int32, (span, width), 0)
    )
    inside = (place >= 0) & (place < width)
    lower = halves((SUB, width))
    if side:
        nothing = jnp.zeros((groups, 2, SUB // 2 * side, width), BF16)
        cols_ref[:, :, 0 : SUB // 2 * side, :] = nothing
        cols_ref[:, :, SUB // 2 * (side + height) :, :] = nothing

    def shifted(row):
        line = jnp.broadcast_to(tmpl_ref[pl.ds(row, 1), :].astype(F32), (span, width))
        line = pltpu.roll(line, width - margin, 1, stride=1, stride_axis=0)
        if edge_ref is None:
            return jnp.where(inside, line, 0.0).astype(BF16)
        other = jnp.broadcast_to(edge_ref[pl.ds(row, 1), :].astype(F32), (span, width))
        other = pltpu.roll(other, width - margin, 1, stride=1, stride_axis=0)
        return jnp.where(inside, line, other).astype(BF16)

    def quad(index):
        results = []
        for odd in range(2):
            row = 4 * index + odd
            both = jnp.concatenate([shifted(row), shifted(row + 2)], axis=1)
            results.append(jnp.dot(flipped_ref[odd], both, preferred_element_type=F32))
        start = 2 * SUB * index + SUB // 2 * side
        if not isinstance(start, int):
            start = pl.multiple_of(start, 2 * SUB)
        for group in range(groups):
            even, odd = [value[SUB * group : SUB * (group + 1)] for value in results]
            even, odd = [[v[:, 0:width], v[:, width:]] for v in (even, odd)]
            for half in range(2):
                tiles = [
                    jnp.where(lower, e, o) if half == 0 else jnp.where(lower, o, e)
                    for e, o in zip(even, odd)
                ]
                two = jnp.concatenate(tiles, axis=0)
                cols_ref[group, half, pl.ds(start, 2 * SUB), :] = two.astype(BF16)

    each(height // 4, quad)


def row_stage(band_ref, cols_ref, tail_ref, conv_ref):
    height, _, width = conv_ref.shape
    groups = band_ref.shape[0]
    rows, side = chunk_rows(height)
    lower = halves((SUB, width))

    def chunk(index):
        first = index * rows
        start = SUB // 2 * first
        if not isinstance(start, int):
            start = pl.multiple_of(start, SUB // 2 * rows)
        for group in range(0, groups, 2):
            members = range(group, min(group + 2, groups))
            pairs = [
                [
                    jnp.dot(
                        band_ref[g, half],
                        cols_ref[g, half, pl.ds(start, SUB // 2 * (rows + 2 * side)), :],
                        preferred_element_type=F32,
                    )
                    for half in range(2)
                ]
                for g in members
            ]
            for pair in range(rows // 2):
                here = slice(SUB * pair, SUB * (pair + 1))
                both = []
                for near, far in pairs:
                    even = jnp.where(lower, near[here], far[here])
                    odd = pltpu.roll(jnp.where(lower, far[here], near[here]), SUB // 2, 0)
                    both.append((even, odd))
                for half in range(2):
                    row = first + 2 * pair + half
                    tiles = [one[half] for one in both]
                    if members[-1] == groups - 1:
                        tiles[-1] = tiles[-1] + tail_ref[row]
                    if len(tiles) == 1:
                        tiles.append(jnp.zeros((SUB, width), F32))
                    conv_ref[row, SUB * group : SUB * (group + 2), :] = jnp.concatenate(
                        tiles, axis=0
                    ).astype(BF16)

    each(height // rows, chunk)


def weight_stage(sci_ref, var_ref, rows_ref, cols_ref, weight_ref, inverse_ref, tail_ref, kernels):
    height, width = weight_ref.shape
    stamps = rows_ref.shape[-1]
    sub = lax.broadcasted_iota(jnp.int32, (SUB, width), 0)
    ones = kernels % SUB

    def held(starts_ref, length):
        place = lax.broadcasted_iota(jnp.int32, (length, stamps), 0) - starts_ref[0]
        return jnp.where((place >= 0) & (place < STAMP), 1.0, 0.0).astype(BF16)

    weight_ref[...] = lax.dot_general(
        held(rows_ref, height),
        held(cols_ref, width),
        (((1,), (1,)), ((), ())),
        preferred_element_type=F32,
    )

    def block(index):
        first = index * SUB
        if not isinstance(first, int):
            first = pl.multiple_of(first, SUB)
        here = pl.ds(first, SUB)
        inverse = 1.0 / var_ref[0, here, :]
        inverse_ref[here, :] = inverse
        weight_ref[here, :] = inverse * weight_ref[here, :]
        pieces = [p.astype(F32) for p in split_bf16(sci_ref[0, here, :], 3)]
        for line in range(SUB):
            value = jnp.where(sub == ones, 1.0, 0.0)
            for piece, part in enumerate(pieces):
                spread = jnp.broadcast_to(part[line : line + 1, :], (SUB, width))
                value = jnp.where(sub == ones + 1 + piece, spread, value)
            tail_ref[first + line] = value

    each(height // SUB, block)


def normal_stage(weight_ref, conv_ref, size):
    height, _, width = conv_ref.shape
    rows = 2

    def chunk(first):
        left, right = [], []
        for row in range(rows):
            design = conv_ref[first + row]
            weight = jnp.broadcast_to(weight_ref[pl.ds(first + row, 1), :], (size, width))
            left.append(jnp.concatenate(split_bf16(design.astype(F32) * weight, 2), axis=0))
            right.append(design)
        return lax.dot_general(
            jnp.concatenate(left, axis=1),
            jnp.concatenate(right, axis=1),
            (((1,), (1,)), ((), ())),
            preferred_element_type=F32,
        )

    if height <= UNROLL:
        product = chunk(0)
        for first in range(rows, height, rows):
            product = product + chunk(first)
    else:
        product = lax.fori_loop(
            0,
            height // rows,
            lambda index, total: total + chunk(index * rows),
            jnp.zeros((2 * size, size), F32),
        )
    return product[0:size] + product[size : 2 * size]


def solve_stage(normal, kernels):
    unknowns = kernels + 1
    width = LANE
    groups = ceil_to(unknowns, SUB) // SUB
    size = normal.shape[1]
    parts = [normal[SUB * g : SUB * (g + 1)] for g in range(groups)]
    if size < width:
        parts = [
            jnp.concatenate([part, jnp.zeros((SUB, width - size), F32)], axis=1)
            for part in parts
        ]

    def pick(value, index, axis):
        where = jnp.full((SUB, width), index, jnp.int32)
        return jnp.take_along_axis(value, where, axis, mode="promise_in_bounds")

    row = lax.broadcasted_iota(jnp.int32, (SUB, width), 0)

    nothing = jnp.zeros((SUB, width), F32)
    straight, across = [nothing] * groups, [nothing] * groups
    edges = [2 * e for e in range(groups // 2)] + [groups]
    for low, high in zip(edges[:-1], edges[1:]):
        members = range(low, high)
        count = ceil_to(min(SUB * high, unknowns) - SUB * low, 2)
        copied = [
            [pick(part, SUB * low + index, 1) for part in parts] for index in range(count)
        ]
        columns = [[one[g] for g in members] for one in copied]
        block = [parts[g] for g in members]
        pivots = []
        for at in range(0, count, 2):
            own, line = at // SUB, at % SUB
            first, second = columns[at], columns[at + 1]
            a, b = pick(first[own], line, 0), pick(second[own], line, 0)
            d = pick(second[own], line + 1, 0)
            inverse = 1.0 / (a * d - b * b)
            a, b, d = a * inverse, b * inverse, d * inverse
            pivots.append((own, line, a, b, d))
            here = (row == line) | (row == line + 1)
            near = [x * d - y * b for x, y in zip(first, second)]
            far = [y * a - x * b for x, y in zip(first, second)]
            near[own] = jnp.where(here, 0.0, near[own])
            far[own] = jnp.where(here, 0.0, far[own])

            def update(value):
                r0, r1 = pick(value[own], line, 0), pick(value[own], line + 1, 0)
                return [v - x * r0 - y * r1 for v, x, y in zip(value, near, far)]

            columns[at + 2 :] = [update(value) for value in columns[at + 2 :]]
            block = update(block)
            group = low + own
            diagonal = jnp.where(row == line + 1, a, straight[group])
            straight[group] = jnp.where(row == line, d, diagonal)
            across[group] = jnp.where(here, b, across[group])
        lines = []
        for own, line, a, b, d in pivots:
            r0, r1 = pick(block[own], line, 0), pick(block[own], line + 1, 0)
            lines += [d * r0 - b * r1, a * r1 - b * r0]
        for group in range(groups):
            if group in members:
                parts[group] = block[group - low]
                continue
            terms = [copied[index][group] * lines[index] for index in range(count)]
            while len(terms) > 1:
                terms = [sum(terms[i : i + 2][1:], terms[i]) for i in range(0, len(terms), 2)]
            parts[group] = parts[group] - terms[0]
    other = row ^ 1
    parts = [
        x * p - y * jnp.take_along_axis(p, other, 0, mode="promise_in_bounds")
        for x, y, p in zip(straight, across, parts)
    ]
    values = [
        pick(p, unknowns, 1) + (pick(p, unknowns + 1, 1) + pick(p, unknowns + 2, 1))
        for p in parts
    ]
    return [jnp.where(row + SUB * g < unknowns, v, 0.0) for g, v in enumerate(values)]


def residual_stage(values, conv_ref, sci_ref, inverse_ref, diff_ref, out_ref, rows_each):
    height, _, width = conv_ref.shape

    def block(index):
        first = index * SUB
        if not isinstance(first, int):
            first = pl.multiple_of(first, SUB)
        lines = []
        for row in range(SUB):
            design = conv_ref[first + row].astype(F32)
            total = design[0:SUB] * values[0]
            for group in range(1, len(values)):
                total = total + design[SUB * group : SUB * (group + 1)] * values[group]
            lines.append(jnp.sum(total, axis=0, keepdims=True))
        model = jnp.concatenate(lines, axis=0)
        here = pl.ds(first, SUB)
        residual = sci_ref[0, here, :] - model
        inverse = inverse_ref[here, :]
        diff_ref[0, here, :] = residual * jnp.sqrt(inverse)
        weighted = residual * inverse
        for start in range(0, SUB, rows_each):
            target = (first + start) // rows_each
            out_ref[target, 0:rows_each, :] = weighted[start : start + rows_each]
            out_ref[target, rows_each : 2 * rows_each, :] = inverse[start : start + rows_each]

    each(height // SUB, block)


def store_coefficients(values, coef_ref, unknowns):
    row = lax.broadcasted_iota(jnp.int32, (SUB, LANE), 0)
    column = lax.broadcasted_iota(jnp.int32, (SUB, LANE), 1)
    total = jnp.zeros((SUB, LANE), F32)
    for group, value in enumerate(values):
        total = total + jnp.where(column == row + SUB * group, value, 0.0)
    coef_ref[...] = jnp.sum(total, axis=0, keepdims=True)[:, 0:unknowns]


def fit(tile, edge, science, variance, col_taps, row_taps, stamp_rows, stamp_cols, rows_each, sky):
    height, width = science.shape[1:]
    tap_count, kernels = col_taps.shape
    unknowns = kernels + 1
    groups = ceil_to(unknowns + 3, SUB) // SUB
    size = ceil_to(unknowns + 3, 2 * SUB)
    tall = ceil_to(kernels, 2 * SUB)
    rows, side = chunk_rows(height)
    local = sky == 1
    vmem = pl.BlockSpec(memory_space=pltpu.VMEM)
    params = pltpu.CompilerParams(vmem_limit_bytes=56 * 1024 * 1024)
    taps = (col_taps, row_taps)

    def result(shape, dtype=F32):
        return pltpu.VMEM(shape, dtype) if local else jax.ShapeDtypeStruct(shape, dtype)

    prepared = [
        ((2, tall, ceil_to(tap_count, SUB)), BF16),
        ((groups, 2, SUB // 2 * rows, SUB // 2 * (rows + 2 * side)), BF16),
        ((height, width), F32),
        ((height, width), F32),
        ((height, SUB, width), F32),
    ]
    pad_shape = pltpu.VMEM((LANE, LANE), F32)
    conv_shape = (height, size, width)
    cols_shape = pltpu.VMEM((groups, 2, SUB // 2 * (height + 2 * side), width), BF16)
    out_shapes = [
        result((1, height, width)),
        result((1, unknowns)),
        result((height // rows_each, 2 * rows_each, width)),
    ]

    def before(sci, var, ct, rt, sr, sc, flipped, band, weight, inverse, tail, pad):
        taps_stage(ct, rt, pad, flipped, band, height)
        weight_stage(sci, var, sr, sc, weight, inverse, tail, kernels)

    def front(tmpl, edges, flipped, band, weight, tail, conv, cols):
        column_stage(tmpl, edges, flipped, cols, height, tap_count)
        row_stage(band, cols, tail, conv)
        return normal_stage(weight, conv, size)

    def back(normal, conv, sci, inverse, diff, coef, out):
        values = solve_stage(normal, kernels)
        residual_stage(values, conv, sci, inverse, diff, out, rows_each)
        store_coefficients(values, coef, unknowns)

    if local:

        def kernel(tmpl, sci, var, ct, rt, sr, sc, diff, coef, out, conv, cols, pad, *tables):
            before(sci, var, ct, rt, sr, sc, *tables, pad)
            flipped, band, weight, inverse, tail = tables
            normal = front(tmpl, None, flipped, band, weight, tail, conv, cols)
            back(normal, conv, sci, inverse, diff, coef, out)

        args = (tile, science, variance) + taps + (stamp_rows, stamp_cols)
        return pl.pallas_call(
            kernel,
            out_shape=out_shapes,
            in_specs=[vmem] * 7,
            out_specs=[vmem] * 3,
            scratch_shapes=[pltpu.VMEM(conv_shape, BF16), cols_shape, pad_shape]
            + [pltpu.VMEM(shape, dtype) for shape, dtype in prepared],
            compiler_params=params,
            name="fit",
        )(*[pltpu.with_memory_space_constraint(arg, pltpu.VMEM) for arg in args])

    flipped, band, weight, inverse, tail = pl.pallas_call(
        before,
        out_shape=[result(shape, dtype) for shape, dtype in prepared],
        in_specs=[vmem] * 6,
        out_specs=[vmem] * 5,
        scratch_shapes=[pad_shape],
        compiler_params=params,
        name="before",
    )(science, variance, *taps, stamp_rows, stamp_cols)

    def first(tmpl, edges, flipped, band, weight, tail, conv, normal, cols):
        normal[...] = front(tmpl, edges, flipped, band, weight, tail, conv, cols)

    conv, normal = pl.pallas_call(
        first,
        out_shape=[result(conv_shape, BF16), result((size, size))],
        in_specs=[vmem] * 6,
        out_specs=[vmem] * 2,
        scratch_shapes=[cols_shape],
        compiler_params=params,
        name="fit_normal",
    )(tile.astype(F32), edge.astype(F32), flipped, band, weight, tail)
    normal = lax.psum(normal, "sky")

    def second(normal, conv, sci, inverse, diff, coef, out):
        back(normal[...], conv, sci, inverse, diff, coef, out)

    return pl.pallas_call(
        second,
        out_shape=out_shapes,
        in_specs=[vmem] * 4,
        out_specs=[vmem] * 3,
        compiler_params=params,
        name="fit_solve",
    )(normal, conv, science, inverse)


def sky_edges(tile, margin, sky):
    ends = sky - 1
    width = tile.shape[1]
    head = tile[:, 0:margin]
    tail = tile[:, width - margin :]
    after = lax.ppermute(head, "sky", [(i + 1, i) for i in range(ends)])
    before = lax.ppermute(tail, "sky", [(i, i + 1) for i in range(ends)])
    middle = jnp.zeros((tile.shape[0], width - 2 * margin), tile.dtype)
    return jnp.concatenate([after, middle, before], axis=1)


def stage_inputs(lines, count, others):
    def kernel(*refs):
        taken, given = refs[: len(refs) // 2], refs[len(refs) // 2 :]
        given[0][...] = jnp.broadcast_to(taken[0][...][None], given[0].shape)
        for source, target in zip(taken[1:], given[1:]):
            target[...] = source[...]

    vmem = pl.BlockSpec(memory_space=pltpu.VMEM)
    return pl.pallas_call(
        kernel,
        out_shape=[pltpu.VMEM((count,) + lines.shape, lines.dtype)]
        + [pltpu.VMEM(other.shape, other.dtype) for other in others],
        in_specs=[vmem] * (1 + len(others)),
        out_specs=[vmem] * (1 + len(others)),
        name="stage_inputs",
    )(lines, *others)


def gather_results(shares, difference, coefficients):
    rows_each = shares.shape[1] // 2

    def kernel(shares_ref, diff_ref, coef_ref, diff_out, coef_out, out_ref):
        diff_out[...] = diff_ref[...]
        coef_out[...] = coef_ref[...]
        total = jnp.sum(shares_ref[...], axis=0)
        out_ref[...] = total[0:rows_each] / jnp.sqrt(total[rows_each:])

    vmem = pl.BlockSpec(memory_space=pltpu.VMEM)
    args = (shares, difference, coefficients)
    return pl.pallas_call(
        kernel,
        out_shape=[
            jax.ShapeDtypeStruct(difference.shape, F32),
            jax.ShapeDtypeStruct(coefficients.shape, F32),
            jax.ShapeDtypeStruct((rows_each, shares.shape[2]), F32),
        ],
        in_specs=[vmem] * 3,
        out_specs=[vmem] * 3,
        name="results",
    )(*[pltpu.with_memory_space_constraint(arg, pltpu.VMEM) for arg in args])


def solution(mesh):
    visits = mesh.shape["visit"]
    sky = mesh.shape["sky"]

    def on_device(template, science, variance, col_taps, row_taps, stamp_rows, stamp_cols):
        rows_each, width = template.shape
        margin = (col_taps.shape[1] - 1) // 2
        others = (science, variance, col_taps.T, row_taps.T, stamp_rows, stamp_cols)
        if sky == 1:
            copies, *rest = stage_inputs(template, visits, others[2:])
            others = others[:2] + tuple(rest)
        else:
            copies = jnp.broadcast_to(template[None], (visits, rows_each, width))
        tile = lax.all_to_all(copies, "visit", 0, 0, tiled=True).reshape(-1, width)
        edge = sky_edges(tile, margin, sky) if sky > 1 else None
        difference, coefficients, shares = fit(tile, edge, *others, rows_each, sky)
        shares = lax.all_to_all(shares, "visit", 0, 0, tiled=True)
        if sky == 1:
            return gather_results(shares, difference, coefficients)
        total = jnp.sum(shares, axis=0)
        detection = total[0:rows_each] / jnp.sqrt(total[rows_each:])
        return difference, coefficients, detection

    in_specs = (
        P(("group", "visit"), "sky"),
        P(("group", "visit"), None, "sky"),
        P(("group", "visit"), None, "sky"),
        P(),
        P(),
        P(("group", "visit"), "sky", None),
        P(("group", "visit"), "sky", None),
    )
    out_specs = (
        P(("group", "visit"), None, "sky"),
        P(("group", "visit"), None),
        P(("group", "visit"), "sky"),
    )
    return jax.shard_map(
        on_device, mesh=mesh, in_specs=in_specs, out_specs=out_specs, check_vma=False
    )
```

```python
import jax
import jax.numpy as jnp
from jax import lax
from jax.experimental import pallas as pl
from jax.experimental.pallas import tpu as pltpu
from jax.sharding import PartitionSpec as P

STAMP = 16
SUB = 8
LANE = 128
UNROLL = 32
CHUNK = 32
F32 = jnp.float32
BF16 = jnp.bfloat16


def ceil_to(value, step):
    return (value + step - 1) // step * step


def each(count, body):
    if count <= UNROLL:
        for index in range(count):
            body(index)
    else:
        lax.fori_loop(0, count, lambda index, carry: (body(index), carry)[1], 0)


def lanes_of(index, width):
    if isinstance(index, int):
        return slice(index * width, (index + 1) * width)
    return pl.ds(pl.multiple_of(index * width, width), width)


def split_bf16(value, pieces):
    out = []
    for piece in range(pieces):
        part = value.astype(BF16)
        out.append(part)
        if piece + 1 < pieces:
            value = value - part.astype(F32)
    return out


def load_taps(taps_ref, pad_ref):
    taps, kernels = taps_ref.shape
    pad_ref[...] = jnp.zeros(pad_ref.shape, F32)
    pad_ref[0:taps, 0:kernels] = taps_ref[...].astype(F32)
    return pad_ref[...].T


def chunk_rows(height):
    rows = min(CHUNK, height)
    return rows, (0 if rows == height else CHUNK // 2)


def halves(shape):
    return (lax.broadcasted_iota(jnp.int32, shape, 0) & (SUB - 1)) < SUB // 2


def turned(value):
    tiles = [value[at : at + SUB] for at in range(0, value.shape[0], SUB)]
    return jnp.concatenate([pltpu.roll(tile, SUB // 2, 0) for tile in tiles], axis=0)


def taps_stage(col_taps_ref, row_taps_ref, pad_ref, flipped_ref, band_ref, height):
    tap_count = col_taps_ref.shape[0]
    margin = (tap_count - 1) // 2
    span = ceil_to(tap_count, SUB)
    groups = band_ref.shape[0]
    rows, side = chunk_rows(height)
    reach = rows + 2 * side
    wide = SUB // 2 * reach
    tall = groups * SUB
    taps = load_taps(col_taps_ref, pad_ref)[0 : flipped_ref.shape[1], 0:span]
    flip = (
        lax.broadcasted_iota(jnp.int32, (span, span), 0)
        + lax.broadcasted_iota(jnp.int32, (span, span), 1)
        == tap_count - 1
    ).astype(BF16)
    reversed_taps = jnp.dot(taps.astype(BF16), flip, preferred_element_type=F32)
    flipped_ref[0] = reversed_taps.astype(BF16)
    flipped_ref[1] = turned(reversed_taps).astype(BF16)
    taps = load_taps(row_taps_ref, pad_ref)[0:tall, 0:span]
    other = turned(taps)
    lower = halves((tall, span))
    tap = lax.broadcasted_iota(jnp.int32, (span, wide), 0)
    lane = lax.broadcasted_iota(jnp.int32, (span, wide), 1)
    sub = lax.broadcasted_iota(jnp.int32, (SUB, wide), 0)
    along = lax.broadcasted_iota(jnp.int32, (SUB, wide), 1)
    own = (sub & (SUB // 2 - 1)) == (along & (SUB // 2 - 1))
    bit = (SUB // 2).bit_length() - 1
    for half in range(2):
        four = jnp.where(lower, taps, other) if half == 0 else jnp.where(lower, other, taps)

        def line_of(index):
            return 2 * (index >> (bit + 1)) + (((index >> bit) & 1) ^ half)

        def base(shift):
            source = line_of(lane) - shift - side + margin
            source = jnp.where(source >= reach, source - reach, source)
            source = jnp.where(source < 0, source + reach, source)
            repeat = jnp.where(source == tap, 1.0, 0.0).astype(BF16)
            return jnp.dot(four.astype(BF16), repeat, preferred_element_type=F32)

        first, second = base(0), base(1)
        place = line_of(along) - line_of(sub) - side
        late = line_of(sub) == 1
        spread = []
        for group in range(groups):
            here = slice(SUB * group, SUB * (group + 1))
            spread.append(jnp.where(own, jnp.where(late, second[here], first[here]), 0.0))

        for index in range(0, rows // 2, 2):
            inside = [
                (place >= 2 * pair - margin) & (place <= 2 * pair + margin)
                for pair in (index, index + 1)
            ]
            for group in range(groups):
                both = [
                    jnp.where(inside[pair], pltpu.roll(spread[group], SUB * (index + pair), 1), 0.0)
                    for pair in range(2)
                ]
                both = jnp.concatenate(both, axis=0).astype(BF16)
                band_ref[group, half, SUB * index : SUB * (index + 2), :] = both


def column_stage(tmpl_ref, edge_ref, flipped_ref, cols_ref, height, tap_count):
    width = tmpl_ref.shape[1]
    margin = (tap_count - 1) // 2
    span = ceil_to(tap_count, SUB)
    groups = cols_ref.shape[0]
    _, side = chunk_rows(height)
    place = lax.broadcasted_iota(jnp.int32, (span, width), 1) + (
        margin - lax.broadcasted_iota(jnp.int32, (span, width), 0)
    )
    inside = (place >= 0) & (place < width)
    lower = halves((SUB, width))
    if side:
        nothing = jnp.zeros((groups, 2, SUB // 2 * side, width), BF16)
        cols_ref[:, :, 0 : SUB // 2 * side, :] = nothing
        cols_ref[:, :, SUB // 2 * (side + height) :, :] = nothing

    def shifted(row):
        line = jnp.broadcast_to(tmpl_ref[pl.ds(row, 1), :].astype(F32), (span, width))
        line = pltpu.roll(line, width - margin, 1, stride=1, stride_axis=0)
        if edge_ref is None:
            return jnp.where(inside, line, 0.0).astype(BF16)
        other = jnp.broadcast_to(edge_ref[pl.ds(row, 1), :].astype(F32), (span, width))
        other = pltpu.roll(other, width - margin, 1, stride=1, stride_axis=0)
        return jnp.where(inside, line, other).astype(BF16)

    def quad(index):
        results = []
        for odd in range(2):
            row = 4 * index + odd
            both = jnp.concatenate([shifted(row), shifted(row + 2)], axis=1)
            results.append(jnp.dot(flipped_ref[odd], both, preferred_element_type=F32))
        start = 2 * SUB * index + SUB // 2 * side
        if not isinstance(start, int):
            start = pl.multiple_of(start, 2 * SUB)
        for group in range(groups):
            even, odd = [value[SUB * group : SUB * (group + 1)] for value in results]
            even, odd = [[v[:, 0:width], v[:, width:]] for v in (even, odd)]
            for half in range(2):
                tiles = [
                    jnp.where(lower, e, o) if half == 0 else jnp.where(lower, o, e)
                    for e, o in zip(even, odd)
                ]
                two = jnp.concatenate(tiles, axis=0)
                cols_ref[group, half, pl.ds(start, 2 * SUB), :] = two.astype(BF16)

    each(height // 4, quad)


def row_stage(band_ref, cols_ref, tail_ref, conv_ref):
    height, _, width = conv_ref.shape
    groups = band_ref.shape[0]
    rows, side = chunk_rows(height)
    lower = halves((SUB, width))

    def chunk(index):
        first = index * rows
        start = SUB // 2 * first
        if not isinstance(start, int):
            start = pl.multiple_of(start, SUB // 2 * rows)
        for group in range(0, groups, 2):
            members = range(group, min(group + 2, groups))
            pairs = [
                [
                    jnp.dot(
                        band_ref[g, half],
                        cols_ref[g, half, pl.ds(start, SUB // 2 * (rows + 2 * side)), :],
                        preferred_element_type=F32,
                    )
                    for half in range(2)
                ]
                for g in members
            ]
            for pair in range(rows // 2):
                here = slice(SUB * pair, SUB * (pair + 1))
                both = []
                for near, far in pairs:
                    even = jnp.where(lower, near[here], far[here])
                    odd = pltpu.roll(jnp.where(lower, far[here], near[here]), SUB // 2, 0)
                    both.append((even, odd))
                for half in range(2):
                    row = first + 2 * pair + half
                    tiles = [one[half] for one in both]
                    if members[-1] == groups - 1:
                        tiles[-1] = tiles[-1] + tail_ref[row]
                    if len(tiles) == 1:
                        tiles.append(jnp.zeros((SUB, width), F32))
                    conv_ref[row, SUB * group : SUB * (group + 2), :] = jnp.concatenate(
                        tiles, axis=0
                    ).astype(BF16)

    each(height // rows, chunk)


def weight_stage(sci_ref, var_ref, rows_ref, cols_ref, weight_ref, inverse_ref, tail_ref, kernels):
    height, width = weight_ref.shape
    stamps = rows_ref.shape[-1]
    sub = lax.broadcasted_iota(jnp.int32, (SUB, width), 0)
    ones = kernels % SUB

    def held(starts_ref, length):
        place = lax.broadcasted_iota(jnp.int32, (length, stamps), 0) - starts_ref[0]
        return jnp.where((place >= 0) & (place < STAMP), 1.0, 0.0).astype(BF16)

    weight_ref[...] = lax.dot_general(
        held(rows_ref, height),
        held(cols_ref, width),
        (((1,), (1,)), ((), ())),
        preferred_element_type=F32,
    )

    def block(index):
        first = index * SUB
        if not isinstance(first, int):
            first = pl.multiple_of(first, SUB)
        here = pl.ds(first, SUB)
        inverse = 1.0 / var_ref[0, here, :]
        inverse_ref[here, :] = inverse
        weight_ref[here, :] = inverse * weight_ref[here, :]
        pieces = [p.astype(F32) for p in split_bf16(sci_ref[0, here, :], 3)]
        for line in range(SUB):
            value = jnp.where(sub == ones, 1.0, 0.0)
            for piece, part in enumerate(pieces):
                spread = jnp.broadcast_to(part[line : line + 1, :], (SUB, width))
                value = jnp.where(sub == ones + 1 + piece, spread, value)
            tail_ref[first + line] = value

    each(height // SUB, block)


def normal_stage(weight_ref, conv_ref, size):
    height, _, width = conv_ref.shape
    rows = 8

    def chunk(first):
        left, right = [], []
        for row in range(rows):
            design = conv_ref[first + row]
            weight = jnp.broadcast_to(weight_ref[pl.ds(first + row, 1), :], (size, width))
            left.append(jnp.concatenate(split_bf16(design.astype(F32) * weight, 2), axis=0))
            right.append(design)
        return lax.dot_general(
            jnp.concatenate(left, axis=1),
            jnp.concatenate(right, axis=1),
            (((1,), (1,)), ((), ())),
            preferred_element_type=F32,
        )

    if height <= UNROLL:
        product = chunk(0)
        for first in range(rows, height, rows):
            product = product + chunk(first)
    else:
        product = lax.fori_loop(
            0,
            height // rows,
            lambda index, total: total + chunk(index * rows),
            jnp.zeros((2 * size, size), F32),
        )
    return product[0:size] + product[size : 2 * size]


def solve_stage(normal, kernels):
    unknowns = kernels + 1
    width = LANE
    groups = ceil_to(unknowns, SUB) // SUB
    size = normal.shape[1]
    parts = [normal[SUB * g : SUB * (g + 1)] for g in range(groups)]
    if size < width:
        parts = [
            jnp.concatenate([part, jnp.zeros((SUB, width - size), F32)], axis=1)
            for part in parts
        ]

    def pick(value, index, axis):
        where = jnp.full((SUB, width), index, jnp.int32)
        return jnp.take_along_axis(value, where, axis, mode="promise_in_bounds")

    row = lax.broadcasted_iota(jnp.int32, (SUB, width), 0)

    nothing = jnp.zeros((SUB, width), F32)
    straight, across = [nothing] * groups, [nothing] * groups
    edges = [2 * e for e in range(groups // 2)] + [groups]
    for low, high in zip(edges[:-1], edges[1:]):
        members = range(low, high)
        count = ceil_to(min(SUB * high, unknowns) - SUB * low, 2)
        copied = [
            [pick(part, SUB * low + index, 1) for part in parts] for index in range(count)
        ]
        columns = [[one[g] for g in members] for one in copied]
        block = [parts[g] for g in members]
        pivots = []
        for at in range(0, count, 2):
            own, line = at // SUB, at % SUB
            first, second = columns[at], columns[at + 1]
            a, b = pick(first[own], line, 0), pick(second[own], line, 0)
            d = pick(second[own], line + 1, 0)
            inverse = 1.0 / (a * d - b * b)
            a, b, d = a * inverse, b * inverse, d * inverse
            pivots.append((own, line, a, b, d))
            here = (row == line) | (row == line + 1)
            near = [x * d - y * b for x, y in zip(first, second)]
            far = [y * a - x * b for x, y in zip(first, second)]
            near[own] = jnp.where(here, 0.0, near[own])
            far[own] = jnp.where(here, 0.0, far[own])

            def update(value):
                r0, r1 = pick(value[own], line, 0), pick(value[own], line + 1, 0)
                return [v - x * r0 - y * r1 for v, x, y in zip(value, near, far)]

            columns[at + 2 :] = [update(value) for value in columns[at + 2 :]]
            block = update(block)
            group = low + own
            diagonal = jnp.where(row == line + 1, a, straight[group])
            straight[group] = jnp.where(row == line, d, diagonal)
            across[group] = jnp.where(here, b, across[group])
        lines = []
        for own, line, a, b, d in pivots:
            r0, r1 = pick(block[own], line, 0), pick(block[own], line + 1, 0)
            lines += [d * r0 - b * r1, a * r1 - b * r0]
        for group in range(groups):
            if group in members:
                parts[group] = block[group - low]
                continue
            terms = [copied[index][group] * lines[index] for index in range(count)]
            while len(terms) > 1:
                terms = [sum(terms[i : i + 2][1:], terms[i]) for i in range(0, len(terms), 2)]
            parts[group] = parts[group] - terms[0]
    other = row ^ 1
    parts = [
        x * p - y * jnp.take_along_axis(p, other, 0, mode="promise_in_bounds")
        for x, y, p in zip(straight, across, parts)
    ]
    values = [
        pick(p, unknowns, 1) + (pick(p, unknowns + 1, 1) + pick(p, unknowns + 2, 1))
        for p in parts
    ]
    return [jnp.where(row + SUB * g < unknowns, v, 0.0) for g, v in enumerate(values)]


def residual_stage(values, conv_ref, sci_ref, inverse_ref, diff_ref, out_ref, rows_each):
    height, _, width = conv_ref.shape

    def block(index):
        first = index * SUB
        if not isinstance(first, int):
            first = pl.multiple_of(first, SUB)
        lines = []
        for row in range(SUB):
            design = conv_ref[first + row].astype(F32)
            total = design[0:SUB] * values[0]
            for group in range(1, len(values)):
                total = total + design[SUB * group : SUB * (group + 1)] * values[group]
            lines.append(jnp.sum(total, axis=0, keepdims=True))
        model = jnp.concatenate(lines, axis=0)
        here = pl.ds(first, SUB)
        residual = sci_ref[0, here, :] - model
        inverse = inverse_ref[here, :]
        diff_ref[0, here, :] = residual * jnp.sqrt(inverse)
        weighted = residual * inverse
        for start in range(0, SUB, rows_each):
            target = (first + start) // rows_each
            out_ref[target, 0:rows_each, :] = weighted[start : start + rows_each]
            out_ref[target, rows_each : 2 * rows_each, :] = inverse[start : start + rows_each]

    each(height // SUB, block)


def store_coefficients(values, coef_ref, unknowns):
    row = lax.broadcasted_iota(jnp.int32, (SUB, LANE), 0)
    column = lax.broadcasted_iota(jnp.int32, (SUB, LANE), 1)
    total = jnp.zeros((SUB, LANE), F32)
    for group, value in enumerate(values):
        total = total + jnp.where(column == row + SUB * group, value, 0.0)
    coef_ref[...] = jnp.sum(total, axis=0, keepdims=True)[:, 0:unknowns]


def fit(tile, edge, science, variance, col_taps, row_taps, stamp_rows, stamp_cols, rows_each, sky):
    height, width = science.shape[1:]
    tap_count, kernels = col_taps.shape
    unknowns = kernels + 1
    groups = ceil_to(unknowns + 3, SUB) // SUB
    size = ceil_to(unknowns + 3, 2 * SUB)
    tall = ceil_to(kernels, 2 * SUB)
    rows, side = chunk_rows(height)
    local = sky == 1
    vmem = pl.BlockSpec(memory_space=pltpu.VMEM)
    params = pltpu.CompilerParams(vmem_limit_bytes=56 * 1024 * 1024)
    taps = (col_taps, row_taps)

    def result(shape, dtype=F32):
        return pltpu.VMEM(shape, dtype) if local else jax.ShapeDtypeStruct(shape, dtype)

    prepared = [
        ((2, tall, ceil_to(tap_count, SUB)), BF16),
        ((groups, 2, SUB // 2 * rows, SUB // 2 * (rows + 2 * side)), BF16),
        ((height, width), F32),
        ((height, width), F32),
        ((height, SUB, width), F32),
    ]
    pad_shape = pltpu.VMEM((LANE, LANE), F32)
    conv_shape = (height, size, width)
    cols_shape = pltpu.VMEM((groups, 2, SUB // 2 * (height + 2 * side), width), BF16)
    out_shapes = [
        result((1, height, width)),
        result((1, unknowns)),
        result((height // rows_each, 2 * rows_each, width)),
    ]

    def before(sci, var, ct, rt, sr, sc, flipped, band, weight, inverse, tail, pad):
        taps_stage(ct, rt, pad, flipped, band, height)
        weight_stage(sci, var, sr, sc, weight, inverse, tail, kernels)

    def front(tmpl, edges, flipped, band, weight, tail, conv, cols):
        column_stage(tmpl, edges, flipped, cols, height, tap_count)
        row_stage(band, cols, tail, conv)
        return normal_stage(weight, conv, size)

    def back(normal, conv, sci, inverse, diff, coef, out):
        values = solve_stage(normal, kernels)
        residual_stage(values, conv, sci, inverse, diff, out, rows_each)
        store_coefficients(values, coef, unknowns)

    if local:

        def kernel(tmpl, sci, var, ct, rt, sr, sc, diff, coef, out, conv, cols, pad, *tables):
            before(sci, var, ct, rt, sr, sc, *tables, pad)
            flipped, band, weight, inverse, tail = tables
            normal = front(tmpl, None, flipped, band, weight, tail, conv, cols)
            back(normal, conv, sci, inverse, diff, coef, out)

        args = (tile, science, variance) + taps + (stamp_rows, stamp_cols)
        return pl.pallas_call(
            kernel,
            out_shape=out_shapes,
            in_specs=[vmem] * 7,
            out_specs=[vmem] * 3,
            scratch_shapes=[pltpu.VMEM(conv_shape, BF16), cols_shape, pad_shape]
            + [pltpu.VMEM(shape, dtype) for shape, dtype in prepared],
            compiler_params=params,
            name="fit",
        )(*[pltpu.with_memory_space_constraint(arg, pltpu.VMEM) for arg in args])

    flipped, band, weight, inverse, tail = pl.pallas_call(
        before,
        out_shape=[result(shape, dtype) for shape, dtype in prepared],
        in_specs=[vmem] * 6,
        out_specs=[vmem] * 5,
        scratch_shapes=[pad_shape],
        compiler_params=params,
        name="before",
    )(science, variance, *taps, stamp_rows, stamp_cols)

    def first(tmpl, edges, flipped, band, weight, tail, conv, normal, cols):
        normal[...] = front(tmpl, edges, flipped, band, weight, tail, conv, cols)

    conv, normal = pl.pallas_call(
        first,
        out_shape=[result(conv_shape, BF16), result((size, size))],
        in_specs=[vmem] * 6,
        out_specs=[vmem] * 2,
        scratch_shapes=[cols_shape],
        compiler_params=params,
        name="fit_normal",
    )(tile.astype(F32), edge.astype(F32), flipped, band, weight, tail)
    normal = lax.psum(normal, "sky")

    def second(normal, conv, sci, inverse, diff, coef, out):
        back(normal[...], conv, sci, inverse, diff, coef, out)

    return pl.pallas_call(
        second,
        out_shape=out_shapes,
        in_specs=[vmem] * 4,
        out_specs=[vmem] * 3,
        compiler_params=params,
        name="fit_solve",
    )(normal, conv, science, inverse)


def sky_edges(tile, margin, sky):
    ends = sky - 1
    width = tile.shape[1]
    head = tile[:, 0:margin]
    tail = tile[:, width - margin :]
    after = lax.ppermute(head, "sky", [(i + 1, i) for i in range(ends)])
    before = lax.ppermute(tail, "sky", [(i, i + 1) for i in range(ends)])
    middle = jnp.zeros((tile.shape[0], width - 2 * margin), tile.dtype)
    return jnp.concatenate([after, middle, before], axis=1)


def stage_inputs(lines, count, others):
    def kernel(*refs):
        taken, given = refs[: len(refs) // 2], refs[len(refs) // 2 :]
        given[0][...] = jnp.broadcast_to(taken[0][...][None], given[0].shape)
        for source, target in zip(taken[1:], given[1:]):
            target[...] = source[...]

    vmem = pl.BlockSpec(memory_space=pltpu.VMEM)
    return pl.pallas_call(
        kernel,
        out_shape=[pltpu.VMEM((count,) + lines.shape, lines.dtype)]
        + [pltpu.VMEM(other.shape, other.dtype) for other in others],
        in_specs=[vmem] * (1 + len(others)),
        out_specs=[vmem] * (1 + len(others)),
        name="stage_inputs",
    )(lines, *others)


def gather_results(shares, difference, coefficients):
    rows_each = shares.shape[1] // 2

    def kernel(shares_ref, diff_ref, coef_ref, diff_out, coef_out, out_ref):
        diff_out[...] = diff_ref[...]
        coef_out[...] = coef_ref[...]
        total = jnp.sum(shares_ref[...], axis=0)
        out_ref[...] = total[0:rows_each] / jnp.sqrt(total[rows_each:])

    vmem = pl.BlockSpec(memory_space=pltpu.VMEM)
    args = (shares, difference, coefficients)
    return pl.pallas_call(
        kernel,
        out_shape=[
            jax.ShapeDtypeStruct(difference.shape, F32),
            jax.ShapeDtypeStruct(coefficients.shape, F32),
            jax.ShapeDtypeStruct((rows_each, shares.shape[2]), F32),
        ],
        in_specs=[vmem] * 3,
        out_specs=[vmem] * 3,
        name="results",
    )(*[pltpu.with_memory_space_constraint(arg, pltpu.VMEM) for arg in args])


def solution(mesh):
    visits = mesh.shape["visit"]
    sky = mesh.shape["sky"]

    def on_device(template, science, variance, col_taps, row_taps, stamp_rows, stamp_cols):
        rows_each, width = template.shape
        margin = (col_taps.shape[1] - 1) // 2
        others = (science, variance, col_taps.T, row_taps.T, stamp_rows, stamp_cols)
        if sky == 1:
            copies, *rest = stage_inputs(template, visits, others[2:])
            others = others[:2] + tuple(rest)
        else:
            copies = jnp.broadcast_to(template[None], (visits, rows_each, width))
        tile = lax.all_to_all(copies, "visit", 0, 0, tiled=True).reshape(-1, width)
        edge = sky_edges(tile, margin, sky) if sky > 1 else None
        difference, coefficients, shares = fit(tile, edge, *others, rows_each, sky)
        shares = lax.all_to_all(shares, "visit", 0, 0, tiled=True)
        if sky == 1:
            return gather_results(shares, difference, coefficients)
        total = jnp.sum(shares, axis=0)
        detection = total[0:rows_each] / jnp.sqrt(total[rows_each:])
        return difference, coefficients, detection

    in_specs = (
        P(("group", "visit"), "sky"),
        P(("group", "visit"), None, "sky"),
        P(("group", "visit"), None, "sky"),
        P(),
        P(),
        P(("group", "visit"), "sky", None),
        P(("group", "visit"), "sky", None),
    )
    out_specs = (
        P(("group", "visit"), None, "sky"),
        P(("group", "visit"), None),
        P(("group", "visit"), "sky"),
    )
    return jax.shard_map(
        on_device, mesh=mesh, in_specs=in_specs, out_specs=out_specs, check_vma=False
    )
```

```python
import jax
import jax.numpy as jnp
from jax import lax
from jax.experimental import pallas as pl
from jax.experimental.pallas import tpu as pltpu
from jax.sharding import PartitionSpec as P

STAMP = 16
SUB = 8
LANE = 128
UNROLL = 32
CHUNK = 32
F32 = jnp.float32
BF16 = jnp.bfloat16


def ceil_to(value, step):
    return (value + step - 1) // step * step


def each(count, body):
    if count <= UNROLL:
        for index in range(count):
            body(index)
    else:
        lax.fori_loop(0, count, lambda index, carry: (body(index), carry)[1], 0)


def lanes_of(index, width):
    if isinstance(index, int):
        return slice(index * width, (index + 1) * width)
    return pl.ds(pl.multiple_of(index * width, width), width)


def split_bf16(value, pieces):
    out = []
    for piece in range(pieces):
        part = value.astype(BF16)
        out.append(part)
        if piece + 1 < pieces:
            value = value - part.astype(F32)
    return out


def load_taps(taps_ref, pad_ref):
    taps, kernels = taps_ref.shape
    pad_ref[...] = jnp.zeros(pad_ref.shape, F32)
    pad_ref[0:taps, 0:kernels] = taps_ref[...].astype(F32)
    return pad_ref[...].T


def chunk_rows(height):
    rows = min(CHUNK, height)
    return rows, (0 if rows == height else CHUNK // 2)


def halves(shape):
    return (lax.broadcasted_iota(jnp.int32, shape, 0) & (SUB - 1)) < SUB // 2


def turned(value):
    tiles = [value[at : at + SUB] for at in range(0, value.shape[0], SUB)]
    return jnp.concatenate([pltpu.roll(tile, SUB // 2, 0) for tile in tiles], axis=0)


def taps_stage(col_taps_ref, row_taps_ref, pad_ref, flipped_ref, band_ref, height):
    tap_count = col_taps_ref.shape[0]
    margin = (tap_count - 1) // 2
    span = ceil_to(tap_count, SUB)
    groups = band_ref.shape[0]
    rows, side = chunk_rows(height)
    reach = rows + 2 * side
    wide = SUB // 2 * reach
    tall = groups * SUB
    taps = load_taps(col_taps_ref, pad_ref)[0 : flipped_ref.shape[1], 0:span]
    flip = (
        lax.broadcasted_iota(jnp.int32, (span, span), 0)
        + lax.broadcasted_iota(jnp.int32, (span, span), 1)
        == tap_count - 1
    ).astype(BF16)
    reversed_taps = jnp.dot(taps.astype(BF16), flip, preferred_element_type=F32)
    flipped_ref[0] = reversed_taps.astype(BF16)
    flipped_ref[1] = turned(reversed_taps).astype(BF16)
    taps = load_taps(row_taps_ref, pad_ref)[0:tall, 0:span]
    other = turned(taps)
    lower = halves((tall, span))
    tap = lax.broadcasted_iota(jnp.int32, (span, wide), 0)
    lane = lax.broadcasted_iota(jnp.int32, (span, wide), 1)
    sub = lax.broadcasted_iota(jnp.int32, (SUB, wide), 0)
    along = lax.broadcasted_iota(jnp.int32, (SUB, wide), 1)
    own = (sub & (SUB // 2 - 1)) == (along & (SUB // 2 - 1))
    bit = (SUB // 2).bit_length() - 1
    for half in range(2):
        four = jnp.where(lower, taps, other) if half == 0 else jnp.where(lower, other, taps)

        def line_of(index):
            return 2 * (index >> (bit + 1)) + (((index >> bit) & 1) ^ half)

        def base(shift):
            source = line_of(lane) - shift - side + margin
            source = jnp.where(source >= reach, source - reach, source)
            source = jnp.where(source < 0, source + reach, source)
            repeat = jnp.where(source == tap, 1.0, 0.0).astype(BF16)
            return jnp.dot(four.astype(BF16), repeat, preferred_element_type=F32)

        first, second = base(0), base(1)
        place = line_of(along) - line_of(sub) - side
        late = line_of(sub) == 1
        spread = []
        for group in range(groups):
            here = slice(SUB * group, SUB * (group + 1))
            spread.append(jnp.where(own, jnp.where(late, second[here], first[here]), 0.0))

        for index in range(0, rows // 2, 2):
            inside = [
                (place >= 2 * pair - margin) & (place <= 2 * pair + margin)
                for pair in (index, index + 1)
            ]
            for group in range(groups):
                both = [
                    jnp.where(inside[pair], pltpu.roll(spread[group], SUB * (index + pair), 1), 0.0)
                    for pair in range(2)
                ]
                both = jnp.concatenate(both, axis=0).astype(BF16)
                band_ref[group, half, SUB * index : SUB * (index + 2), :] = both


def column_stage(tmpl_ref, edge_ref, flipped_ref, cols_ref, height, tap_count):
    width = tmpl_ref.shape[1]
    margin = (tap_count - 1) // 2
    span = ceil_to(tap_count, SUB)
    groups = cols_ref.shape[0]
    _, side = chunk_rows(height)
    place = lax.broadcasted_iota(jnp.int32, (span, width), 1) + (
        margin - lax.broadcasted_iota(jnp.int32, (span, width), 0)
    )
    inside = (place >= 0) & (place < width)
    lower = halves((SUB, width))
    if side:
        nothing = jnp.zeros((groups, 2, SUB // 2 * side, width), BF16)
        cols_ref[:, :, 0 : SUB // 2 * side, :] = nothing
        cols_ref[:, :, SUB // 2 * (side + height) :, :] = nothing

    def shifted(row):
        line = jnp.broadcast_to(tmpl_ref[pl.ds(row, 1), :].astype(F32), (span, width))
        line = pltpu.roll(line, width - margin, 1, stride=1, stride_axis=0)
        if edge_ref is None:
            return jnp.where(inside, line, 0.0).astype(BF16)
        other = jnp.broadcast_to(edge_ref[pl.ds(row, 1), :].astype(F32), (span, width))
        other = pltpu.roll(other, width - margin, 1, stride=1, stride_axis=0)
        return jnp.where(inside, line, other).astype(BF16)

    def quad(index):
        results = []
        for odd in range(2):
            row = 4 * index + odd
            both = jnp.concatenate([shifted(row), shifted(row + 2)], axis=1)
            results.append(jnp.dot(flipped_ref[odd], both, preferred_element_type=F32))
        start = 2 * SUB * index + SUB // 2 * side
        if not isinstance(start, int):
            start = pl.multiple_of(start, 2 * SUB)
        for group in range(groups):
            even, odd = [value[SUB * group : SUB * (group + 1)] for value in results]
            even, odd = [[v[:, 0:width], v[:, width:]] for v in (even, odd)]
            for half in range(2):
                tiles = [
                    jnp.where(lower, e, o) if half == 0 else jnp.where(lower, o, e)
                    for e, o in zip(even, odd)
                ]
                two = jnp.concatenate(tiles, axis=0)
                cols_ref[group, half, pl.ds(start, 2 * SUB), :] = two.astype(BF16)

    each(height // 4, quad)


def row_stage(band_ref, cols_ref, tail_ref, conv_ref):
    height, _, width = conv_ref.shape
    groups = band_ref.shape[0]
    rows, side = chunk_rows(height)
    lower = halves((SUB, width))

    def chunk(index):
        first = index * rows
        start = SUB // 2 * first
        if not isinstance(start, int):
            start = pl.multiple_of(start, SUB // 2 * rows)
        for group in range(0, groups, 2):
            members = range(group, min(group + 2, groups))
            pairs = [
                [
                    jnp.dot(
                        band_ref[g, half],
                        cols_ref[g, half, pl.ds(start, SUB // 2 * (rows + 2 * side)), :],
                        preferred_element_type=F32,
                    )
                    for half in range(2)
                ]
                for g in members
            ]
            for pair in range(rows // 2):
                here = slice(SUB * pair, SUB * (pair + 1))
                both = []
                for near, far in pairs:
                    even = jnp.where(lower, near[here], far[here])
                    odd = pltpu.roll(jnp.where(lower, far[here], near[here]), SUB // 2, 0)
                    both.append((even, odd))
                for half in range(2):
                    row = first + 2 * pair + half
                    tiles = [one[half] for one in both]
                    if members[-1] == groups - 1:
                        tiles[-1] = tiles[-1] + tail_ref[row]
                    if len(tiles) == 1:
                        tiles.append(jnp.zeros((SUB, width), F32))
                    conv_ref[row, SUB * group : SUB * (group + 2), :] = jnp.concatenate(
                        tiles, axis=0
                    ).astype(BF16)

    each(height // rows, chunk)


def weight_stage(sci_ref, var_ref, rows_ref, cols_ref, weight_ref, inverse_ref, tail_ref, kernels):
    height, width = weight_ref.shape
    stamps = rows_ref.shape[-1]
    sub = lax.broadcasted_iota(jnp.int32, (SUB, width), 0)
    ones = kernels % SUB

    def held(starts_ref, length):
        place = lax.broadcasted_iota(jnp.int32, (length, stamps), 0) - starts_ref[0]
        return jnp.where((place >= 0) & (place < STAMP), 1.0, 0.0).astype(BF16)

    weight_ref[...] = lax.dot_general(
        held(rows_ref, height),
        held(cols_ref, width),
        (((1,), (1,)), ((), ())),
        preferred_element_type=F32,
    )

    def block(index):
        first = index * SUB
        if not isinstance(first, int):
            first = pl.multiple_of(first, SUB)
        here = pl.ds(first, SUB)
        inverse = 1.0 / var_ref[0, here, :]
        inverse_ref[here, :] = inverse
        weight_ref[here, :] = inverse * weight_ref[here, :]
        pieces = [p.astype(F32) for p in split_bf16(sci_ref[0, here, :], 3)]
        for line in range(SUB):
            value = jnp.where(sub == ones, 1.0, 0.0)
            for piece, part in enumerate(pieces):
                spread = jnp.broadcast_to(part[line : line + 1, :], (SUB, width))
                value = jnp.where(sub == ones + 1 + piece, spread, value)
            tail_ref[first + line] = value

    each(height // SUB, block)


def normal_stage(weight_ref, conv_ref, size):
    height, _, width = conv_ref.shape
    rows = 8

    def chunk(first):
        left, right = [], []
        for row in range(rows):
            design = conv_ref[first + row]
            weight = jnp.broadcast_to(weight_ref[pl.ds(first + row, 1), :], (size, width))
            left.append(jnp.concatenate(split_bf16(design.astype(F32) * weight, 2), axis=0))
            right.append(design)
        return lax.dot_general(
            jnp.concatenate(left, axis=1),
            jnp.concatenate(right, axis=1),
            (((1,), (1,)), ((), ())),
            preferred_element_type=F32,
        )

    if height <= UNROLL:
        product = chunk(0)
        for first in range(rows, height, rows):
            product = product + chunk(first)
    else:
        product = lax.fori_loop(
            0,
            height // rows,
            lambda index, total: total + chunk(index * rows),
            jnp.zeros((2 * size, size), F32),
        )
    return product[0:size] + product[size : 2 * size]


def solve_stage(normal, kernels):
    unknowns = kernels + 1
    width = LANE
    groups = ceil_to(unknowns, SUB) // SUB
    size = normal.shape[1]
    parts = [normal[SUB * g : SUB * (g + 1)] for g in range(groups)]
    if size < width:
        parts = [
            jnp.concatenate([part, jnp.zeros((SUB, width - size), F32)], axis=1)
            for part in parts
        ]

    def pick(value, index, axis):
        where = jnp.full((SUB, width), index, jnp.int32)
        return jnp.take_along_axis(value, where, axis, mode="promise_in_bounds")

    row = lax.broadcasted_iota(jnp.int32, (SUB, width), 0)

    nothing = jnp.zeros((SUB, width), F32)
    straight, across = [nothing] * groups, [nothing] * groups
    edges = [0] + list(range(2 - groups % 2, groups + 1, 2))
    for low, high in zip(edges[:-1], edges[1:]):
        members = range(low, high)
        count = ceil_to(min(SUB * high, unknowns) - SUB * low, 2)
        copied = [
            [pick(part, SUB * low + index, 1) for part in parts] for index in range(count)
        ]
        columns = [[one[g] for g in members] for one in copied]
        block = [parts[g] for g in members]
        pivots = []
        for at in range(0, count, 2):
            own, line = at // SUB, at % SUB
            first, second = columns[at], columns[at + 1]
            a, b = pick(first[own], line, 0), pick(second[own], line, 0)
            d = pick(second[own], line + 1, 0)
            inverse = 1.0 / (a * d - b * b)
            a, b, d = a * inverse, b * inverse, d * inverse
            pivots.append((own, line, a, b, d))
            here = (row == line) | (row == line + 1)
            near = [x * d - y * b for x, y in zip(first, second)]
            far = [y * a - x * b for x, y in zip(first, second)]
            near[own] = jnp.where(here, 0.0, near[own])
            far[own] = jnp.where(here, 0.0, far[own])

            def update(value):
                r0, r1 = pick(value[own], line, 0), pick(value[own], line + 1, 0)
                return [v - x * r0 - y * r1 for v, x, y in zip(value, near, far)]

            columns[at + 2 :] = [update(value) for value in columns[at + 2 :]]
            block = update(block)
            group = low + own
            diagonal = jnp.where(row == line + 1, a, straight[group])
            straight[group] = jnp.where(row == line, d, diagonal)
            across[group] = jnp.where(here, b, across[group])
        lines = []
        for own, line, a, b, d in pivots:
            r0, r1 = pick(block[own], line, 0), pick(block[own], line + 1, 0)
            lines += [d * r0 - b * r1, a * r1 - b * r0]
        for group in range(groups):
            if group in members:
                parts[group] = block[group - low]
                continue
            terms = [copied[index][group] * lines[index] for index in range(count)]
            while len(terms) > 1:
                terms = [sum(terms[i : i + 2][1:], terms[i]) for i in range(0, len(terms), 2)]
            parts[group] = parts[group] - terms[0]
    other = row ^ 1
    parts = [
        x * p - y * jnp.take_along_axis(p, other, 0, mode="promise_in_bounds")
        for x, y, p in zip(straight, across, parts)
    ]
    values = [
        pick(p, unknowns, 1) + (pick(p, unknowns + 1, 1) + pick(p, unknowns + 2, 1))
        for p in parts
    ]
    return [jnp.where(row + SUB * g < unknowns, v, 0.0) for g, v in enumerate(values)]


def residual_stage(values, conv_ref, sci_ref, inverse_ref, diff_ref, out_ref, rows_each):
    height, _, width = conv_ref.shape

    def block(index):
        first = index * SUB
        if not isinstance(first, int):
            first = pl.multiple_of(first, SUB)
        lines = []
        for row in range(SUB):
            design = conv_ref[first + row].astype(F32)
            total = design[0:SUB] * values[0]
            for group in range(1, len(values)):
                total = total + design[SUB * group : SUB * (group + 1)] * values[group]
            lines.append(jnp.sum(total, axis=0, keepdims=True))
        model = jnp.concatenate(lines, axis=0)
        here = pl.ds(first, SUB)
        residual = sci_ref[0, here, :] - model
        inverse = inverse_ref[here, :]
        diff_ref[0, here, :] = residual * jnp.sqrt(inverse)
        weighted = residual * inverse
        for start in range(0, SUB, rows_each):
            target = (first + start) // rows_each
            out_ref[target, 0:rows_each, :] = weighted[start : start + rows_each]
            out_ref[target, rows_each : 2 * rows_each, :] = inverse[start : start + rows_each]

    each(height // SUB, block)


def store_coefficients(values, coef_ref, unknowns):
    row = lax.broadcasted_iota(jnp.int32, (SUB, LANE), 0)
    column = lax.broadcasted_iota(jnp.int32, (SUB, LANE), 1)
    total = jnp.zeros((SUB, LANE), F32)
    for group, value in enumerate(values):
        total = total + jnp.where(column == row + SUB * group, value, 0.0)
    coef_ref[...] = jnp.sum(total, axis=0, keepdims=True)[:, 0:unknowns]


def fit(tile, edge, science, variance, col_taps, row_taps, stamp_rows, stamp_cols, rows_each, sky):
    height, width = science.shape[1:]
    tap_count, kernels = col_taps.shape
    unknowns = kernels + 1
    groups = ceil_to(unknowns + 3, SUB) // SUB
    size = ceil_to(unknowns + 3, 2 * SUB)
    tall = ceil_to(kernels, 2 * SUB)
    rows, side = chunk_rows(height)
    local = sky == 1
    vmem = pl.BlockSpec(memory_space=pltpu.VMEM)
    params = pltpu.CompilerParams(vmem_limit_bytes=56 * 1024 * 1024)
    taps = (col_taps, row_taps)

    def result(shape, dtype=F32):
        return pltpu.VMEM(shape, dtype) if local else jax.ShapeDtypeStruct(shape, dtype)

    prepared = [
        ((2, tall, ceil_to(tap_count, SUB)), BF16),
        ((groups, 2, SUB // 2 * rows, SUB // 2 * (rows + 2 * side)), BF16),
        ((height, width), F32),
        ((height, width), F32),
        ((height, SUB, width), F32),
    ]
    pad_shape = pltpu.VMEM((LANE, LANE), F32)
    conv_shape = (height, size, width)
    cols_shape = pltpu.VMEM((groups, 2, SUB // 2 * (height + 2 * side), width), BF16)
    out_shapes = [
        result((1, height, width)),
        result((1, unknowns)),
        result((height // rows_each, 2 * rows_each, width)),
    ]

    def before(sci, var, ct, rt, sr, sc, flipped, band, weight, inverse, tail, pad):
        taps_stage(ct, rt, pad, flipped, band, height)
        weight_stage(sci, var, sr, sc, weight, inverse, tail, kernels)

    def front(tmpl, edges, flipped, band, weight, tail, conv, cols):
        column_stage(tmpl, edges, flipped, cols, height, tap_count)
        row_stage(band, cols, tail, conv)
        return normal_stage(weight, conv, size)

    def back(normal, conv, sci, inverse, diff, coef, out):
        values = solve_stage(normal, kernels)
        residual_stage(values, conv, sci, inverse, diff, out, rows_each)
        store_coefficients(values, coef, unknowns)

    if local:

        def kernel(tmpl, sci, var, ct, rt, sr, sc, diff, coef, out, conv, cols, pad, *tables):
            before(sci, var, ct, rt, sr, sc, *tables, pad)
            flipped, band, weight, inverse, tail = tables
            normal = front(tmpl, None, flipped, band, weight, tail, conv, cols)
            back(normal, conv, sci, inverse, diff, coef, out)

        args = (tile, science, variance) + taps + (stamp_rows, stamp_cols)
        return pl.pallas_call(
            kernel,
            out_shape=out_shapes,
            in_specs=[vmem] * 7,
            out_specs=[vmem] * 3,
            scratch_shapes=[pltpu.VMEM(conv_shape, BF16), cols_shape, pad_shape]
            + [pltpu.VMEM(shape, dtype) for shape, dtype in prepared],
            compiler_params=params,
            name="fit",
        )(*[pltpu.with_memory_space_constraint(arg, pltpu.VMEM) for arg in args])

    flipped, band, weight, inverse, tail = pl.pallas_call(
        before,
        out_shape=[result(shape, dtype) for shape, dtype in prepared],
        in_specs=[vmem] * 6,
        out_specs=[vmem] * 5,
        scratch_shapes=[pad_shape],
        compiler_params=params,
        name="before",
    )(science, variance, *taps, stamp_rows, stamp_cols)

    def first(tmpl, edges, flipped, band, weight, tail, conv, normal, cols):
        normal[...] = front(tmpl, edges, flipped, band, weight, tail, conv, cols)

    conv, normal = pl.pallas_call(
        first,
        out_shape=[result(conv_shape, BF16), result((size, size))],
        in_specs=[vmem] * 6,
        out_specs=[vmem] * 2,
        scratch_shapes=[cols_shape],
        compiler_params=params,
        name="fit_normal",
    )(tile.astype(F32), edge.astype(F32), flipped, band, weight, tail)
    normal = lax.psum(normal, "sky")

    def second(normal, conv, sci, inverse, diff, coef, out):
        back(normal[...], conv, sci, inverse, diff, coef, out)

    return pl.pallas_call(
        second,
        out_shape=out_shapes,
        in_specs=[vmem] * 4,
        out_specs=[vmem] * 3,
        compiler_params=params,
        name="fit_solve",
    )(normal, conv, science, inverse)


def sky_edges(tile, margin, sky):
    ends = sky - 1
    width = tile.shape[1]
    head = tile[:, 0:margin]
    tail = tile[:, width - margin :]
    after = lax.ppermute(head, "sky", [(i + 1, i) for i in range(ends)])
    before = lax.ppermute(tail, "sky", [(i, i + 1) for i in range(ends)])
    middle = jnp.zeros((tile.shape[0], width - 2 * margin), tile.dtype)
    return jnp.concatenate([after, middle, before], axis=1)


def stage_inputs(lines, count, others):
    def kernel(*refs):
        taken, given = refs[: len(refs) // 2], refs[len(refs) // 2 :]
        given[0][...] = jnp.broadcast_to(taken[0][...][None], given[0].shape)
        for source, target in zip(taken[1:], given[1:]):
            target[...] = source[...]

    vmem = pl.BlockSpec(memory_space=pltpu.VMEM)
    return pl.pallas_call(
        kernel,
        out_shape=[pltpu.VMEM((count,) + lines.shape, lines.dtype)]
        + [pltpu.VMEM(other.shape, other.dtype) for other in others],
        in_specs=[vmem] * (1 + len(others)),
        out_specs=[vmem] * (1 + len(others)),
        name="stage_inputs",
    )(lines, *others)


def gather_results(shares, difference, coefficients):
    rows_each = shares.shape[1] // 2

    def kernel(shares_ref, diff_ref, coef_ref, diff_out, coef_out, out_ref):
        diff_out[...] = diff_ref[...]
        coef_out[...] = coef_ref[...]
        total = jnp.sum(shares_ref[...], axis=0)
        out_ref[...] = total[0:rows_each] / jnp.sqrt(total[rows_each:])

    vmem = pl.BlockSpec(memory_space=pltpu.VMEM)
    args = (shares, difference, coefficients)
    return pl.pallas_call(
        kernel,
        out_shape=[
            jax.ShapeDtypeStruct(difference.shape, F32),
            jax.ShapeDtypeStruct(coefficients.shape, F32),
            jax.ShapeDtypeStruct((rows_each, shares.shape[2]), F32),
        ],
        in_specs=[vmem] * 3,
        out_specs=[vmem] * 3,
        name="results",
    )(*[pltpu.with_memory_space_constraint(arg, pltpu.VMEM) for arg in args])


def solution(mesh):
    visits = mesh.shape["visit"]
    sky = mesh.shape["sky"]

    def on_device(template, science, variance, col_taps, row_taps, stamp_rows, stamp_cols):
        rows_each, width = template.shape
        margin = (col_taps.shape[1] - 1) // 2
        others = (science, variance, col_taps.T, row_taps.T, stamp_rows, stamp_cols)
        if sky == 1:
            copies, *rest = stage_inputs(template, visits, others[2:])
            others = others[:2] + tuple(rest)
        else:
            copies = jnp.broadcast_to(template[None], (visits, rows_each, width))
        tile = lax.all_to_all(copies, "visit", 0, 0, tiled=True).reshape(-1, width)
        edge = sky_edges(tile, margin, sky) if sky > 1 else None
        difference, coefficients, shares = fit(tile, edge, *others, rows_each, sky)
        shares = lax.all_to_all(shares, "visit", 0, 0, tiled=True)
        if sky == 1:
            return gather_results(shares, difference, coefficients)
        total = jnp.sum(shares, axis=0)
        detection = total[0:rows_each] / jnp.sqrt(total[rows_each:])
        return difference, coefficients, detection

    in_specs = (
        P(("group", "visit"), "sky"),
        P(("group", "visit"), None, "sky"),
        P(("group", "visit"), None, "sky"),
        P(),
        P(),
        P(("group", "visit"), "sky", None),
        P(("group", "visit"), "sky", None),
    )
    out_specs = (
        P(("group", "visit"), None, "sky"),
        P(("group", "visit"), None),
        P(("group", "visit"), "sky"),
    )
    return jax.shard_map(
        on_device, mesh=mesh, in_specs=in_specs, out_specs=out_specs, check_vma=False
    )
```
